32 devices in a mesh: gx: 8 (over z, x), gy: 4 (over y, core).
Axes of the slice: x: 2, y: 2, z: 4, core: 2. Of those that a mesh axis runs over, the one named last changes fastest.
Arguments:
- positions: float32 [3, 1048576], P(None, ('gx', 'gy')), may hold values from -5 to 5, as said below
- noise: float32 [3, 1048576], P(None, ('gx', 'gy')), may hold values from -0.6 to 0.6
- route: int32 [1048576], P(('gx', 'gy')), may hold values from 0 to 65535, as said below
- node_perm: int32 [8, 4, 65536], P(None, 'gy'), may hold values from 0 to 65535, each once within a row
- pair_first: int32 [32, 1024], P(('gx', 'gy')), may hold values from 0 to 1023
- pair_second: int32 [32, 1024], P(('gx', 'gy')), may hold values from 0 to 2047
- pair_count: int32 [32], P(('gx', 'gy')), may hold values from 512 to 1024, as said below
Outputs:
- moved: float32 [3, 1048576], P(None, ('gx', 'gy'))
- drift: float32 [3, 1048576], P(None, ('gx', 'gy'))
The draws below stay inside these ranges and needn't reach their ends.
Inputs may be any that keep to these rules, and one draw needn't show every extreme that they name: `positions`: consecutive beads of a chain lie between 0.25 and 0.95 apart. `route`: within one device the values are distinct and rise along its beads; at most 2048 beads of one device go to one device, and every device sends exactly 2048 beads to some device. `pair_count`: some device's count is 1024.
All inputs are finite; a program needn't handle non-finite values.
Results may differ from the reference program's by a relative error of at most 0.015.
Values sent between devices are 32-bit elements; how exact they have to be, the bound alone decides.
No kernel may reach another device: no remote copies, remote signals or barrier semaphores. Data moves between devices by JAX's collectives and lax.ppermute only.
A program may use at most 192 MiB of HBM per device.

```python
import math
import jax
import jax.numpy as jnp
from jax import lax

G = 128
BEAD_CH = 64
CELL = 64
PAIRS_DEV = 1024
SLOTS_DEV = 65536
CAP = 2048
BEADS_DEV = 32768
BEADS = 1048576
BLK_DEV = 1024
N_GX = 8
N_GY = 4
DEVICES = 32


def draw_positions(key, part):
    keys = jax.random.split(key, 3)
    chains = BEADS // BEAD_CH
    centre = jax.random.uniform(keys[0], (3, chains), jnp.float32, -1.5, 1.5)
    twist = jax.random.uniform(keys[1], (chains,), jnp.float32, -math.pi, math.pi)
    jitter = jax.random.uniform(keys[2], (3, BEADS), jnp.float32, -0.1, 0.1)
    along = jnp.arange(BEAD_CH, dtype=jnp.float32)
    angle = twist[:, None] + 0.6 * along[None, :]
    rise = jnp.broadcast_to(0.1 * (along[None, :] - 31.5), angle.shape)
    helix = jnp.stack([jnp.cos(angle), jnp.sin(angle), rise])
    return (centre[:, :, None] + helix).reshape(3, BEADS) + jitter


def draw_route(key, part):

    def one_device(device_key):
        keys = jax.random.split(device_key, 2)
        order = jax.random.permutation(keys[0], DEVICES * CAP).astype(jnp.int32)
        chosen = jax.random.randint(keys[1], (), 0, DEVICES)
        place = jnp.arange(DEVICES * CAP, dtype=jnp.int32)
        priority = order + jnp.where(place // CAP == chosen, DEVICES * CAP, 0).astype(jnp.int32)
        _, picked = lax.top_k(priority, BEADS_DEV)
        return jnp.sort(picked.astype(jnp.int32))
    return jax.vmap(one_device)(jax.random.split(key, DEVICES)).reshape(BEADS)


def draw_pair_count(key, part):
    keys = jax.random.split(key, 2)
    halving = jax.random.randint(keys[0], (DEVICES,), 0, 2)
    counts = jnp.right_shift(jnp.full((DEVICES,), PAIRS_DEV, jnp.int32), halving.astype(jnp.int32))
    fullest = jax.random.randint(keys[1], (), 0, DEVICES)
    return jnp.where(jnp.arange(DEVICES) == fullest, PAIRS_DEV, counts).astype(jnp.int32)


def plant(drawn, stream_key, low, high):
    dims = drawn.shape
    spot = [jax.random.randint(jax.random.fold_in(stream_key, axis), (), 0, dims[axis]) for axis in range(len(dims))]
    drawn = drawn.at[tuple(spot)].set(low)
    longest = dims.index(max(dims))
    spot[longest] = (spot[longest] + 1) % dims[longest]
    return drawn.at[tuple(spot)].set(high)


def block_scale(rng, shape, cuts, low, high):
    factor_of = 1.0
    for dim, parts in cuts:
        steps = jax.random.uniform(jax.random.fold_in(jax.random.fold_in(rng, 6), dim), (parts,), jnp.float32, low / len(cuts), high / len(cuts))
        factor_of = factor_of * jnp.repeat(jnp.exp(steps), shape[dim] // parts).reshape((-1,) + (1,) * (len(shape) - 1 - dim))
    return factor_of


def scatter_about(stream_key, shape, width, bound, cuts=(), kind=jnp.bfloat16):
    values = width * jax.random.normal(stream_key, shape, jnp.float32)
    if cuts:
        values = values * block_scale(stream_key, shape, cuts, -0.22, 0.18)
    return jnp.clip(values, -bound, bound).astype(kind)


def setup_inputs(seed: int = 0) -> dict:
    streams_of = jax.random.split(jax.random.key(seed), 8)
    return {
        "positions": draw_positions(jax.random.fold_in(streams_of[7], 71), 0),
        "noise": scatter_about(streams_of[1], (3, BEADS), 0.1, 0.6, ((1, 32),), jnp.float32),
        "route": draw_route(jax.random.fold_in(streams_of[7], 71), 0),
        "node_perm": jax.vmap(lambda own: jax.random.permutation(own, SLOTS_DEV))(jax.random.split(streams_of[3], N_GX * N_GY)).reshape((N_GX, N_GY, SLOTS_DEV)).astype(jnp.int32),
        "pair_first": plant(jax.random.randint(streams_of[4], (DEVICES, PAIRS_DEV), 0, BLK_DEV), jax.random.fold_in(streams_of[4], 1), 0, BLK_DEV - 1).astype(jnp.int32),
        "pair_second": plant(jax.random.randint(streams_of[5], (DEVICES, PAIRS_DEV), 0, 2 * BLK_DEV), jax.random.fold_in(streams_of[5], 1), 0, (2 * BLK_DEV) - 1).astype(jnp.int32),
        "pair_count": draw_pair_count(jax.random.fold_in(streams_of[7], 71), 0),
    }


bead_radius = 0.5
split_xi = 0.5
time_step = 0.01
fene_k = 30.0
fene_reach = 1.5
bend_k = 2.0
grid_spacing = 4.0
pair_block = 64

def bonded_forces(positions):
    chains = positions.reshape(3, -1, BEAD_CH)

    def energy(coords):
        bond = coords[:, :, 1:] - coords[:, :, :-1]
        square = lax.optimization_barrier(jnp.sum(bond * bond, axis=0))
        stretch = -0.5 * fene_k * fene_reach ** 2 * jnp.sum(jnp.log(1.0 - square / fene_reach ** 2))
        length = jnp.sqrt(square)
        cosine = lax.optimization_barrier(jnp.sum(bond[:, :, 1:] * bond[:, :, :-1], axis=0)) / (length[:, 1:] * length[:, :-1])
        return stretch + bend_k * jnp.sum(1.0 - cosine)
    return (-jax.grad(energy)(chains)).reshape(3, -1)

def tile_pairs(near_pos, near_force, far_pos, far_force):
    offsets = [near_pos[channel][:, :, None] - far_pos[channel][:, None, :] for channel in range(3)]
    square = offsets[0] * offsets[0] + offsets[1] * offsets[1] + offsets[2] * offsets[2] + bead_radius ** 2
    distance = jnp.sqrt(square)
    scaled = bead_radius / distance
    scaled_cube = scaled * scaled * scaled
    screen = jax.scipy.special.erfc(split_xi * distance)
    gauss_part = 0.5 * split_xi * bead_radius * jnp.exp(-split_xi ** 2 * square)
    along_part = screen * (0.75 * scaled + 0.5 * scaled_cube) + gauss_part
    across = (screen * (0.75 * scaled - 1.5 * scaled_cube) - gauss_part) / square
    onto_far = across * sum((offsets[channel] * far_force[channel][:, None, :] for channel in range(3)))
    onto_near = across * sum((offsets[channel] * near_force[channel][:, :, None] for channel in range(3)))
    near_vel = jnp.stack([lax.optimization_barrier(jnp.sum(along_part * far_force[channel][:, None, :] + onto_far * offsets[channel], axis=2)) for channel in range(3)])
    far_vel = jnp.stack([lax.optimization_barrier(jnp.sum(along_part * near_force[channel][:, :, None] + onto_near * offsets[channel], axis=1)) for channel in range(3)])
    return (near_vel, far_vel)

def real_space(cells, pair_first, pair_second, pair_count):
    devices = N_GX * N_GY
    owner = jnp.arange(devices, dtype=jnp.int32)[:, None]
    beside = (owner // N_GY + 1) % N_GX * N_GY + owner % N_GY
    first_glob = owner * BLK_DEV + pair_first
    second_glob = jnp.where(pair_second < BLK_DEV, owner * BLK_DEV + pair_second, beside * BLK_DEV + pair_second - BLK_DEV)
    live_mask = (jnp.arange(PAIRS_DEV, dtype=jnp.int32)[None, :] < pair_count[:, None]).astype(jnp.float32)
    batches = (first_glob.reshape(-1, pair_block), second_glob.reshape(-1, pair_block), live_mask.reshape(-1, pair_block))

    def turn(velocity_sum, batch):
        near_idx, far_idx, live_row = batch
        near_cells = jnp.take(cells, near_idx, axis=1)
        far_cells = jnp.take(cells, far_idx, axis=1)
        near_vel, far_vel = tile_pairs(near_cells[:3], near_cells[3:], far_cells[:3], far_cells[3:])
        cross_mask = live_row * (near_idx != far_idx).astype(jnp.float32)
        velocity_sum = velocity_sum.at[:, near_idx].add(near_vel * live_row[None, :, None])
        velocity_sum = velocity_sum.at[:, far_idx].add(far_vel * cross_mask[None, :, None])
        return (velocity_sum, None)
    start_sum = jnp.zeros((3, cells.shape[1], CELL), jnp.float32)
    velocity_sum, _ = lax.scan(turn, start_sum, batches)
    return velocity_sum

def kspace(force_grid):
    spectrum = jnp.fft.fftn(force_grid, axes=(1, 2, 3))
    wave = jnp.fft.fftfreq(G) * (2.0 * math.pi / grid_spacing)
    wave_x = wave[:, None, None]
    wave_y = wave[None, :, None]
    wave_z = wave[None, None, :]
    wave_sq = wave_x * wave_x + wave_y * wave_y + wave_z * wave_z
    wave_safe = jnp.where(wave_sq > 0, wave_sq, 1.0)
    spread_sq = wave_sq / (4.0 * split_xi ** 2)
    green_fn = jnp.where(wave_sq > 0, (1.0 - bead_radius ** 2 * wave_sq / 3.0) * (1.0 + spread_sq) * jnp.exp(-spread_sq) / wave_safe, 0.0)
    along_wave = (wave_x * spectrum[0] + wave_y * spectrum[1] + wave_z * spectrum[2]) / wave_safe
    flow = jnp.stack([green_fn * (spectrum[0] - wave_x * along_wave), green_fn * (spectrum[1] - wave_y * along_wave), green_fn * (spectrum[2] - wave_z * along_wave)])
    return jnp.real(jnp.fft.ifftn(flow, axes=(1, 2, 3)))

def reference(positions, noise, route, node_perm, pair_first, pair_second, pair_count):
    forces = bonded_forces(positions)
    devices = N_GX * N_GY
    source = jnp.arange(BEADS_DEV * devices, dtype=jnp.int32) // BEADS_DEV
    target = route // CAP
    message = source * CAP + route % CAP
    node_at = node_perm[target // N_GY, target % N_GY, message]
    place_at = target * SLOTS_DEV + node_at
    layout = jnp.zeros((6, devices * SLOTS_DEV), jnp.float32).at[:, place_at].set(jnp.concatenate([positions, forces], axis=0))
    local_x = G // N_GX
    local_y = G // N_GY
    force_grid = layout[3:].reshape(3, N_GX, N_GY, local_x, local_y, G).transpose(0, 1, 3, 2, 4, 5).reshape(3, G, G, G)
    wave_vel = kspace(force_grid).reshape(3, N_GX, local_x, N_GY, local_y, G).transpose(0, 1, 3, 2, 4, 5).reshape(3, devices * SLOTS_DEV)
    real_vel = real_space(layout.reshape(6, devices * BLK_DEV, CELL), pair_first, pair_second, pair_count).reshape(3, devices * SLOTS_DEV)
    velocity = (real_vel + wave_vel)[:, place_at]
    drift = time_step * velocity
    moved = positions + drift + noise
    return (moved, drift)
```

```python
import functools
from functools import partial
import math

import jax
import jax.numpy as jnp
from jax import lax
from jax.experimental import pallas as pl
from jax.experimental.pallas import tpu as pltpu
from jax.sharding import PartitionSpec as P

G = 128
BEAD_CH = 64
CELL = 64


bead_radius = 0.5
split_xi = 0.5
time_step = 0.01
fene_k = 30.0
fene_reach = 1.5
bend_k = 2.0
grid_spacing = 4.0
pair_block = 64


def shifted(value, axis, by):
    devices = lax.axis_size(axis)
    return lax.ppermute(value, axis, [(i, (i + by) % devices) for i in range(devices)])


def bonded_forces(positions):
    chains = positions.reshape(3, -1, BEAD_CH)

    def energy(coords):
        bond = coords[:, :, 1:] - coords[:, :, :-1]
        square = jnp.sum(bond * bond, axis=0)
        stretch = -0.5 * fene_k * fene_reach**2 * jnp.sum(jnp.log(1.0 - square / fene_reach**2))
        length = jnp.sqrt(square)
        cosine = jnp.sum(bond[:, :, 1:] * bond[:, :, :-1], axis=0) / (
            length[:, 1:] * length[:, :-1]
        )
        return stretch + bend_k * jnp.sum(1.0 - cosine)

    return (-jax.grad(energy)(chains)).reshape(3, -1)


ERFCX_COEF = (0.06548172872398669,
    -0.3609186250151195,
    0.6338942267842493,
    -0.3384301108125971,
    0.4003704641202259,
    0.13581047899030682,
    0.2395463173952274,
    0.22417089752024144,
    7.010614160106155e-05)


def pair_math(dx, dy, dz, coef):
    s2 = dx*dx + dy*dy + dz*dz + 0.25
    u = lax.rsqrt(s2)
    r = s2*u
    t = pl.reciprocal(1.0 + 0.2*r)
    w = coef[0]*t + coef[1]
    for k in coef[2:]:
        w = w*t + k
    ex = jnp.exp(-0.25*s2)
    u2 = u*u
    a = w*u
    f = ex*(a*(0.375 + 0.0625*u2) + 0.125)
    h = ex*u2*(a*(0.375 - 0.1875*u2) - 0.125)
    return f, h

def pair_kernel(first, second, count, own_ref, far_ref, vown_ref, vfar_ref, pc, xr, vc, vr, *, rp, coef, unroll):
    lane = lax.broadcasted_iota(jnp.int32, (8, 128), 1)
    sub = lax.broadcasted_iota(jnp.int32, (8, 128), 0)
    left = lane < 64
    groups = rp // 4

    @pl.loop(0, rp // 8)
    def _(i):
        for src, off in ((own_ref, 0), (far_ref, rp)):
            for c in range(6):
                pc[pl.ds((off + i*8)*8 + c, 8, stride=8), :] = src[c, pl.ds(pl.multiple_of(i*8, 8), 8), :]
            for c in (6, 7):
                pc[pl.ds((off + i*8)*8 + c, 8, stride=8), :] = jnp.zeros((8, 128), jnp.float32)
            vc[pl.ds(pl.multiple_of((off + i*8)*8, 64), 64), :] = jnp.zeros((64, 128), jnp.float32)

    lane32 = lax.broadcasted_iota(jnp.int32, (32, 128), 1)

    @pl.loop(0, groups)
    def _(g):
        blk = pc[pl.ds(pl.multiple_of(g*32, 32), 32), :]
        tr = jnp.transpose(blk)
        tr = jnp.concatenate([tr[32*b:32*b + 32, :] for b in range(4)], axis=1)
        xr[pl.ds(pl.multiple_of(g*32, 32), 32), :] = tr
        vr[pl.ds(pl.multiple_of(g*32, 32), 32), :] = jnp.zeros((32, 128), jnp.float32)

    total = count[0]

    def one(p):
        ka = first[p]
        kb = second[p]
        jv = pc[pl.ds(pl.multiple_of((kb >> 1)*8, 8), 8), :]
        dup = jnp.where(left == ((kb & 1) == 0), jv, pltpu.roll(jv, 64, 1))
        xj = [jnp.broadcast_to(dup[c:c+1, :], (8, 128)) for c in range(6)]
        base = (ka & 1)*64 + ((ka >> 1) & 3)*8
        idx0 = base + jnp.where(left, 0, 32)
        row0 = pl.multiple_of((ka >> 3)*32, 32)
        facc = [jnp.zeros((8, 128), jnp.float32) for _ in range(3)]
        near = []
        for q in range(4):
            row = xr[pl.ds(row0 + 8*q, 8), :]
            xi = [jnp.take_along_axis(row, idx0 + c, axis=1) for c in range(6)]
            d = [xi[c] - xj[c] for c in range(3)]
            f, h = pair_math(d[0], d[1], d[2], coef)
            dj = d[0]*xj[3] + d[1]*xj[4] + d[2]*xj[5]
            di = d[0]*xi[3] + d[1]*xi[4] + d[2]*xi[5]
            hj = h*dj
            hi = h*di
            val = jnp.zeros((8, 128), jnp.float32)
            for c in range(3):
                nv = f*xj[3+c] + hj*d[c]
                lo = jnp.sum(jnp.where(left, nv, 0.0), axis=1, keepdims=True)
                hi_ = jnp.sum(jnp.where(left, 0.0, nv), axis=1, keepdims=True)
                val = jnp.where(lane == base + c, lo, val)
                val = jnp.where(lane == base + 32 + c, hi_, val)
                facc[c] = facc[c] + (f*xi[3+c] + hi*d[c])
            near.append(val)
        fv = jnp.zeros((8, 128), jnp.float32)
        for c in range(3):
            s = jnp.sum(facc[c], axis=0, keepdims=True)
            fv = jnp.where(sub == c, s, fv)
        fv = fv + pltpu.roll(fv, 64, 1)
        keep = (left == ((kb & 1) == 0)) & (ka != kb)
        fv = jnp.where(keep, fv, 0.0)
        return row0, near, kb, fv

    def turn(i, carry):
        outs = []
        for k in range(unroll):
            outs.append((i*unroll + k, one(i*unroll + k)))
        for p, (row0, near, kb, fv) in outs:
            alive = (p < total).astype(jnp.float32) if unroll > 1 else None
            if unroll > 1:
                near = [n*alive for n in near]
                fv = fv*alive
            for q in range(4):
                at = pl.ds(row0 + 8*q, 8)
                vr[at, :] = vr[at, :] + near[q]
            at = pl.ds(pl.multiple_of((kb >> 1)*8, 8), 8)
            vc[at, :] = vc[at, :] + fv
        return carry

    lax.fori_loop(0, lax.div(total + (unroll - 1), jnp.int32(unroll)), turn, 0)

    @pl.loop(0, groups)
    def _(g):
        m = vr[pl.ds(pl.multiple_of(g*32, 32), 32), :]
        st = jnp.concatenate([m[:, 32*b:32*b + 32] for b in range(4)], axis=0)
        at = pl.ds(pl.multiple_of(g*32, 32), 32)
        vc[at, :] = vc[at, :] + jnp.transpose(st)

    @pl.loop(0, rp // 8)
    def _(i):
        for dst, off in ((vown_ref, 0), (vfar_ref, rp)):
            for c in range(3):
                dst[c, pl.ds(pl.multiple_of(i*8, 8), 8), :] = vc[pl.ds((off + i*8)*8 + c, 8, stride=8), :]

def pair_call(first, second, count, own, far, coef=ERFCX_COEF, unroll=1):
    rp = own.shape[1]
    f32 = jnp.float32
    return pl.pallas_call(
        functools.partial(pair_kernel, rp=rp, coef=coef, unroll=unroll),
        out_shape=(jax.ShapeDtypeStruct((3, rp, 128), f32),)*2,
        in_specs=[pl.BlockSpec(memory_space=pltpu.SMEM)]*3 + [pl.BlockSpec(memory_space=pltpu.VMEM)]*2,
        out_specs=(pl.BlockSpec(memory_space=pltpu.VMEM),)*2,
        scratch_shapes=[pltpu.VMEM((2*rp*8, 128), f32), pltpu.VMEM((rp*8, 128), f32),
                        pltpu.VMEM((2*rp*8, 128), f32), pltpu.VMEM((rp*8, 128), f32)],
        compiler_params=pltpu.CompilerParams(vmem_limit_bytes=48*1024*1024),
        name="pairs",
    )(first, second, count, own, far)


def signed_wave(grid_index):
    return jnp.where(grid_index < G // 2, grid_index, grid_index - G).astype(jnp.float32) * (
        2.0 * math.pi / (G * grid_spacing)
    )


def forward_pass(real_in, imag_in, form, cos_part, sin_part):
    contract = partial(jnp.einsum, precision=lax.Precision.HIGHEST)
    real_out = contract(form, real_in, cos_part) + contract(form, imag_in, sin_part)
    imag_out = contract(form, imag_in, cos_part) - contract(form, real_in, sin_part)
    return (real_out, imag_out)


def inverse_pass(real_in, imag_in, form, cos_part, sin_part):
    contract = partial(jnp.einsum, precision=lax.Precision.HIGHEST)
    real_out = contract(form, real_in, cos_part) - contract(form, imag_in, sin_part)
    imag_out = contract(form, imag_in, cos_part) + contract(form, real_in, sin_part)
    return (real_out, imag_out)


def project_flow(spectrum, wave_x, wave_y, wave_z):
    wave_sq = wave_x * wave_x + wave_y * wave_y + wave_z * wave_z
    wave_safe = jnp.where(wave_sq > 0, wave_sq, 1.0)
    spread_sq = wave_sq / (4.0 * split_xi**2)
    green_fn = jnp.where(
        wave_sq > 0,
        (1.0 - bead_radius**2 * wave_sq / 3.0)
        * (1.0 + spread_sq)
        * jnp.exp(-spread_sq)
        / wave_safe,
        0.0,
    )
    along_wave = (wave_x * spectrum[0] + wave_y * spectrum[1] + wave_z * spectrum[2]) / wave_safe
    return jnp.stack(
        [
            green_fn * (spectrum[0] - wave_x * along_wave),
            green_fn * (spectrum[1] - wave_y * along_wave),
            green_fn * (spectrum[2] - wave_z * along_wave),
        ]
    )


def kspace_part(force_rows, n_gx, n_gy):
    local_x = G // n_gx
    local_y = G // n_gy
    grid_index = jnp.arange(G, dtype=jnp.int32)
    phase_grid = (grid_index[:, None] * grid_index[None, :] % G).astype(jnp.float32) * (
        2.0 * math.pi / G
    )
    cosine_table = jnp.cos(phase_grid)
    sine_table = jnp.sin(phase_grid)
    contract = partial(jnp.einsum, precision=lax.Precision.HIGHEST)
    force_field = force_rows.reshape(3, local_x, local_y, G)
    wave_full = signed_wave(grid_index)
    row_gx = lax.axis_index("gx")
    row_gy = lax.axis_index("gy")
    freq_count = G
    spec_z = jnp.stack(
        [
            contract("cabz,zk->cabk", force_field, cosine_table),
            -contract("cabz,zk->cabk", force_field, sine_table),
        ]
    )
    cos_x = cosine_table.reshape(n_gx, local_x, G)
    sin_x = sine_table.reshape(n_gx, local_x, G)
    cos_y = cosine_table.reshape(n_gy, local_y, G)
    sin_y = sine_table.reshape(n_gy, local_y, G)
    depth_part = freq_count // n_gx
    width_part = G // n_gy
    slabs = lax.all_to_all(spec_z[:, :, None], "gx", split_axis=5, concat_axis=2, tiled=True)
    xr_part, xi_part = forward_pass(slabs[0], slabs[1], "ciabl,iak->cbkl", cos_x, sin_x)
    pencils = lax.all_to_all(
        jnp.stack([xr_part, xi_part])[:, :, None], "gy", split_axis=4, concat_axis=2, tiled=True
    )
    yr_part, yi_part = forward_pass(pencils[0], pencils[1], "cjbkl,jbm->ckml", cos_y, sin_y)
    wave_x = signed_wave(row_gy * width_part + jnp.arange(width_part, dtype=jnp.int32))[
        :, None, None
    ]
    wave_y = wave_full[None, :, None]
    wave_z = signed_wave(row_gx * depth_part + jnp.arange(depth_part, dtype=jnp.int32))[
        None, None, :
    ]
    flow_real = project_flow(yr_part, wave_x, wave_y, wave_z)
    flow_imag = project_flow(yi_part, wave_x, wave_y, wave_z)
    br_part, bi_part = inverse_pass(flow_real, flow_imag, "ckml,jbm->cjbkl", cos_y, sin_y)
    back = lax.all_to_all(
        jnp.stack([br_part, bi_part]), "gy", split_axis=2, concat_axis=4, tiled=True
    )[:, :, 0]
    ar_part, ai_part = inverse_pass(back[0], back[1], "cbkl,iak->ciabl", cos_x, sin_x)
    gathered = lax.all_to_all(
        jnp.stack([ar_part, ai_part]), "gx", split_axis=2, concat_axis=5, tiled=True
    )[:, :, 0]
    result = contract("cabk,zk->cabz", gathered[0], cosine_table) - contract(
        "cabk,zk->cabz", gathered[1], sine_table
    )
    return (result / float(G**3)).reshape(3, local_x * local_y * G)


def shards(positions, noise, route, node_perm, pair_first, pair_second, pair_count):
    forces = bonded_forces(positions)
    n_gx = lax.axis_size("gx")
    n_gy = lax.axis_size("gy")
    devices = n_gx * n_gy
    slots = node_perm.shape[2]
    per_peer = slots // devices
    row_gx = lax.axis_index("gx")
    own_order = node_perm[row_gx, 0]
    stacked = jnp.concatenate([positions, forces], axis=0)
    outgoing = (
        jnp.zeros((6, slots), jnp.float32).at[:, route].set(stacked).reshape(6, devices, per_peer)
    )
    incoming = lax.all_to_all(outgoing, ("gx", "gy"), split_axis=1, concat_axis=1, tiled=True)
    grid_data = jnp.zeros((6, slots), jnp.float32).at[:, own_order].set(incoming.reshape(6, slots))
    beside_data = shifted(grid_data, "gx", -1)
    near_vel, far_vel = pair_call(
        pair_first[0],
        pair_second[0],
        pair_count,
        grid_data.reshape(6, slots // 128, 128),
        beside_data.reshape(6, slots // 128, 128),
    )
    wave_vel = kspace_part(grid_data[3:], n_gx, n_gy)
    own_vel = near_vel.reshape(3, slots) + wave_vel
    own_vel = own_vel + shifted(far_vel.reshape(3, slots), "gx", 1)
    back_msg = own_vel[:, own_order].reshape(3, devices, per_peer)
    arrived = lax.all_to_all(
        back_msg, ("gx", "gy"), split_axis=1, concat_axis=1, tiled=True
    ).reshape(3, slots)
    velocity = arrived[:, route]
    drift = time_step * velocity
    moved = positions + drift + noise
    return (moved, drift)


def solution(mesh):
    in_specs = (
        P(None, ("gx", "gy")),
        P(None, ("gx", "gy")),
        P(("gx", "gy")),
        P(None, "gy", None),
        P(("gx", "gy"), None),
        P(("gx", "gy"), None),
        P(("gx", "gy")),
    )
    out_specs = (P(None, ("gx", "gy")), P(None, ("gx", "gy")))
    return jax.shard_map(shards, mesh=mesh, in_specs=in_specs, out_specs=out_specs, check_vma=False)
```

```python
import functools
from functools import partial
import math

import jax
import jax.numpy as jnp
from jax import lax
from jax.experimental import pallas as pl
from jax.experimental.pallas import tpu as pltpu
from jax.sharding import PartitionSpec as P

G = 128
BEAD_CH = 64
CELL = 64


bead_radius = 0.5
split_xi = 0.5
time_step = 0.01
fene_k = 30.0
fene_reach = 1.5
bend_k = 2.0
grid_spacing = 4.0
pair_block = 64


def shifted(value, axis, by):
    devices = lax.axis_size(axis)
    return lax.ppermute(value, axis, [(i, (i + by) % devices) for i in range(devices)])


UNROLL = 16

SMEM_SPEC = pl.BlockSpec(memory_space=pltpu.SMEM)
VMEM_SPEC = pl.BlockSpec(memory_space=pltpu.VMEM)


def lane_index(rows):
    return lax.broadcasted_iota(jnp.int32, (rows, 128), 1)


def window(table, at, rows):
    row = lax.shift_right_logical(at, 7)
    lead = at & 127
    head = pltpu.roll(table[pl.ds(row, rows), :], (128 - lead) & 127, 1)
    tail = pltpu.roll(table[pl.ds(row + 1, rows), :], (128 - lead) & 127, 1)
    return jnp.where(lane_index(rows) < 128 - lead, head, tail)


def slots_kernel(starts, route_ref, out_ref, table, *, rows, depth):
    table[pl.ds(0, rows), :] = route_ref[...]
    table[pl.ds(rows, depth + 8), :] = jnp.zeros((depth + 8, 128), jnp.int32)
    place = lane_index(depth) + lax.broadcasted_iota(jnp.int32, (depth, 128), 0) * 128

    @pl.loop(0, out_ref.shape[0])
    def _(t):
        at = starts[t]
        slot = window(table, at, depth) - t * (depth * 128)
        out_ref[t] = jnp.where(place < starts[t + 1] - at, slot, -1)


def slots_call(starts, route, depth):
    rows = route.shape[0]
    peers = starts.shape[0] - 1
    return pl.pallas_call(
        functools.partial(slots_kernel, rows=rows, depth=depth),
        out_shape=jax.ShapeDtypeStruct((peers, depth, 128), jnp.int32),
        in_specs=[SMEM_SPEC, VMEM_SPEC],
        out_specs=VMEM_SPEC,
        scratch_shapes=[pltpu.VMEM((rows + depth + 8, 128), jnp.int32)],
        name="slots",
    )(starts, route)


def chain_forces(pos):
    rows = pos[0].shape[0]
    place = lane_index(rows) & (BEAD_CH - 1)
    bonded = place < BEAD_CH - 1
    bent = place < BEAD_CH - 2
    after = (place > 0) & bonded
    bond = [jnp.where(bonded, pltpu.roll(x, 127, 1) - x, 0.5) for x in pos]
    square = bond[0] * bond[0] + bond[1] * bond[1] + bond[2] * bond[2]
    inverse = lax.rsqrt(square)
    unit = [b * inverse for b in bond]
    following = [pltpu.roll(u, 127, 1) for u in unit]
    previous = [pltpu.roll(u, 1, 1) for u in unit]
    cosine = sum(u * v for u, v in zip(unit, following))
    cosine_before = pltpu.roll(cosine, 1, 1)
    pull = fene_k / (1.0 - square / fene_reach**2)
    out = []
    for c in range(3):
        turn = jnp.where(bent, following[c] - cosine * unit[c], 0.0)
        turn = turn + jnp.where(after, previous[c] - cosine_before * unit[c], 0.0)
        slope = jnp.where(bonded, pull * bond[c] - bend_k * inverse * turn, 0.0)
        out.append(slope - pltpu.roll(slope, 1, 1))
    return out


def pack_kernel(starts, pos_ref, out_ref, table, *, rows, depth, stride):
    step = 8

    @pl.loop(0, rows // step)
    def _(i):
        at = pl.multiple_of(i * step, step)
        pos = [pos_ref[c, pl.ds(at, step), :] for c in range(3)]
        for c, value in enumerate(pos + chain_forces(pos)):
            table[pl.ds(c * stride + at, step), :] = value

    for c in range(6):
        table[pl.ds(c * stride + rows, stride - rows), :] = jnp.zeros((stride - rows, 128), jnp.float32)

    @pl.loop(0, out_ref.shape[0])
    def _(t):
        at = starts[t]
        for c in range(6):
            out_ref[t, c * depth : (c + 1) * depth, :] = window(table, at + c * stride * 128, depth)


def pack_call(starts, pos, depth):
    rows = pos.shape[1]
    peers = starts.shape[0] - 1
    stride = rows + depth + 8
    stride += -stride % 8
    return pl.pallas_call(
        functools.partial(pack_kernel, rows=rows, depth=depth, stride=stride),
        out_shape=jax.ShapeDtypeStruct((peers, 6 * depth, 128), jnp.float32),
        in_specs=[SMEM_SPEC, VMEM_SPEC],
        out_specs=VMEM_SPEC,
        scratch_shapes=[pltpu.VMEM((6 * stride, 128), jnp.float32)],
        name="pack",
    )(starts, pos)


def nodes_kernel(slots_ref, perm_ref, out_ref, *, depth, spare):
    tile = 8 if depth % 8 == 0 else 1

    @pl.loop(0, slots_ref.shape[0])
    def _(t):
        rows = [jnp.broadcast_to(perm_ref[t, w : w + 1, :], (8, 128)) for w in range(depth)]
        for r in range(depth // tile):
            slot = jnp.broadcast_to(slots_ref[t, r * tile : (r + 1) * tile, :], (8, 128))
            place = slot & 127
            which = slot >> 7
            node = jnp.full((8, 128), spare, jnp.int32)
            for w in range(depth):
                node = jnp.where(which == w, jnp.take_along_axis(rows[w], place, axis=1), node)
            out_ref[t, r * tile : (r + 1) * tile, :] = node[:tile]


def nodes_call(slots, perm, spare):
    return pl.pallas_call(
        functools.partial(nodes_kernel, depth=slots.shape[1], spare=spare),
        out_shape=jax.ShapeDtypeStruct(slots.shape, jnp.int32),
        in_specs=[VMEM_SPEC] * 2,
        out_specs=VMEM_SPEC,
        name="nodes",
    )(slots, perm)


def scatter_kernel(nodes, counts, in_ref, out_ref, table, rows_ref, *, depth, rp):
    t = pl.program_id(0)

    @pl.when(t == 0)
    def _():
        @pl.loop(0, rp)
        def _(k):
            table[pl.ds(pl.multiple_of(k * 128, 128), 128), :] = jnp.zeros((128, 128), jnp.float32)

    for r in range(depth):
        piece = in_ref[0, pl.ds(r, 6, stride=depth), :]
        piece = jnp.concatenate([piece, jnp.zeros((2, 128), jnp.float32)], axis=0)
        rows_ref[r * 128 : (r + 1) * 128, 0:8] = jnp.transpose(piece)

    base = t * (depth * 128)

    def some(i, carry):
        at = pl.multiple_of(i * UNROLL, UNROLL)
        for u in range(UNROLL):
            table[pl.ds(nodes[base + at + u], 1), :] = rows_ref[pl.ds(at + u, 1), :]
        return carry

    lax.fori_loop(0, lax.div(counts[t] + (UNROLL - 1), jnp.int32(UNROLL)), some, 0)

    @pl.when(t == pl.num_programs(0) - 1)
    def _():
        @pl.loop(0, rp, unroll=4)
        def _(k):
            turned = jnp.transpose(table[pl.ds(pl.multiple_of(k * 128, 128), 128), 0:8])
            out_ref[pl.ds(k, 6, stride=rp), :] = turned[:6]


def scatter_call(nodes, counts, data, rp):
    peers, height, _ = data.shape
    depth = height // 6
    return pl.pallas_call(
        functools.partial(scatter_kernel, depth=depth, rp=rp),
        out_shape=jax.ShapeDtypeStruct((6 * rp, 128), jnp.float32),
        grid=(peers,),
        in_specs=[SMEM_SPEC, SMEM_SPEC, pl.BlockSpec((1, height, 128), lambda t: (t, 0, 0))],
        out_specs=VMEM_SPEC,
        scratch_shapes=[pltpu.VMEM((rp * 128 + 8, 128), jnp.float32), pltpu.VMEM((depth * 128, 128), jnp.float32)],
        compiler_params=pltpu.CompilerParams(vmem_limit_bytes=52 * 1024 * 1024),
        name="scatter",
    )(nodes, counts, data)


def gather_kernel(nodes, counts, one_ref, two_ref, three_ref, out_ref, table, rows_ref, *, depth, rp):
    t = pl.program_id(0)

    @pl.when(t == 0)
    def _():
        @pl.loop(0, rp, unroll=4)
        def _(k):
            at = pl.ds(k, 3, stride=rp)
            value = one_ref[at, :] + two_ref[at, :] + three_ref[at, :]
            value = jnp.concatenate([value, jnp.zeros((5, 128), jnp.float32)], axis=0)
            table[pl.ds(pl.multiple_of(k * 128, 128), 128), 0:8] = jnp.transpose(value)

    base = t * (depth * 128)

    def some(i, carry):
        at = pl.multiple_of(i * UNROLL, UNROLL)
        for u in range(UNROLL):
            rows_ref[pl.ds(at + u, 1), :] = table[pl.ds(nodes[base + at + u], 1), :]
        return carry

    lax.fori_loop(0, lax.div(counts[t] + (UNROLL - 1), jnp.int32(UNROLL)), some, 0)
    for r in range(depth):
        turned = jnp.transpose(rows_ref[r * 128 : (r + 1) * 128, 0:8])
        out_ref[0, pl.ds(r, 3, stride=depth), :] = turned[:3]


def gather_call(nodes, counts, one, two, three, depth):
    rp = one.shape[0] // 3
    peers = counts.shape[0]
    return pl.pallas_call(
        functools.partial(gather_kernel, depth=depth, rp=rp),
        out_shape=jax.ShapeDtypeStruct((peers, 3 * depth, 128), jnp.float32),
        grid=(peers,),
        in_specs=[SMEM_SPEC, SMEM_SPEC] + [VMEM_SPEC] * 3,
        out_specs=pl.BlockSpec((1, 3 * depth, 128), lambda t: (t, 0, 0)),
        scratch_shapes=[pltpu.VMEM((rp * 128 + 8, 128), jnp.float32), pltpu.VMEM((depth * 128, 128), jnp.float32)],
        compiler_params=pltpu.CompilerParams(vmem_limit_bytes=52 * 1024 * 1024),
        name="gather",
    )(nodes, counts, one, two, three)


def finish_kernel(starts, in_ref, pos_ref, noise_ref, moved_ref, drift_ref, table, *, rows, depth, stride):
    lane = lane_index(depth)
    first = lane_index(1)

    @pl.loop(0, in_ref.shape[0])
    def _(t):
        at = starts[t]
        row = lax.shift_right_logical(at, 7)
        lead = at & 127
        for c in range(3):
            value = pltpu.roll(in_ref[t, c * depth : (c + 1) * depth, :], lead, 1)
            here = pl.ds(c * stride + row, depth)
            behind = pl.ds(c * stride + row + 1, depth)
            edge = table[pl.ds(c * stride + row, 1), :]
            table[behind, :] = value
            if depth > 1:
                body = jnp.where(lane[1:] < lead, value[:-1], value[1:])
                table[pl.ds(c * stride + row + 1, depth - 1), :] = body
            table[pl.ds(c * stride + row, 1), :] = jnp.where(first < lead, edge, value[:1])

    step = 8

    @pl.loop(0, rows // step)
    def _(i):
        at = pl.multiple_of(i * step, step)
        for c in range(3):
            drift = time_step * table[pl.ds(c * stride + at, step), :]
            drift_ref[c, pl.ds(at, step), :] = drift
            moved_ref[c, pl.ds(at, step), :] = pos_ref[c, pl.ds(at, step), :] + drift + noise_ref[c, pl.ds(at, step), :]


def finish_call(starts, data, pos, noise):
    rows = pos.shape[1]
    depth = data.shape[1] // 3
    stride = rows + depth + 8
    stride += -stride % 8
    return pl.pallas_call(
        functools.partial(finish_kernel, rows=rows, depth=depth, stride=stride),
        out_shape=(jax.ShapeDtypeStruct(pos.shape, jnp.float32),) * 2,
        in_specs=[SMEM_SPEC] + [VMEM_SPEC] * 3,
        out_specs=(VMEM_SPEC,) * 2,
        scratch_shapes=[pltpu.VMEM((3 * stride, 128), jnp.float32)],
        name="finish",
    )(starts, data, pos, noise)


ERFCX_COEF = (0.06548172872398669,
    -0.3609186250151195,
    0.6338942267842493,
    -0.3384301108125971,
    0.4003704641202259,
    0.13581047899030682,
    0.2395463173952274,
    0.22417089752024144,
    7.010614160106155e-05)


def pair_math(dx, dy, dz, coef):
    s2 = dx*dx + dy*dy + dz*dz + 0.25
    u = lax.rsqrt(s2)
    r = s2*u
    t = pl.reciprocal(1.0 + 0.2*r)
    w = coef[0]*t + coef[1]
    for k in coef[2:]:
        w = w*t + k
    ex = jnp.exp(-0.25*s2)
    u2 = u*u
    a = w*u
    f = ex*(a*(0.375 + 0.0625*u2) + 0.125)
    h = ex*u2*(a*(0.375 - 0.1875*u2) - 0.125)
    return f, h

def pair_kernel(first, second, count, own_ref, far_ref, vown_ref, vfar_ref, pc, xr, vc, vr, *, rp, coef, unroll):
    lane = lax.broadcasted_iota(jnp.int32, (8, 128), 1)
    sub = lax.broadcasted_iota(jnp.int32, (8, 128), 0)
    left = lane < 64
    groups = rp // 4

    @pl.loop(0, rp // 8)
    def _(i):
        for src, off in ((own_ref, 0), (far_ref, rp)):
            for c in range(6):
                pc[pl.ds((off + i*8)*8 + c, 8, stride=8), :] = src[c, pl.ds(pl.multiple_of(i*8, 8), 8), :]
            for c in (6, 7):
                pc[pl.ds((off + i*8)*8 + c, 8, stride=8), :] = jnp.zeros((8, 128), jnp.float32)
            vc[pl.ds(pl.multiple_of((off + i*8)*8, 64), 64), :] = jnp.zeros((64, 128), jnp.float32)

    lane32 = lax.broadcasted_iota(jnp.int32, (32, 128), 1)

    @pl.loop(0, groups)
    def _(g):
        blk = pc[pl.ds(pl.multiple_of(g*32, 32), 32), :]
        tr = jnp.transpose(blk)
        tr = jnp.concatenate([tr[32*b:32*b + 32, :] for b in range(4)], axis=1)
        xr[pl.ds(pl.multiple_of(g*32, 32), 32), :] = tr
        vr[pl.ds(pl.multiple_of(g*32, 32), 32), :] = jnp.zeros((32, 128), jnp.float32)

    total = count[0]

    def one(p):
        ka = first[p]
        kb = second[p]
        jv = pc[pl.ds(pl.multiple_of((kb >> 1)*8, 8), 8), :]
        dup = jnp.where(left == ((kb & 1) == 0), jv, pltpu.roll(jv, 64, 1))
        xj = [jnp.broadcast_to(dup[c:c+1, :], (8, 128)) for c in range(6)]
        base = (ka & 1)*64 + ((ka >> 1) & 3)*8
        idx0 = base + jnp.where(left, 0, 32)
        row0 = pl.multiple_of((ka >> 3)*32, 32)
        facc = [jnp.zeros((8, 128), jnp.float32) for _ in range(3)]
        near = []
        for q in range(4):
            row = xr[pl.ds(row0 + 8*q, 8), :]
            xi = [jnp.take_along_axis(row, idx0 + c, axis=1) for c in range(6)]
            d = [xi[c] - xj[c] for c in range(3)]
            f, h = pair_math(d[0], d[1], d[2], coef)
            dj = d[0]*xj[3] + d[1]*xj[4] + d[2]*xj[5]
            di = d[0]*xi[3] + d[1]*xi[4] + d[2]*xi[5]
            hj = h*dj
            hi = h*di
            val = jnp.zeros((8, 128), jnp.float32)
            for c in range(3):
                nv = f*xj[3+c] + hj*d[c]
                lo = jnp.sum(jnp.where(left, nv, 0.0), axis=1, keepdims=True)
                hi_ = jnp.sum(jnp.where(left, 0.0, nv), axis=1, keepdims=True)
                val = jnp.where(lane == base + c, lo, val)
                val = jnp.where(lane == base + 32 + c, hi_, val)
                facc[c] = facc[c] + (f*xi[3+c] + hi*d[c])
            near.append(val)
        fv = jnp.zeros((8, 128), jnp.float32)
        for c in range(3):
            s = jnp.sum(facc[c], axis=0, keepdims=True)
            fv = jnp.where(sub == c, s, fv)
        fv = fv + pltpu.roll(fv, 64, 1)
        keep = (left == ((kb & 1) == 0)) & (ka != kb)
        fv = jnp.where(keep, fv, 0.0)
        return row0, near, kb, fv

    def turn(i, carry):
        outs = []
        for k in range(unroll):
            outs.append((i*unroll + k, one(i*unroll + k)))
        for p, (row0, near, kb, fv) in outs:
            alive = (p < total).astype(jnp.float32) if unroll > 1 else None
            if unroll > 1:
                near = [n*alive for n in near]
                fv = fv*alive
            for q in range(4):
                at = pl.ds(row0 + 8*q, 8)
                vr[at, :] = vr[at, :] + near[q]
            at = pl.ds(pl.multiple_of((kb >> 1)*8, 8), 8)
            vc[at, :] = vc[at, :] + fv
        return carry

    lax.fori_loop(0, lax.div(total + (unroll - 1), jnp.int32(unroll)), turn, 0)

    @pl.loop(0, groups)
    def _(g):
        m = vr[pl.ds(pl.multiple_of(g*32, 32), 32), :]
        st = jnp.concatenate([m[:, 32*b:32*b + 32] for b in range(4)], axis=0)
        at = pl.ds(pl.multiple_of(g*32, 32), 32)
        vc[at, :] = vc[at, :] + jnp.transpose(st)

    @pl.loop(0, rp // 8)
    def _(i):
        for dst, off in ((vown_ref, 0), (vfar_ref, rp)):
            for c in range(3):
                dst[c, pl.ds(pl.multiple_of(i*8, 8), 8), :] = vc[pl.ds((off + i*8)*8 + c, 8, stride=8), :]

def pair_call(first, second, count, own, far, coef=ERFCX_COEF, unroll=1):
    rp = own.shape[1]
    f32 = jnp.float32
    return pl.pallas_call(
        functools.partial(pair_kernel, rp=rp, coef=coef, unroll=unroll),
        out_shape=(jax.ShapeDtypeStruct((3, rp, 128), f32),)*2,
        in_specs=[pl.BlockSpec(memory_space=pltpu.SMEM)]*3 + [pl.BlockSpec(memory_space=pltpu.VMEM)]*2,
        out_specs=(pl.BlockSpec(memory_space=pltpu.VMEM),)*2,
        scratch_shapes=[pltpu.VMEM((2*rp*8, 128), f32), pltpu.VMEM((rp*8, 128), f32),
                        pltpu.VMEM((2*rp*8, 128), f32), pltpu.VMEM((rp*8, 128), f32)],
        compiler_params=pltpu.CompilerParams(vmem_limit_bytes=48*1024*1024),
        name="pairs",
    )(first, second, count, own, far)


def signed_wave(grid_index):
    return jnp.where(grid_index < G // 2, grid_index, grid_index - G).astype(jnp.float32) * (
        2.0 * math.pi / (G * grid_spacing)
    )


def forward_pass(real_in, imag_in, form, cos_part, sin_part):
    contract = partial(jnp.einsum, precision=lax.Precision.HIGHEST)
    real_out = contract(form, real_in, cos_part) + contract(form, imag_in, sin_part)
    imag_out = contract(form, imag_in, cos_part) - contract(form, real_in, sin_part)
    return (real_out, imag_out)


def inverse_pass(real_in, imag_in, form, cos_part, sin_part):
    contract = partial(jnp.einsum, precision=lax.Precision.HIGHEST)
    real_out = contract(form, real_in, cos_part) - contract(form, imag_in, sin_part)
    imag_out = contract(form, imag_in, cos_part) + contract(form, real_in, sin_part)
    return (real_out, imag_out)


def project_flow(spectrum, wave_x, wave_y, wave_z):
    wave_sq = wave_x * wave_x + wave_y * wave_y + wave_z * wave_z
    wave_safe = jnp.where(wave_sq > 0, wave_sq, 1.0)
    spread_sq = wave_sq / (4.0 * split_xi**2)
    green_fn = jnp.where(
        wave_sq > 0,
        (1.0 - bead_radius**2 * wave_sq / 3.0)
        * (1.0 + spread_sq)
        * jnp.exp(-spread_sq)
        / wave_safe,
        0.0,
    )
    along_wave = (wave_x * spectrum[0] + wave_y * spectrum[1] + wave_z * spectrum[2]) / wave_safe
    return jnp.stack(
        [
            green_fn * (spectrum[0] - wave_x * along_wave),
            green_fn * (spectrum[1] - wave_y * along_wave),
            green_fn * (spectrum[2] - wave_z * along_wave),
        ]
    )


def kspace_part(force_rows, n_gx, n_gy):
    local_x = G // n_gx
    local_y = G // n_gy
    grid_index = jnp.arange(G, dtype=jnp.int32)
    phase_grid = (grid_index[:, None] * grid_index[None, :] % G).astype(jnp.float32) * (
        2.0 * math.pi / G
    )
    cosine_table = jnp.cos(phase_grid)
    sine_table = jnp.sin(phase_grid)
    contract = partial(jnp.einsum, precision=lax.Precision.HIGHEST)
    force_field = force_rows.reshape(3, local_x, local_y, G)
    wave_full = signed_wave(grid_index)
    row_gx = lax.axis_index("gx")
    row_gy = lax.axis_index("gy")
    freq_count = G
    spec_z = jnp.stack(
        [
            contract("cabz,zk->cabk", force_field, cosine_table),
            -contract("cabz,zk->cabk", force_field, sine_table),
        ]
    )
    cos_x = cosine_table.reshape(n_gx, local_x, G)
    sin_x = sine_table.reshape(n_gx, local_x, G)
    cos_y = cosine_table.reshape(n_gy, local_y, G)
    sin_y = sine_table.reshape(n_gy, local_y, G)
    depth_part = freq_count // n_gx
    width_part = G // n_gy
    slabs = lax.all_to_all(spec_z[:, :, None], "gx", split_axis=5, concat_axis=2, tiled=True)
    xr_part, xi_part = forward_pass(slabs[0], slabs[1], "ciabl,iak->cbkl", cos_x, sin_x)
    pencils = lax.all_to_all(
        jnp.stack([xr_part, xi_part])[:, :, None], "gy", split_axis=4, concat_axis=2, tiled=True
    )
    yr_part, yi_part = forward_pass(pencils[0], pencils[1], "cjbkl,jbm->ckml", cos_y, sin_y)
    wave_x = signed_wave(row_gy * width_part + jnp.arange(width_part, dtype=jnp.int32))[
        :, None, None
    ]
    wave_y = wave_full[None, :, None]
    wave_z = signed_wave(row_gx * depth_part + jnp.arange(depth_part, dtype=jnp.int32))[
        None, None, :
    ]
    flow_real = project_flow(yr_part, wave_x, wave_y, wave_z)
    flow_imag = project_flow(yi_part, wave_x, wave_y, wave_z)
    br_part, bi_part = inverse_pass(flow_real, flow_imag, "ckml,jbm->cjbkl", cos_y, sin_y)
    back = lax.all_to_all(
        jnp.stack([br_part, bi_part]), "gy", split_axis=2, concat_axis=4, tiled=True
    )[:, :, 0]
    ar_part, ai_part = inverse_pass(back[0], back[1], "cbkl,iak->ciabl", cos_x, sin_x)
    gathered = lax.all_to_all(
        jnp.stack([ar_part, ai_part]), "gx", split_axis=2, concat_axis=5, tiled=True
    )[:, :, 0]
    result = contract("cabk,zk->cabz", gathered[0], cosine_table) - contract(
        "cabk,zk->cabz", gathered[1], sine_table
    )
    return (result / float(G**3)).reshape(3, local_x * local_y * G)


def shards(positions, noise, route, node_perm, pair_first, pair_second, pair_count):
    n_gx = lax.axis_size("gx")
    n_gy = lax.axis_size("gy")
    both = ("gx", "gy")
    peers = n_gx * n_gy
    slots = node_perm.shape[2]
    depth = slots // peers // 128
    rows = positions.shape[1] // 128
    rp = slots // 128
    swap = partial(lax.all_to_all, axis_name=both, split_axis=0, concat_axis=0, tiled=True)

    bounds = jnp.arange(peers + 1, dtype=jnp.int32) * (slots // peers)
    starts = jnp.sum(route[None, :] < bounds[:, None], axis=1, dtype=jnp.int32)
    taken = swap(slots_call(starts, route.reshape(rows, 128), depth))
    places = positions.reshape(3, rows, 128)
    data = swap(pack_call(starts, places, depth))
    counts = jnp.sum(taken >= 0, axis=(1, 2), dtype=jnp.int32)
    own_order = lax.dynamic_index_in_dim(node_perm, lax.axis_index("gx"), 0, False)
    nodes = nodes_call(taken, own_order.reshape(peers, depth, 128), slots).reshape(slots)
    grid_data = scatter_call(nodes, counts, data, rp)

    beside_data = shifted(grid_data, "gx", -1)
    near_vel, far_vel = pair_call(
        pair_first[0],
        pair_second[0],
        pair_count,
        grid_data.reshape(6, rp, 128),
        beside_data.reshape(6, rp, 128),
    )
    wave_vel = kspace_part(grid_data[3 * rp :], n_gx, n_gy).reshape(3 * rp, 128)
    back_vel = shifted(far_vel.reshape(3 * rp, 128), "gx", 1)
    back = swap(gather_call(nodes, counts, near_vel.reshape(3 * rp, 128), wave_vel, back_vel, depth))
    moved, drift = finish_call(starts, back, places, noise.reshape(3, rows, 128))
    return (moved.reshape(positions.shape), drift.reshape(positions.shape))


def solution(mesh):
    in_specs = (
        P(None, ("gx", "gy")),
        P(None, ("gx", "gy")),
        P(("gx", "gy")),
        P(None, "gy", None),
        P(("gx", "gy"), None),
        P(("gx", "gy"), None),
        P(("gx", "gy")),
    )
    out_specs = (P(None, ("gx", "gy")), P(None, ("gx", "gy")))
    return jax.shard_map(shards, mesh=mesh, in_specs=in_specs, out_specs=out_specs, check_vma=False)
```

```python
import functools
from functools import partial
import math

import jax
import jax.numpy as jnp
import numpy as np
from jax import lax
from jax.experimental import pallas as pl
from jax.experimental.pallas import tpu as pltpu
from jax.sharding import PartitionSpec as P

G = 128
BEAD_CH = 64
CELL = 64


bead_radius = 0.5
split_xi = 0.5
time_step = 0.01
fene_k = 30.0
fene_reach = 1.5
bend_k = 2.0
grid_spacing = 4.0
pair_block = 64


def shifted(value, axis, by):
    devices = lax.axis_size(axis)
    return lax.ppermute(value, axis, [(i, (i + by) % devices) for i in range(devices)])


UNROLL = 16

SMEM_SPEC = pl.BlockSpec(memory_space=pltpu.SMEM)
VMEM_SPEC = pl.BlockSpec(memory_space=pltpu.VMEM)


def lane_index(rows):
    return lax.broadcasted_iota(jnp.int32, (rows, 128), 1)


def window(table, at, rows):
    row = lax.shift_right_logical(at, 7)
    lead = at & 127
    head = pltpu.roll(table[pl.ds(row, rows), :], (128 - lead) & 127, 1)
    tail = pltpu.roll(table[pl.ds(row + 1, rows), :], (128 - lead) & 127, 1)
    return jnp.where(lane_index(rows) < 128 - lead, head, tail)


def slots_kernel(starts, route_ref, out_ref, table, *, rows, depth):
    table[pl.ds(0, rows), :] = route_ref[...]
    table[pl.ds(rows, depth + 8), :] = jnp.zeros((depth + 8, 128), jnp.int32)
    place = lane_index(depth) + lax.broadcasted_iota(jnp.int32, (depth, 128), 0) * 128

    @pl.loop(0, out_ref.shape[0])
    def _(t):
        at = starts[t]
        slot = window(table, at, depth) - t * (depth * 128)
        out_ref[t] = jnp.where(place < starts[t + 1] - at, slot, -1)


def slots_call(starts, route, depth):
    rows = route.shape[0]
    peers = starts.shape[0] - 1
    return pl.pallas_call(
        functools.partial(slots_kernel, rows=rows, depth=depth),
        out_shape=jax.ShapeDtypeStruct((peers, depth, 128), jnp.int32),
        in_specs=[SMEM_SPEC, VMEM_SPEC],
        out_specs=VMEM_SPEC,
        scratch_shapes=[pltpu.VMEM((rows + depth + 8, 128), jnp.int32)],
        name="slots",
    )(starts, route)


def chain_forces(pos):
    rows = pos[0].shape[0]
    place = lane_index(rows) & (BEAD_CH - 1)
    bonded = place < BEAD_CH - 1
    bent = place < BEAD_CH - 2
    after = (place > 0) & bonded
    bond = [jnp.where(bonded, pltpu.roll(x, 127, 1) - x, 0.5) for x in pos]
    square = bond[0] * bond[0] + bond[1] * bond[1] + bond[2] * bond[2]
    inverse = lax.rsqrt(square)
    unit = [b * inverse for b in bond]
    following = [pltpu.roll(u, 127, 1) for u in unit]
    previous = [pltpu.roll(u, 1, 1) for u in unit]
    cosine = sum(u * v for u, v in zip(unit, following))
    cosine_before = pltpu.roll(cosine, 1, 1)
    pull = fene_k / (1.0 - square / fene_reach**2)
    out = []
    for c in range(3):
        turn = jnp.where(bent, following[c] - cosine * unit[c], 0.0)
        turn = turn + jnp.where(after, previous[c] - cosine_before * unit[c], 0.0)
        slope = jnp.where(bonded, pull * bond[c] - bend_k * inverse * turn, 0.0)
        out.append(slope - pltpu.roll(slope, 1, 1))
    return out


def pack_kernel(starts, pos_ref, out_ref, table, *, rows, depth, stride):
    step = 8

    @pl.loop(0, rows // step)
    def _(i):
        at = pl.multiple_of(i * step, step)
        pos = [pos_ref[c, pl.ds(at, step), :] for c in range(3)]
        for c, value in enumerate(pos + chain_forces(pos)):
            table[pl.ds(c * stride + at, step), :] = value

    for c in range(6):
        table[pl.ds(c * stride + rows, stride - rows), :] = jnp.zeros((stride - rows, 128), jnp.float32)

    @pl.loop(0, out_ref.shape[0])
    def _(t):
        at = starts[t]
        for c in range(6):
            out_ref[t, c * depth : (c + 1) * depth, :] = window(table, at + c * stride * 128, depth)


def pack_call(starts, pos, depth):
    rows = pos.shape[1]
    peers = starts.shape[0] - 1
    stride = rows + depth + 8
    stride += -stride % 8
    return pl.pallas_call(
        functools.partial(pack_kernel, rows=rows, depth=depth, stride=stride),
        out_shape=jax.ShapeDtypeStruct((peers, 6 * depth, 128), jnp.float32),
        in_specs=[SMEM_SPEC, VMEM_SPEC],
        out_specs=VMEM_SPEC,
        scratch_shapes=[pltpu.VMEM((6 * stride, 128), jnp.float32)],
        name="pack",
    )(starts, pos)


def nodes_kernel(slots_ref, perm_ref, out_ref, *, depth, spare):
    tile = 8 if depth % 8 == 0 else 1

    @pl.loop(0, slots_ref.shape[0])
    def _(t):
        rows = [jnp.broadcast_to(perm_ref[t, w : w + 1, :], (8, 128)) for w in range(depth)]
        for r in range(depth // tile):
            slot = jnp.broadcast_to(slots_ref[t, r * tile : (r + 1) * tile, :], (8, 128))
            place = slot & 127
            which = slot >> 7
            node = jnp.full((8, 128), spare, jnp.int32)
            for w in range(depth):
                node = jnp.where(which == w, jnp.take_along_axis(rows[w], place, axis=1), node)
            out_ref[t, r * tile : (r + 1) * tile, :] = node[:tile]


def nodes_call(slots, perm, spare):
    return pl.pallas_call(
        functools.partial(nodes_kernel, depth=slots.shape[1], spare=spare),
        out_shape=jax.ShapeDtypeStruct(slots.shape, jnp.int32),
        in_specs=[VMEM_SPEC] * 2,
        out_specs=VMEM_SPEC,
        name="nodes",
    )(slots, perm)


def scatter_kernel(nodes, counts, in_ref, out_ref, table, rows_ref, *, depth, rp):
    t = pl.program_id(0)

    @pl.when(t == 0)
    def _():
        @pl.loop(0, rp)
        def _(k):
            table[pl.ds(pl.multiple_of(k * 128, 128), 128), :] = jnp.zeros((128, 128), jnp.float32)

    for r in range(depth):
        piece = in_ref[0, pl.ds(r, 6, stride=depth), :]
        piece = jnp.concatenate([piece, jnp.zeros((2, 128), jnp.float32)], axis=0)
        rows_ref[r * 128 : (r + 1) * 128, 0:8] = jnp.transpose(piece)

    base = t * (depth * 128)

    def some(i, carry):
        at = pl.multiple_of(i * UNROLL, UNROLL)
        for u in range(UNROLL):
            table[pl.ds(nodes[base + at + u], 1), :] = rows_ref[pl.ds(at + u, 1), :]
        return carry

    lax.fori_loop(0, lax.div(counts[t] + (UNROLL - 1), jnp.int32(UNROLL)), some, 0)

    @pl.when(t == pl.num_programs(0) - 1)
    def _():
        @pl.loop(0, rp, unroll=4)
        def _(k):
            turned = jnp.transpose(table[pl.ds(pl.multiple_of(k * 128, 128), 128), 0:8])
            out_ref[pl.ds(k, 6, stride=rp), :] = turned[:6]


def scatter_call(nodes, counts, data, rp):
    peers, height, _ = data.shape
    depth = height // 6
    return pl.pallas_call(
        functools.partial(scatter_kernel, depth=depth, rp=rp),
        out_shape=jax.ShapeDtypeStruct((6 * rp, 128), jnp.float32),
        grid=(peers,),
        in_specs=[SMEM_SPEC, SMEM_SPEC, pl.BlockSpec((1, height, 128), lambda t: (t, 0, 0))],
        out_specs=VMEM_SPEC,
        scratch_shapes=[pltpu.VMEM((rp * 128 + 8, 128), jnp.float32), pltpu.VMEM((depth * 128, 128), jnp.float32)],
        compiler_params=pltpu.CompilerParams(vmem_limit_bytes=52 * 1024 * 1024),
        name="scatter",
    )(nodes, counts, data)


def gather_kernel(nodes, counts, one_ref, two_ref, three_ref, out_ref, table, rows_ref, *, depth, rp):
    t = pl.program_id(0)

    @pl.when(t == 0)
    def _():
        @pl.loop(0, rp, unroll=4)
        def _(k):
            at = pl.ds(k, 3, stride=rp)
            value = one_ref[at, :] + two_ref[at, :] + three_ref[at, :]
            value = jnp.concatenate([value, jnp.zeros((5, 128), jnp.float32)], axis=0)
            table[pl.ds(pl.multiple_of(k * 128, 128), 128), 0:8] = jnp.transpose(value)

    base = t * (depth * 128)

    def some(i, carry):
        at = pl.multiple_of(i * UNROLL, UNROLL)
        for u in range(UNROLL):
            rows_ref[pl.ds(at + u, 1), :] = table[pl.ds(nodes[base + at + u], 1), :]
        return carry

    lax.fori_loop(0, lax.div(counts[t] + (UNROLL - 1), jnp.int32(UNROLL)), some, 0)
    for r in range(depth):
        turned = jnp.transpose(rows_ref[r * 128 : (r + 1) * 128, 0:8])
        out_ref[0, pl.ds(r, 3, stride=depth), :] = turned[:3]


def gather_call(nodes, counts, one, two, three, depth):
    rp = one.shape[0] // 3
    peers = counts.shape[0]
    return pl.pallas_call(
        functools.partial(gather_kernel, depth=depth, rp=rp),
        out_shape=jax.ShapeDtypeStruct((peers, 3 * depth, 128), jnp.float32),
        grid=(peers,),
        in_specs=[SMEM_SPEC, SMEM_SPEC] + [VMEM_SPEC] * 3,
        out_specs=pl.BlockSpec((1, 3 * depth, 128), lambda t: (t, 0, 0)),
        scratch_shapes=[pltpu.VMEM((rp * 128 + 8, 128), jnp.float32), pltpu.VMEM((depth * 128, 128), jnp.float32)],
        compiler_params=pltpu.CompilerParams(vmem_limit_bytes=52 * 1024 * 1024),
        name="gather",
    )(nodes, counts, one, two, three)


def finish_kernel(starts, in_ref, pos_ref, noise_ref, moved_ref, drift_ref, table, *, rows, depth, stride):
    lane = lane_index(depth)
    first = lane_index(1)

    @pl.loop(0, in_ref.shape[0])
    def _(t):
        at = starts[t]
        row = lax.shift_right_logical(at, 7)
        lead = at & 127
        for c in range(3):
            value = pltpu.roll(in_ref[t, c * depth : (c + 1) * depth, :], lead, 1)
            here = pl.ds(c * stride + row, depth)
            behind = pl.ds(c * stride + row + 1, depth)
            edge = table[pl.ds(c * stride + row, 1), :]
            table[behind, :] = value
            if depth > 1:
                body = jnp.where(lane[1:] < lead, value[:-1], value[1:])
                table[pl.ds(c * stride + row + 1, depth - 1), :] = body
            table[pl.ds(c * stride + row, 1), :] = jnp.where(first < lead, edge, value[:1])

    step = 8

    @pl.loop(0, rows // step)
    def _(i):
        at = pl.multiple_of(i * step, step)
        for c in range(3):
            drift = time_step * table[pl.ds(c * stride + at, step), :]
            drift_ref[c, pl.ds(at, step), :] = drift
            moved_ref[c, pl.ds(at, step), :] = pos_ref[c, pl.ds(at, step), :] + drift + noise_ref[c, pl.ds(at, step), :]


def finish_call(starts, data, pos, noise):
    rows = pos.shape[1]
    depth = data.shape[1] // 3
    stride = rows + depth + 8
    stride += -stride % 8
    return pl.pallas_call(
        functools.partial(finish_kernel, rows=rows, depth=depth, stride=stride),
        out_shape=(jax.ShapeDtypeStruct(pos.shape, jnp.float32),) * 2,
        in_specs=[SMEM_SPEC] + [VMEM_SPEC] * 3,
        out_specs=(VMEM_SPEC,) * 2,
        scratch_shapes=[pltpu.VMEM((3 * stride, 128), jnp.float32)],
        name="finish",
    )(starts, data, pos, noise)


ERFCX_COEF = (0.06548172872398669,
    -0.3609186250151195,
    0.6338942267842493,
    -0.3384301108125971,
    0.4003704641202259,
    0.13581047899030682,
    0.2395463173952274,
    0.22417089752024144,
    7.010614160106155e-05)


def pair_math(square, coef):
    inverse = lax.rsqrt(square)
    ratio = pl.reciprocal(1.0 + 0.2 * (square * inverse))
    scaled = coef[0] * ratio + coef[1]
    for k in coef[2:]:
        scaled = scaled * ratio + k
    decay = jnp.exp(-0.25 * square)
    inverse_sq = inverse * inverse
    screen = scaled * inverse
    along = decay * (screen * (0.375 + 0.0625 * inverse_sq) + 0.125)
    across = (decay * inverse_sq) * (screen * (0.375 - 0.1875 * inverse_sq) - 0.125)
    return along, across

def pair_kernel(first, second, count, own_ref, far_ref, vown_ref, vfar_ref, cells, sums, *, rp, coef, unroll):
    lane = lax.broadcasted_iota(jnp.int32, (8, 128), 1)
    sub = lax.broadcasted_iota(jnp.int32, (8, 128), 0)
    left = lane < 64
    unturn = (lane + sub) & 127

    @pl.loop(0, rp // 8)
    def _(i):
        at = pl.ds(pl.multiple_of(i * 8, 8), 8)
        for src, off in ((own_ref, 0), (far_ref, rp)):
            for c in range(6):
                cells[pl.ds((off + i * 8) * 8 + c, 8, stride=8), :] = src[c, at, :]
            sums[pl.ds(pl.multiple_of((off + i * 8) * 8, 64), 64), :] = jnp.zeros((64, 128), jnp.float32)

    def both_halves(k):
        cell = cells[pl.ds(pl.multiple_of((k >> 1) * 8, 8), 8), :]
        return jnp.where(left == ((k & 1) == 0), cell, pltpu.roll(cell, 64, 1))

    def stacked(parts):
        out = jnp.zeros((8, 128), jnp.float32)
        for c, part in enumerate(parts):
            out = jnp.where(sub == c, jnp.sum(part, axis=0, keepdims=True), out)
        return out

    def one(p):
        ka = first[p]
        kb = second[p]
        near = both_halves(ka)
        near = jnp.where(left, near, pltpu.roll(near, 96, 1))
        far = both_halves(kb)
        mine = [jnp.broadcast_to(near[c : c + 1, :], (8, 128)) for c in range(6)]
        other = [jnp.broadcast_to(far[c : c + 1, :], (8, 128)) for c in range(6)]
        near_sum = None
        far_sum = None
        for q in (3, 2, 1, 0):
            turned = [pltpu.roll(x, 8 * q, 1, stride=1, stride_axis=0) for x in other]
            gap = [mine[c] - turned[c] for c in range(3)]
            along, across = pair_math(gap[0] * gap[0] + gap[1] * gap[1] + gap[2] * gap[2] + 0.25, coef)
            to_near = across * (gap[0] * turned[3] + gap[1] * turned[4] + gap[2] * turned[5])
            to_far = across * (gap[0] * mine[3] + gap[1] * mine[4] + gap[2] * mine[5])
            near_add = [along * turned[3 + c] + to_near * gap[c] for c in range(3)]
            far_add = [along * mine[3 + c] + to_far * gap[c] for c in range(3)]
            if near_sum is None:
                near_sum, far_sum = near_add, far_add
            else:
                near_sum = [a + b for a, b in zip(near_sum, near_add)]
                far_sum = [pltpu.roll(a, 120, 1) + b for a, b in zip(far_sum, far_add)]
        far_sum = [jnp.take_along_axis(a, unturn, axis=1) for a in far_sum]
        near_vel = stacked(near_sum)
        half = jnp.where(left, pltpu.roll(near_vel, 64, 1), 0.0)
        near_vel = jnp.where(left, near_vel, 0.0) + pltpu.roll(half, 32, 1)
        near_vel = near_vel + pltpu.roll(near_vel, 64, 1)
        far_vel = stacked(far_sum)
        far_vel = far_vel + pltpu.roll(far_vel, 64, 1)
        return ka, near_vel, kb, far_vel

    total = count[0]

    def turn(i, carry):
        found = []
        for k in range(unroll):
            p = i * unroll + k
            found.append((p < total, one(p)))
        for alive, (ka, near_vel, kb, far_vel) in found:
            at = pl.ds(pl.multiple_of((ka >> 1) * 8, 8), 8)
            sums[at, :] = sums[at, :] + jnp.where((left == ((ka & 1) == 0)) & alive, near_vel, 0.0)
            at = pl.ds(pl.multiple_of((kb >> 1) * 8, 8), 8)
            keep = (left == ((kb & 1) == 0)) & (alive & (ka != kb))
            sums[at, :] = sums[at, :] + jnp.where(keep, far_vel, 0.0)
        return carry

    lax.fori_loop(0, lax.div(total + (unroll - 1), jnp.int32(unroll)), turn, 0)

    @pl.loop(0, rp // 8)
    def _(i):
        at = pl.ds(pl.multiple_of(i * 8, 8), 8)
        for dst, off in ((vown_ref, 0), (vfar_ref, rp)):
            for c in range(3):
                dst[c, at, :] = sums[pl.ds((off + i * 8) * 8 + c, 8, stride=8), :]

def pair_call(first, second, count, own, far, coef=ERFCX_COEF, unroll=8):
    rp = own.shape[1]
    f32 = jnp.float32
    return pl.pallas_call(
        functools.partial(pair_kernel, rp=rp, coef=coef, unroll=unroll),
        out_shape=(jax.ShapeDtypeStruct((3, rp, 128), f32),)*2,
        in_specs=[pl.BlockSpec(memory_space=pltpu.SMEM)]*3 + [pl.BlockSpec(memory_space=pltpu.VMEM)]*2,
        out_specs=(pl.BlockSpec(memory_space=pltpu.VMEM),)*2,
        scratch_shapes=[pltpu.VMEM((2*rp*8, 128), f32), pltpu.VMEM((2*rp*8, 128), f32)],
        compiler_params=pltpu.CompilerParams(vmem_limit_bytes=48*1024*1024),
        name="pairs",
    )(first, second, count, own, far)


def signed_wave(grid_index):
    return jnp.where(grid_index < G // 2, grid_index, grid_index - G).astype(jnp.float32) * (
        2.0 * math.pi / (G * grid_spacing)
    )


def forward_pass(real_in, imag_in, form, cos_part, sin_part):
    contract = partial(jnp.einsum, precision=lax.Precision.HIGHEST)
    real_out = contract(form, real_in, cos_part) + contract(form, imag_in, sin_part)
    imag_out = contract(form, imag_in, cos_part) - contract(form, real_in, sin_part)
    return (real_out, imag_out)


def inverse_pass(real_in, imag_in, form, cos_part, sin_part):
    contract = partial(jnp.einsum, precision=lax.Precision.HIGHEST)
    real_out = contract(form, real_in, cos_part) - contract(form, imag_in, sin_part)
    imag_out = contract(form, imag_in, cos_part) + contract(form, real_in, sin_part)
    return (real_out, imag_out)


def project_flow(spectrum, wave_x, wave_y, wave_z):
    wave_sq = wave_x * wave_x + wave_y * wave_y + wave_z * wave_z
    wave_safe = jnp.where(wave_sq > 0, wave_sq, 1.0)
    spread_sq = wave_sq / (4.0 * split_xi**2)
    green_fn = jnp.where(
        wave_sq > 0,
        (1.0 - bead_radius**2 * wave_sq / 3.0)
        * (1.0 + spread_sq)
        * jnp.exp(-spread_sq)
        / wave_safe,
        0.0,
    )
    along_wave = (wave_x * spectrum[0] + wave_y * spectrum[1] + wave_z * spectrum[2]) / wave_safe
    return jnp.stack(
        [
            green_fn * (spectrum[0] - wave_x * along_wave),
            green_fn * (spectrum[1] - wave_y * along_wave),
            green_fn * (spectrum[2] - wave_z * along_wave),
        ]
    )


def kspace_part(force_rows, n_gx, n_gy):
    local_x = G // n_gx
    local_y = G // n_gy
    grid_index = jnp.arange(G, dtype=jnp.int32)
    phase_grid = (grid_index[:, None] * grid_index[None, :] % G).astype(jnp.float32) * (
        2.0 * math.pi / G
    )
    cosine_table = jnp.cos(phase_grid)
    sine_table = jnp.sin(phase_grid)
    contract = partial(jnp.einsum, precision=lax.Precision.HIGHEST)
    force_field = force_rows.reshape(3, local_x, local_y, G)
    wave_full = signed_wave(grid_index)
    row_gx = lax.axis_index("gx")
    row_gy = lax.axis_index("gy")
    freq_count = G
    spec_z = jnp.stack(
        [
            contract("cabz,zk->cabk", force_field, cosine_table),
            -contract("cabz,zk->cabk", force_field, sine_table),
        ]
    )
    cos_x = cosine_table.reshape(n_gx, local_x, G)
    sin_x = sine_table.reshape(n_gx, local_x, G)
    cos_y = cosine_table.reshape(n_gy, local_y, G)
    sin_y = sine_table.reshape(n_gy, local_y, G)
    depth_part = freq_count // n_gx
    width_part = G // n_gy
    slabs = lax.all_to_all(spec_z[:, :, None], "gx", split_axis=5, concat_axis=2, tiled=True)
    xr_part, xi_part = forward_pass(slabs[0], slabs[1], "ciabl,iak->cbkl", cos_x, sin_x)
    pencils = lax.all_to_all(
        jnp.stack([xr_part, xi_part])[:, :, None], "gy", split_axis=4, concat_axis=2, tiled=True
    )
    yr_part, yi_part = forward_pass(pencils[0], pencils[1], "cjbkl,jbm->ckml", cos_y, sin_y)
    wave_x = signed_wave(row_gy * width_part + jnp.arange(width_part, dtype=jnp.int32))[
        :, None, None
    ]
    wave_y = wave_full[None, :, None]
    wave_z = signed_wave(row_gx * depth_part + jnp.arange(depth_part, dtype=jnp.int32))[
        None, None, :
    ]
    flow_real = project_flow(yr_part, wave_x, wave_y, wave_z)
    flow_imag = project_flow(yi_part, wave_x, wave_y, wave_z)
    br_part, bi_part = inverse_pass(flow_real, flow_imag, "ckml,jbm->cjbkl", cos_y, sin_y)
    back = lax.all_to_all(
        jnp.stack([br_part, bi_part]), "gy", split_axis=2, concat_axis=4, tiled=True
    )[:, :, 0]
    ar_part, ai_part = inverse_pass(back[0], back[1], "cbkl,iak->ciabl", cos_x, sin_x)
    gathered = lax.all_to_all(
        jnp.stack([ar_part, ai_part]), "gx", split_axis=2, concat_axis=5, tiled=True
    )[:, :, 0]
    result = contract("cabk,zk->cabz", gathered[0], cosine_table) - contract(
        "cabk,zk->cabz", gathered[1], sine_table
    )
    return (result / float(G**3)).reshape(3, local_x * local_y * G)


matmul = functools.partial(lax.dot_general, precision=lax.Precision.HIGHEST, preferred_element_type=jnp.float32)
PLAIN = (((1,), (0,)), ((), ()))
TURNED = (((1,), (1,)), ((), ()))


def wave_tables(n_gx, n_gy):
    share = G // 2 // n_gx
    width = G // n_gy
    grid = np.arange(G)
    turn = 2.0 * math.pi * (np.outer(grid, grid) % G) / G
    cos, sin = np.cos(turn), np.sin(turn)
    half = width // 2
    order = np.zeros(G, np.int64)
    for j in range(n_gy):
        for p in range(half):
            k = j * half + p
            order[j * width + p] = k
            order[j * width + half + p] = (G - k) % G if k else G // 2
    ahead = np.zeros((G, n_gx, 2, share))
    ahead[:, :, 0] = cos[:, : G // 2].reshape(G, n_gx, share)
    ahead[:, :, 1] = -sin[:, : G // 2].reshape(G, n_gx, share)
    back = 2.0 * ahead
    ahead[:, 0, 1, 0] = cos[:, G // 2]
    back[:, 0, 0, 0] = 1.0
    back[:, 0, 1, 0] = cos[:, G // 2]
    unit = 2.0 * math.pi / (G * grid_spacing)
    signed = np.where(grid < G // 2, grid, grid - G) * unit
    plain = np.where(grid == G // 2, 0.0, signed)
    edge = signed - plain
    lane = np.arange(128)
    across = np.zeros((n_gy, 8, 128))
    across[:, 0] = plain[order].reshape(n_gy, 1, width)[:, 0][:, lane % width]
    across[:, 1] = edge[order].reshape(n_gy, 1, width)[:, 0][:, lane % width]
    across[0, 2] = lane % half == 0
    deep = np.zeros((n_gx, 8, 128))
    per = 128 // width
    for v in range(share // per):
        deep[:, v] = (np.arange(n_gx)[:, None] * share + v * per + lane // width) * unit
    down = np.stack([np.broadcast_to(t[:, None], (G, 128)) for t in (plain, edge)])
    tables = {
        "ahead": ahead.reshape(G, G),
        "back": back.reshape(G, G).T,
        "first": np.concatenate([cos[:, order], sin[:, order]], axis=1),
        "first_back": np.concatenate([cos[:, order], sin[:, order]], axis=1),
        "second": np.concatenate([cos, sin], axis=0),
        "across": across,
        "deep": deep,
        "down": down,
    }
    return {name: np.asarray(table, np.float32) for name, table in tables.items()}


def spread(tiles, at, group, tall):
    count = 128 // group
    lane = lax.shift_right_logical(lax.broadcasted_iota(jnp.int32, (tall, 128), 1), group.bit_length() - 1)
    out = None
    for g, tile in enumerate(tiles):
        moved = pltpu.roll(tile, group * ((g - at) % count), 1) if g != at else tile
        out = moved if out is None else jnp.where(lane == g, moved, out)
    return out


def depth_kernel(field_ref, table_ref, out_ref, spec, *, n_gx, tall, wide):
    rows = tall * wide
    for c in range(3):
        spec[c * rows : (c + 1) * rows, :] = matmul(field_ref[c * rows : (c + 1) * rows, :], table_ref[...], PLAIN)
    group = G // n_gx
    count = n_gx

    @pl.loop(0, 3 * wide // count)
    def _(i):
        c = lax.div(i, jnp.int32(wide // count))
        b = (i - c * (wide // count)) * count
        tiles = [spec[pl.ds(c * rows + b + g, tall, stride=wide), :] for g in range(count)]
        for p in range(n_gx):
            out_ref[p, :, pl.ds(pl.multiple_of(i * 128, 128), 128)] = spread(tiles, p, group, tall)


def first_kernel(data_ref, table_ref, out_ref, turned, *, n_gy, share, wide):
    group = G // n_gy
    per = 128 // (2 * share)

    @pl.loop(0, 3 * wide // per)
    def _(i):
        c = lax.div(i, jnp.int32(wide // per))
        b = (i - c * (wide // per)) * per
        piece = jnp.transpose(data_ref[:, pl.ds(pl.multiple_of(i * 128, 128), 128)])
        both = matmul(piece, table_ref[...], PLAIN)
        for g in range(per):
            lo, mid, hi = g * 2 * share, (g * 2 + 1) * share, (g * 2 + 2) * share
            real = both[lo:mid, :128] + both[mid:hi, 128:]
            imag = both[mid:hi, :128] - both[lo:mid, 128:]
            turned[pl.ds(2 * c * share * wide + b + g, share, stride=wide), :] = real
            turned[pl.ds((2 * c + 1) * share * wide + b + g, share, stride=wide), :] = imag

    count = 128 // group

    @pl.loop(0, 6 * share // count)
    def _(i):
        at = i * (count * wide)
        tiles = [turned[pl.ds(pl.multiple_of(at + u * wide, 8), wide), :] for u in range(count)]
        for j in range(n_gy):
            out_ref[j, i] = spread(tiles, j, group, wide)


def second_kernel(ids, data_ref, table_ref, across_ref, deep_ref, down_ref, out_ref, flow, *, n_gy, views, wide):
    lane = lax.broadcasted_iota(jnp.int32, (G, 128), 1)
    width = G // n_gy
    half = width // 2
    across = across_ref[ids[1]]
    deep = deep_ref[ids[0]]
    alone = (lane < width) & (ids[0] == 0)
    mirror_self = across[2:3, :] > 0.5
    upper = (lane & half) != 0

    def whole(tile):
        return jnp.concatenate([data_ref[j, tile] for j in range(n_gy)], axis=0)

    def mirrored(value):
        other = jnp.where(upper, pltpu.roll(value, half, 1), pltpu.roll(value, 128 - half, 1))
        return jnp.where(mirror_self, value, other)

    def ahead(real, imag):
        one = matmul(table_ref[...], real, PLAIN)
        two = matmul(table_ref[...], imag, PLAIN)
        return one[:G] + two[G:], two[:G] - one[G:]

    def projected(spectrum, deep_plain, deep_edge):
        plain = (across[0:1, :], down_ref[0], deep_plain)
        edge = (across[1:2, :], down_ref[1], deep_edge)
        waves = [p + e for p, e in zip(plain, edge)]
        wave_sq = waves[0] * waves[0] + waves[1] * waves[1] + waves[2] * waves[2]
        live = wave_sq > 0
        inverse = 1.0 / jnp.where(live, wave_sq, 1.0)
        spread_sq = wave_sq / (4.0 * split_xi**2)
        green = (1.0 - bead_radius**2 * wave_sq / 3.0) * (1.0 + spread_sq) * jnp.exp(-spread_sq) * inverse
        green = jnp.where(live, green / float(G**3), 0.0)
        out = []
        for r in range(2):
            regular = sum(w * spectrum[c][r] for c, w in enumerate(plain)) * inverse
            nyquist = sum(w * spectrum[c][r] for c, w in enumerate(edge)) * inverse
            out.append([green * (spectrum[c][r] - plain[c] * regular - edge[c] * nyquist) for c in range(3)])
        return out

    zero = jnp.zeros((1, 128), jnp.float32)
    for v in range(views):
        spectrum = []
        apart = []
        for c in range(3):
            real = whole((2 * c) * views + v)
            imag = whole((2 * c + 1) * views + v)
            if v == 0:
                off_real = jnp.where(alone, 0.5 * (real - mirrored(real)), 0.0)
                off_imag = jnp.where(alone, 0.5 * (imag + mirrored(imag)), 0.0)
                apart.append(ahead(off_real, off_imag))
                real, imag = real - off_real, imag - off_imag
            spectrum.append(ahead(real, imag))
        found = projected(spectrum, deep[v : v + 1, :], zero)
        if v == 0:
            extra = projected(apart, zero, zero - math.pi / grid_spacing)
            found = [[a + b for a, b in zip(one, two)] for one, two in zip(found, extra)]
        for c in range(3):
            one = matmul(table_ref[...], found[0][c], PLAIN)
            two = matmul(table_ref[...], found[1][c], PLAIN)
            real, imag = one[:G] - two[G:], two[:G] + one[G:]
            for j in range(n_gy):
                out_ref[j, (2 * c) * views + v] = real[j * wide : (j + 1) * wide]
                out_ref[j, (2 * c + 1) * views + v] = imag[j * wide : (j + 1) * wide]


def first_back_kernel(data_ref, table_ref, out_ref, turned, *, n_gy, share, wide):
    group = G // n_gy
    count = n_gy
    per = 128 // (2 * share)

    @pl.loop(0, 6 * share // count)
    def _(i):
        tiles = [data_ref[j, i] for j in range(n_gy)]
        for u in range(count):
            turned[pl.ds(pl.multiple_of((i * count + u) * wide, 8), wide), :] = spread(tiles, u, group, wide)

    @pl.loop(0, 3 * wide // per)
    def _(i):
        c = lax.div(i, jnp.int32(wide // per))
        b = (i - c * (wide // per)) * per
        rows = []
        for g in range(per):
            real = turned[pl.ds(2 * c * share * wide + b + g, share, stride=wide), :]
            imag = turned[pl.ds((2 * c + 1) * share * wide + b + g, share, stride=wide), :]
            rows.append(jnp.concatenate([real, -imag], axis=1))
            rows.append(jnp.concatenate([imag, real], axis=1))
        piece = jnp.concatenate(rows, axis=0)
        out_ref[:, pl.ds(pl.multiple_of(i * 128, 128), 128)] = matmul(table_ref[...], piece, TURNED)


def depth_back_kernel(data_ref, table_ref, out_ref, spec, *, n_gx, tall, wide):
    rows = tall * wide
    group = G // n_gx
    count = n_gx

    @pl.loop(0, 3 * wide // count)
    def _(i):
        c = lax.div(i, jnp.int32(wide // count))
        b = (i - c * (wide // count)) * count
        tiles = [data_ref[p, :, pl.ds(pl.multiple_of(i * 128, 128), 128)] for p in range(n_gx)]
        for g in range(count):
            spec[pl.ds(c * rows + b + g, tall, stride=wide), :] = spread(tiles, g, group, tall)

    for c in range(3):
        out_ref[c * rows : (c + 1) * rows, :] = matmul(spec[c * rows : (c + 1) * rows, :], table_ref[...], PLAIN)


def waves(grid_data, n_gx, n_gy):
    tall, wide, share = G // n_gx, G // n_gy, G // 2 // n_gx
    rows = 3 * tall * wide
    views = share * wide // 128
    tables = wave_tables(n_gx, n_gy)
    f32 = jnp.float32

    def run(name, kernel, shape, args, scratch, specs=None, **sizes):
        return pl.pallas_call(
            functools.partial(kernel, **sizes),
            out_shape=jax.ShapeDtypeStruct(shape, f32),
            in_specs=specs or [VMEM_SPEC] * len(args),
            out_specs=VMEM_SPEC,
            scratch_shapes=[pltpu.VMEM(scratch, f32)],
            compiler_params=pltpu.CompilerParams(vmem_limit_bytes=24 * 1024 * 1024),
            name=name,
            grid=(1,),
        )(*args)

    def swap(value, axis):
        return lax.all_to_all(value, axis, split_axis=0, concat_axis=0, tiled=True)

    def full(shape):
        return pl.BlockSpec(shape, lambda i: (0,) * len(shape))

    force = pl.BlockSpec((rows, 128), lambda i: (1, 0))
    lanes = 6 * wide * share
    ids = jnp.stack([lax.axis_index("gx"), lax.axis_index("gy")]).astype(jnp.int32)
    value = run("depth", depth_kernel, (n_gx, tall, lanes), (grid_data, tables["ahead"]), (rows, 128),
                [force, full((G, 128))], n_gx=n_gx, tall=tall, wide=wide)
    value = swap(value, "gx").reshape(G, lanes)
    value = run("first", first_kernel, (n_gy, 6 * views, wide, 128), (value, tables["first"]), (rows, 128),
                n_gy=n_gy, share=share, wide=wide)
    value = swap(value.reshape(n_gy, 6 * views * wide, 128), "gy").reshape(n_gy, 6 * views, wide, 128)
    args = (ids, value, tables["second"], tables["across"], tables["deep"], tables["down"])
    value = run("second", second_kernel, (n_gy, 6 * views, wide, 128), args, (8, 128),
                [SMEM_SPEC] + [VMEM_SPEC] * 5, n_gy=n_gy, views=views, wide=wide)
    value = swap(value.reshape(n_gy, 6 * views * wide, 128), "gy").reshape(n_gy, 6 * views, wide, 128)
    value = run("first_back", first_back_kernel, (G, lanes), (value, tables["first_back"]), (rows, 128),
                n_gy=n_gy, share=share, wide=wide)
    value = swap(value.reshape(n_gx, tall, lanes), "gx")
    return run("depth_back", depth_back_kernel, (rows, 128), (value, tables["back"]), (rows, 128),
               n_gx=n_gx, tall=tall, wide=wide)


def shards(positions, noise, route, node_perm, pair_first, pair_second, pair_count):
    n_gx = lax.axis_size("gx")
    n_gy = lax.axis_size("gy")
    both = ("gx", "gy")
    peers = n_gx * n_gy
    slots = node_perm.shape[2]
    depth = slots // peers // 128
    rows = positions.shape[1] // 128
    rp = slots // 128
    swap = partial(lax.all_to_all, axis_name=both, split_axis=0, concat_axis=0, tiled=True)

    bounds = jnp.arange(peers + 1, dtype=jnp.int32) * (slots // peers)
    starts = jnp.sum(route[None, :] < bounds[:, None], axis=1, dtype=jnp.int32)
    taken = swap(slots_call(starts, route.reshape(rows, 128), depth))
    places = positions.reshape(3, rows, 128)
    data = swap(pack_call(starts, places, depth))
    counts = jnp.sum(taken >= 0, axis=(1, 2), dtype=jnp.int32)
    own_order = lax.dynamic_index_in_dim(node_perm, lax.axis_index("gx"), 0, False)
    nodes = nodes_call(taken, own_order.reshape(peers, depth, 128), slots).reshape(slots)
    grid_data = scatter_call(nodes, counts, data, rp)

    beside_data = shifted(grid_data, "gx", -1)
    near_vel, far_vel = pair_call(
        pair_first[0],
        pair_second[0],
        pair_count,
        grid_data.reshape(6, rp, 128),
        beside_data.reshape(6, rp, 128),
    )
    share = G // 2 // n_gx
    if share % 8 == 0 and share * (G // n_gy) % 128 == 0:
        wave_vel = waves(grid_data, n_gx, n_gy)
    else:
        wave_vel = kspace_part(grid_data[3 * rp :], n_gx, n_gy).reshape(3 * rp, 128)
    back_vel = shifted(far_vel.reshape(3 * rp, 128), "gx", 1)
    back = swap(gather_call(nodes, counts, near_vel.reshape(3 * rp, 128), wave_vel, back_vel, depth))
    moved, drift = finish_call(starts, back, places, noise.reshape(3, rows, 128))
    return (moved.reshape(positions.shape), drift.reshape(positions.shape))


def solution(mesh):
    in_specs = (
        P(None, ("gx", "gy")),
        P(None, ("gx", "gy")),
        P(("gx", "gy")),
        P(None, "gy", None),
        P(("gx", "gy"), None),
        P(("gx", "gy"), None),
        P(("gx", "gy")),
    )
    out_specs = (P(None, ("gx", "gy")), P(None, ("gx", "gy")))
    return jax.shard_map(shards, mesh=mesh, in_specs=in_specs, out_specs=out_specs, check_vma=False)
```

```python
import functools
from functools import partial
import math

import jax
import jax.numpy as jnp
import numpy as np
from jax import lax
from jax.experimental import pallas as pl
from jax.experimental.pallas import tpu as pltpu
from jax.sharding import PartitionSpec as P

G = 128
BEAD_CH = 64
CELL = 64


bead_radius = 0.5
split_xi = 0.5
time_step = 0.01
fene_k = 30.0
fene_reach = 1.5
bend_k = 2.0
grid_spacing = 4.0
pair_block = 64


def shifted(value, axis, by):
    devices = lax.axis_size(axis)
    return lax.ppermute(value, axis, [(i, (i + by) % devices) for i in range(devices)])


SPAN = 16

SMEM_SPEC = pl.BlockSpec(memory_space=pltpu.SMEM)
VMEM_SPEC = pl.BlockSpec(memory_space=pltpu.VMEM)


ANY_SPEC = pl.BlockSpec(memory_space=pl.ANY)


def ignoring(kernel, inputs, extra):
    def run(*refs):
        kernel(*refs[:inputs], *refs[inputs + extra :])

    return run


def lane_index(rows):
    return lax.broadcasted_iota(jnp.int32, (rows, 128), 1)


def window(table, at, rows):
    row = lax.shift_right_logical(at, 7)
    lead = at & 127
    head = pltpu.roll(table[pl.ds(row, rows), :], (128 - lead) & 127, 1)
    tail = pltpu.roll(table[pl.ds(row + 1, rows), :], (128 - lead) & 127, 1)
    return jnp.where(lane_index(rows) < 128 - lead, head, tail)


def slots_kernel(starts, route_ref, out_ref, table, *, rows, depth):
    table[pl.ds(0, rows), :] = route_ref[...]
    table[pl.ds(rows, depth + 8), :] = jnp.zeros((depth + 8, 128), jnp.int32)
    place = lane_index(depth) + lax.broadcasted_iota(jnp.int32, (depth, 128), 0) * 128

    @pl.loop(0, out_ref.shape[0])
    def _(t):
        at = starts[t]
        slot = window(table, at, depth) - t * (depth * 128)
        out_ref[t] = jnp.where(place < starts[t + 1] - at, slot, -1)


def slots_call(starts, route, depth):
    rows = route.shape[0]
    peers = starts.shape[0] - 1
    return pl.pallas_call(
        functools.partial(slots_kernel, rows=rows, depth=depth),
        out_shape=jax.ShapeDtypeStruct((peers, depth, 128), jnp.int32),
        in_specs=[SMEM_SPEC, VMEM_SPEC],
        out_specs=VMEM_SPEC,
        scratch_shapes=[pltpu.VMEM((rows + depth + 8, 128), jnp.int32)],
        name="slots",
    )(starts, route)


def chain_forces(pos):
    rows = pos[0].shape[0]
    place = lane_index(rows) & (BEAD_CH - 1)
    bonded = place < BEAD_CH - 1
    bent = place < BEAD_CH - 2
    after = (place > 0) & bonded
    bond = [jnp.where(bonded, pltpu.roll(x, 127, 1) - x, 0.5) for x in pos]
    square = bond[0] * bond[0] + bond[1] * bond[1] + bond[2] * bond[2]
    inverse = lax.rsqrt(square)
    unit = [b * inverse for b in bond]
    following = [pltpu.roll(u, 127, 1) for u in unit]
    previous = [pltpu.roll(u, 1, 1) for u in unit]
    cosine = sum(u * v for u, v in zip(unit, following))
    cosine_before = pltpu.roll(cosine, 1, 1)
    pull = fene_k / (1.0 - square / fene_reach**2)
    out = []
    for c in range(3):
        turn = jnp.where(bent, following[c] - cosine * unit[c], 0.0)
        turn = turn + jnp.where(after, previous[c] - cosine_before * unit[c], 0.0)
        slope = jnp.where(bonded, pull * bond[c] - bend_k * inverse * turn, 0.0)
        out.append(slope - pltpu.roll(slope, 1, 1))
    return out


def pack_kernel(starts, pos_ref, out_ref, table, *, rows, depth, stride):
    step = 32 if rows % 32 == 0 else 8

    @pl.loop(0, rows // step)
    def _(i):
        at = pl.multiple_of(i * step, step)
        pos = [pos_ref[c, pl.ds(at, step), :] for c in range(3)]
        for c, value in enumerate(pos + chain_forces(pos)):
            table[pl.ds(c * stride + at, step), :] = value

    for c in range(6):
        table[pl.ds(c * stride + rows, stride - rows), :] = jnp.zeros((stride - rows, 128), jnp.float32)

    @pl.loop(0, out_ref.shape[0])
    def _(t):
        at = starts[t]
        for c in range(6):
            out_ref[t, c * depth : (c + 1) * depth, :] = window(table, at + c * stride * 128, depth)


def pack_call(starts, pos, depth):
    rows = pos.shape[1]
    peers = starts.shape[0] - 1
    stride = rows + depth + 8
    stride += -stride % 8
    return pl.pallas_call(
        functools.partial(pack_kernel, rows=rows, depth=depth, stride=stride),
        out_shape=jax.ShapeDtypeStruct((peers, 6 * depth, 128), jnp.float32),
        in_specs=[SMEM_SPEC, VMEM_SPEC],
        out_specs=VMEM_SPEC,
        scratch_shapes=[pltpu.VMEM((6 * stride, 128), jnp.float32)],
        name="pack",
    )(starts, pos)


def list_count(depth):
    return 8 if depth % 8 == 0 else 1


def nodes_kernel(slots_ref, perm_ref, node_ref, *list_refs, depth, spare):
    tile = list_count(depth)
    parts = depth // tile

    @pl.loop(0, slots_ref.shape[0])
    def _(t):
        rows = [jnp.broadcast_to(perm_ref[t, w : w + 1, :], (8, 128)) for w in range(depth)]
        for r in range(parts):
            slot = jnp.broadcast_to(slots_ref[t, r * tile : (r + 1) * tile, :], (8, 128))
            place = slot & 127
            which = slot >> 7
            node = jnp.full((8, 128), spare, jnp.int32)
            for w in range(depth):
                node = jnp.where(which == w, jnp.take_along_axis(rows[w], place, axis=1), node)
            packed = ((node >> 12) << 7) | (node & 127)
            node_ref[t, r * tile : (r + 1) * tile, :] = node[:tile]
            for u in range(tile):
                list_refs[u][pl.ds(t * parts + r, 1), :] = node[u : u + 1]
                list_refs[tile + u][pl.ds(t * parts + r, 1), :] = packed[u : u + 1]


def nodes_call(slots, perm, spare):
    peers, depth, _ = slots.shape
    lists = list_count(depth)
    one = jax.ShapeDtypeStruct((peers * depth // lists, 128), jnp.int32)
    found = pl.pallas_call(
        functools.partial(nodes_kernel, depth=depth, spare=spare),
        out_shape=(jax.ShapeDtypeStruct(slots.shape, jnp.int32),) + (one,) * (2 * lists),
        in_specs=[VMEM_SPEC] * 2,
        out_specs=(VMEM_SPEC,) * (1 + 2 * lists),
        name="nodes",
    )(slots, perm)
    flat = [x.reshape(-1) for x in found[1:]]
    return found[0], flat[:lists], flat[lists:]


def move_rows(lists, count, t, depth, move):
    width = len(lists)
    parts = depth // width

    def part(p, carry):
        live = jnp.minimum(count - p * (width * 128), 128)
        base = (t * parts + p) * 128
        start = p * (width * 128)

        def some(i, carry):
            for k in range(SPAN):
                at = i * SPAN + k
                for u in range(width):
                    move(start + at + u * 128, lists[u][base + at])
            return carry

        return lax.fori_loop(0, lax.div(live + (SPAN - 1), jnp.int32(SPAN)), some, carry)

    whole = width * 128
    lax.fori_loop(0, lax.div(count + (whole - 1), jnp.int32(whole)), part, 0)


def scatter_kernel(counts, in_ref, *refs, depth, rp, lists):
    nodes = refs[:lists]
    out_ref, cells_ref, table, rows_ref = refs[lists:]

    @pl.loop(0, rp)
    def _(k):
        table[pl.ds(pl.multiple_of(k * 128, 128), 128), :] = jnp.zeros((128, 128), jnp.float32)

    together = 4 if depth % 4 == 0 else 1

    @pl.loop(0, in_ref.shape[0])
    def _(t):
        def turn(i, carry):
            for j in range(together):
                r = i * together + j
                piece = in_ref[t, pl.ds(r, 6, stride=depth), :]
                piece = jnp.concatenate([piece, jnp.zeros((2, 128), jnp.float32)], axis=0)
                piece = jnp.concatenate([piece] * 16, axis=0)
                rows_ref[pl.ds(pl.multiple_of(r * 128, 128), 128), :] = jnp.transpose(piece)
            return carry

        def move(at, node):
            table[pl.ds(node, 1), :] = rows_ref[pl.ds(at, 1), :]

        count = counts[t]
        part = together * 128
        lax.fori_loop(0, lax.div(count + (part - 1), jnp.int32(part)), turn, 0)
        move_rows(nodes, count, t, depth, move)

    group = lane_index(8) >> 3

    @pl.loop(0, rp // 16)
    def _(g):
        tiles = []
        for i in range(16):
            tile = table[pl.ds(pl.multiple_of(g * 2048, 2048) + 8 * i, 8), :]
            for k in range(1, 16):
                one = table[pl.ds(pl.multiple_of(g * 2048, 2048) + k * 128 + 8 * i, 8), :]
                tile = jnp.where(group == k, one, tile)
            tiles.append(tile)
        at = pl.multiple_of(g * 128, 128)
        cells_ref[pl.ds(at, 128), :] = jnp.transpose(jnp.concatenate(tiles, axis=0))
        for c in range(6):
            out_ref[pl.ds(pl.multiple_of(c * rp + g * 16, 16), 16), :] = cells_ref[pl.ds(at + c, 16, stride=8), :]


def scatter_call(nodes, counts, data, rp, after=()):
    depth = data.shape[1] // 6
    return pl.pallas_call(
        ignoring(
            functools.partial(scatter_kernel, depth=depth, rp=rp, lists=len(nodes)), 2 + len(nodes), len(after)
        ),
        out_shape=(
            jax.ShapeDtypeStruct((6 * rp, 128), jnp.float32),
            jax.ShapeDtypeStruct((8 * rp, 128), jnp.float32),
        ),
        in_specs=[SMEM_SPEC, VMEM_SPEC] + [SMEM_SPEC] * len(nodes) + [ANY_SPEC] * len(after),
        out_specs=(VMEM_SPEC,) * 2,
        scratch_shapes=[
            pltpu.VMEM((rp * 128 + 8, 128), jnp.float32),
            pltpu.VMEM((depth * 128, 128), jnp.float32),
        ],
        compiler_params=pltpu.CompilerParams(vmem_limit_bytes=52 * 1024 * 1024),
        name="scatter",
    )(counts, data, *nodes, *after)


def gather_kernel(counts, node_ref, sums_ref, one_ref, two_ref, *refs, depth, rp, lists):
    rows = refs[:lists]
    out_ref, table, found, comb = refs[lists:]
    comb[...] = jnp.zeros((128, 128), jnp.float32)

    @pl.loop(0, rp // 32)
    def _(g):
        for c in range(3):
            at = pl.ds(pl.multiple_of(c * rp + g * 32, 32), 32)
            comb[pl.ds(c, 32, stride=4), :] = one_ref[at, :] + two_ref[at, :]
        for i in range(16):
            pair = [sums_ref[pl.ds(pl.multiple_of((g * 32 + 2 * i + h) * 8, 8), 8), :] for h in range(2)]
            both = pair[0] + pltpu.roll(pair[1], 4, 0)
            comb[8 * i : 8 * i + 8, :] = comb[8 * i : 8 * i + 8, :] + both
        table[pl.ds(pl.multiple_of(g * 128, 128), 128), :] = jnp.transpose(comb[...])

    together = 4 if depth % 4 == 0 else 1

    @pl.loop(0, out_ref.shape[0])
    def _(t):
        def move(at, row):
            found[pl.ds(at, 1), :] = table[pl.ds(row, 1), :]

        def turn(i, carry):
            for j in range(together):
                r = i * together + j
                turned = jnp.transpose(found[pl.ds(pl.multiple_of(r * 128, 128), 128), :])
                place = jnp.broadcast_to(node_ref[t, pl.ds(r, 1), :], (8, 128)) >> 7
                half = (place >> 1) & 15
                value = turned[:8]
                for h in range(1, 16):
                    value = jnp.where(half == h, turned[8 * h : 8 * h + 8], value)
                value = jnp.where((place & 1) == 1, pltpu.roll(value, 4, 0), value)
                out_ref[t, pl.ds(r, 3, stride=depth), :] = value[:3]
            return carry

        count = counts[t]
        part = together * 128
        move_rows(rows, count, t, depth, move)
        lax.fori_loop(0, lax.div(count + (part - 1), jnp.int32(part)), turn, 0)


def gather_call(rows, counts, nodes, sums, one, two):
    rp = one.shape[0] // 3
    peers, depth, _ = nodes.shape
    return pl.pallas_call(
        functools.partial(gather_kernel, depth=depth, rp=rp, lists=len(rows)),
        out_shape=jax.ShapeDtypeStruct((peers, 3 * depth, 128), jnp.float32),
        in_specs=[SMEM_SPEC] + [VMEM_SPEC] * 4 + [SMEM_SPEC] * len(rows),
        out_specs=VMEM_SPEC,
        scratch_shapes=[
            pltpu.VMEM((rp * 4 + 8, 128), jnp.float32),
            pltpu.VMEM((depth * 128, 128), jnp.float32),
            pltpu.VMEM((128, 128), jnp.float32),
        ],
        compiler_params=pltpu.CompilerParams(vmem_limit_bytes=32 * 1024 * 1024),
        name="gather",
    )(counts, nodes, sums, one, two, *rows)


def finish_kernel(starts, in_ref, pos_ref, noise_ref, moved_ref, drift_ref, table, *, rows, depth, stride):
    lane = lane_index(depth)
    first = lane_index(1)

    @pl.loop(0, in_ref.shape[0])
    def _(t):
        at = starts[t]
        row = lax.shift_right_logical(at, 7)
        lead = at & 127
        for c in range(3):
            value = pltpu.roll(in_ref[t, c * depth : (c + 1) * depth, :], lead, 1)
            here = pl.ds(c * stride + row, depth)
            behind = pl.ds(c * stride + row + 1, depth)
            edge = table[pl.ds(c * stride + row, 1), :]
            table[behind, :] = value
            if depth > 1:
                body = jnp.where(lane[1:] < lead, value[:-1], value[1:])
                table[pl.ds(c * stride + row + 1, depth - 1), :] = body
            table[pl.ds(c * stride + row, 1), :] = jnp.where(first < lead, edge, value[:1])

    step = 8

    @pl.loop(0, rows // step)
    def _(i):
        at = pl.multiple_of(i * step, step)
        for c in range(3):
            drift = time_step * table[pl.ds(c * stride + at, step), :]
            drift_ref[c, pl.ds(at, step), :] = drift
            moved_ref[c, pl.ds(at, step), :] = pos_ref[c, pl.ds(at, step), :] + drift + noise_ref[c, pl.ds(at, step), :]


def finish_call(starts, data, pos, noise):
    rows = pos.shape[1]
    depth = data.shape[1] // 3
    stride = rows + depth + 8
    stride += -stride % 8
    return pl.pallas_call(
        functools.partial(finish_kernel, rows=rows, depth=depth, stride=stride),
        out_shape=(jax.ShapeDtypeStruct(pos.shape, jnp.float32),) * 2,
        in_specs=[SMEM_SPEC] + [VMEM_SPEC] * 3,
        out_specs=(VMEM_SPEC,) * 2,
        scratch_shapes=[pltpu.VMEM((3 * stride, 128), jnp.float32)],
        name="finish",
    )(starts, data, pos, noise)


ERFCX_COEF = (0.06548172872398669,
    -0.3609186250151195,
    0.6338942267842493,
    -0.3384301108125971,
    0.4003704641202259,
    0.13581047899030682,
    0.2395463173952274,
    0.22417089752024144,
    7.010614160106155e-05)


def pair_math(square, coef):
    inverse = lax.rsqrt(square)
    ratio = pl.reciprocal(1.0 + 0.2 * (square * inverse))
    scaled = coef[0] * ratio + coef[1]
    for k in coef[2:]:
        scaled = scaled * ratio + k
    decay = jnp.exp(-0.25 * square)
    inverse_sq = inverse * inverse
    screen = scaled * inverse
    along = decay * (screen * (0.375 + 0.0625 * inverse_sq) + 0.125)
    across = (decay * inverse_sq) * (screen * (0.375 - 0.1875 * inverse_sq) - 0.125)
    return along, across

def order_kernel(first, second, count, own_ref, far_ref, totals, *, blocks):
    def step(p, sizes):
        own, far = sizes
        other = second[p]
        within = other < blocks
        both = first[p] * 65536 + other
        own_ref[own] = both
        far_ref[far] = both - blocks
        inside = within.astype(jnp.int32)
        return own + inside, far + 1 - inside

    own, far = lax.fori_loop(0, count[0], step, (jnp.int32(0), jnp.int32(0)))
    totals[0] = own
    totals[1] = far


def order_call(first, second, count, blocks):
    size = first.shape[0] + 8
    return pl.pallas_call(
        functools.partial(order_kernel, blocks=blocks),
        out_shape=(jax.ShapeDtypeStruct((size,), jnp.int32),) * 2 + (jax.ShapeDtypeStruct((2,), jnp.int32),),
        in_specs=[SMEM_SPEC] * 3,
        out_specs=(SMEM_SPEC,) * 3,
        name="order",
    )(first, second, count)


def fill_cells(src_ref, cells, rp):
    @pl.loop(0, rp // 8)
    def _(i):
        at = pl.multiple_of(i * 8, 8)
        for c in range(6):
            cells[pl.ds(at * 8 + c, 8, stride=8), :] = src_ref[pl.ds(pl.multiple_of(c * rp + at, 8), 8), :]


def pair_kernel(pairs, bounds, cells_ref, near_in, *refs, rp, coef, unroll, beyond):
    if beyond:
        other_ref, far_in, near_ref, far_ref, other_cells, far_sums = refs
        fill_cells(other_ref, other_cells, rp)
        for c in range(3):
            @pl.loop(0, rp // 8)
            def _(i):
                at = pl.ds(pl.multiple_of(c * rp + i * 8, 8), 8)
                far_sums[pl.ds(i * 64 + c, 8, stride=8), :] = far_in[at, :]
    else:
        (near_ref,) = refs
        other_cells, far_sums = cells_ref, near_ref
    lane = lax.broadcasted_iota(jnp.int32, (8, 128), 1)
    sub = lax.broadcasted_iota(jnp.int32, (8, 128), 0)
    left = lane < 64
    unturn = (lane + sub) & 127
    near_ref[...] = near_in[...]

    def row(k):
        return pl.ds(pl.multiple_of((k >> 1) * 8, 8), 8)

    def both_halves(table, k):
        cell = table[row(k), :]
        return jnp.where(left == ((k & 1) == 0), cell, pltpu.roll(cell, 64, 1))

    def stacked(parts):
        out = jnp.zeros((8, 128), jnp.float32)
        for c, part in enumerate(parts):
            out = jnp.where(sub == c, jnp.sum(part, axis=0, keepdims=True), out)
        return out

    def one(ka, kb):
        near = both_halves(cells_ref, ka)
        near = jnp.where(left, near, pltpu.roll(near, 96, 1))
        far = both_halves(other_cells, kb)
        mine = [jnp.broadcast_to(near[c : c + 1, :], (8, 128)) for c in range(6)]
        other = [jnp.broadcast_to(far[c : c + 1, :], (8, 128)) for c in range(6)]
        near_sum = None
        far_sum = None
        for q in (3, 2, 1, 0):
            turned = [pltpu.roll(x, 8 * q, 1, stride=1, stride_axis=0) for x in other]
            gap = [mine[c] - turned[c] for c in range(3)]
            along, across = pair_math(gap[0] * gap[0] + gap[1] * gap[1] + gap[2] * gap[2] + 0.25, coef)
            to_near = across * (gap[0] * turned[3] + gap[1] * turned[4] + gap[2] * turned[5])
            to_far = across * (gap[0] * mine[3] + gap[1] * mine[4] + gap[2] * mine[5])
            near_add = [along * turned[3 + c] + to_near * gap[c] for c in range(3)]
            far_add = [along * mine[3 + c] + to_far * gap[c] for c in range(3)]
            if near_sum is None:
                near_sum, far_sum = near_add, far_add
            else:
                near_sum = [a + b for a, b in zip(near_sum, near_add)]
                far_sum = [pltpu.roll(a, 120, 1) + b for a, b in zip(far_sum, far_add)]
        far_sum = [jnp.take_along_axis(a, unturn, axis=1) for a in far_sum]
        near_vel = stacked(near_sum)
        half = jnp.where(left, pltpu.roll(near_vel, 64, 1), 0.0)
        near_vel = jnp.where(left, near_vel, 0.0) + pltpu.roll(half, 32, 1)
        near_vel = near_vel + pltpu.roll(near_vel, 64, 1)
        far_vel = stacked(far_sum)
        far_vel = far_vel + pltpu.roll(far_vel, 64, 1)
        return near_vel, far_vel

    low = bounds[0]
    high = bounds[1]

    def turn(i, carry):
        found = []
        for k in range(unroll):
            p = low + i * unroll + k
            alive = p < high
            both = jnp.where(alive, pairs[p], 0)
            ka, kb = both >> 16, both & 65535
            found.append((alive, ka, kb, one(ka, kb)))
        for alive, ka, kb, (near_vel, far_vel) in found:
            near_ref[row(ka), :] += jnp.where((left == ((ka & 1) == 0)) & alive, near_vel, 0.0)
            if not beyond:
                alive = alive & (ka != kb)
            far_sums[row(kb), :] += jnp.where((left == ((kb & 1) == 0)) & alive, far_vel, 0.0)
        return carry

    lax.fori_loop(0, lax.div(jnp.maximum(high - low, 0) + (unroll - 1), jnp.int32(unroll)), turn, 0)

    if beyond:
        for c in range(3):
            @pl.loop(0, rp // 8)
            def _(i):
                at = pl.ds(pl.multiple_of(c * rp + i * 8, 8), 8)
                far_ref[at, :] = far_sums[pl.ds(i * 64 + c, 8, stride=8), :]


def pair_call(pairs, bounds, cells, near, beside=None, far=None, after=(), coef=ERFCX_COEF, unroll=8):
    rp = cells.shape[0] // 8
    beyond = beside is not None
    extra = [beside, far] if beyond else []
    out = [jax.ShapeDtypeStruct((8 * rp, 128), jnp.float32)]
    scratch = []
    if beyond:
        out.append(jax.ShapeDtypeStruct((3 * rp, 128), jnp.float32))
        scratch = [pltpu.VMEM((8 * rp, 128), jnp.float32)] * 2
    return pl.pallas_call(
        ignoring(
            functools.partial(pair_kernel, rp=rp, coef=coef, unroll=unroll, beyond=beyond),
            4 + len(extra),
            len(after),
        ),
        out_shape=tuple(out),
        in_specs=[SMEM_SPEC] * 2 + [VMEM_SPEC] * (2 + len(extra)) + [ANY_SPEC] * len(after),
        out_specs=(VMEM_SPEC,) * len(out),
        scratch_shapes=scratch,
        compiler_params=pltpu.CompilerParams(vmem_limit_bytes=32 * 1024 * 1024),
        name="beyond" if beyond else "within",
    )(pairs, bounds, cells, near, *extra, *after)


def signed_wave(grid_index):
    return jnp.where(grid_index < G // 2, grid_index, grid_index - G).astype(jnp.float32) * (
        2.0 * math.pi / (G * grid_spacing)
    )


def forward_pass(real_in, imag_in, form, cos_part, sin_part):
    contract = partial(jnp.einsum, precision=lax.Precision.HIGHEST)
    real_out = contract(form, real_in, cos_part) + contract(form, imag_in, sin_part)
    imag_out = contract(form, imag_in, cos_part) - contract(form, real_in, sin_part)
    return (real_out, imag_out)


def inverse_pass(real_in, imag_in, form, cos_part, sin_part):
    contract = partial(jnp.einsum, precision=lax.Precision.HIGHEST)
    real_out = contract(form, real_in, cos_part) - contract(form, imag_in, sin_part)
    imag_out = contract(form, imag_in, cos_part) + contract(form, real_in, sin_part)
    return (real_out, imag_out)


def project_flow(spectrum, wave_x, wave_y, wave_z):
    wave_sq = wave_x * wave_x + wave_y * wave_y + wave_z * wave_z
    wave_safe = jnp.where(wave_sq > 0, wave_sq, 1.0)
    spread_sq = wave_sq / (4.0 * split_xi**2)
    green_fn = jnp.where(
        wave_sq > 0,
        (1.0 - bead_radius**2 * wave_sq / 3.0)
        * (1.0 + spread_sq)
        * jnp.exp(-spread_sq)
        / wave_safe,
        0.0,
    )
    along_wave = (wave_x * spectrum[0] + wave_y * spectrum[1] + wave_z * spectrum[2]) / wave_safe
    return jnp.stack(
        [
            green_fn * (spectrum[0] - wave_x * along_wave),
            green_fn * (spectrum[1] - wave_y * along_wave),
            green_fn * (spectrum[2] - wave_z * along_wave),
        ]
    )


def kspace_part(force_rows, n_gx, n_gy):
    local_x = G // n_gx
    local_y = G // n_gy
    grid_index = jnp.arange(G, dtype=jnp.int32)
    phase_grid = (grid_index[:, None] * grid_index[None, :] % G).astype(jnp.float32) * (
        2.0 * math.pi / G
    )
    cosine_table = jnp.cos(phase_grid)
    sine_table = jnp.sin(phase_grid)
    contract = partial(jnp.einsum, precision=lax.Precision.HIGHEST)
    force_field = force_rows.reshape(3, local_x, local_y, G)
    wave_full = signed_wave(grid_index)
    row_gx = lax.axis_index("gx")
    row_gy = lax.axis_index("gy")
    freq_count = G
    spec_z = jnp.stack(
        [
            contract("cabz,zk->cabk", force_field, cosine_table),
            -contract("cabz,zk->cabk", force_field, sine_table),
        ]
    )
    cos_x = cosine_table.reshape(n_gx, local_x, G)
    sin_x = sine_table.reshape(n_gx, local_x, G)
    cos_y = cosine_table.reshape(n_gy, local_y, G)
    sin_y = sine_table.reshape(n_gy, local_y, G)
    depth_part = freq_count // n_gx
    width_part = G // n_gy
    slabs = lax.all_to_all(spec_z[:, :, None], "gx", split_axis=5, concat_axis=2, tiled=True)
    xr_part, xi_part = forward_pass(slabs[0], slabs[1], "ciabl,iak->cbkl", cos_x, sin_x)
    pencils = lax.all_to_all(
        jnp.stack([xr_part, xi_part])[:, :, None], "gy", split_axis=4, concat_axis=2, tiled=True
    )
    yr_part, yi_part = forward_pass(pencils[0], pencils[1], "cjbkl,jbm->ckml", cos_y, sin_y)
    wave_x = signed_wave(row_gy * width_part + jnp.arange(width_part, dtype=jnp.int32))[
        :, None, None
    ]
    wave_y = wave_full[None, :, None]
    wave_z = signed_wave(row_gx * depth_part + jnp.arange(depth_part, dtype=jnp.int32))[
        None, None, :
    ]
    flow_real = project_flow(yr_part, wave_x, wave_y, wave_z)
    flow_imag = project_flow(yi_part, wave_x, wave_y, wave_z)
    br_part, bi_part = inverse_pass(flow_real, flow_imag, "ckml,jbm->cjbkl", cos_y, sin_y)
    back = lax.all_to_all(
        jnp.stack([br_part, bi_part]), "gy", split_axis=2, concat_axis=4, tiled=True
    )[:, :, 0]
    ar_part, ai_part = inverse_pass(back[0], back[1], "cbkl,iak->ciabl", cos_x, sin_x)
    gathered = lax.all_to_all(
        jnp.stack([ar_part, ai_part]), "gx", split_axis=2, concat_axis=5, tiled=True
    )[:, :, 0]
    result = contract("cabk,zk->cabz", gathered[0], cosine_table) - contract(
        "cabk,zk->cabz", gathered[1], sine_table
    )
    return (result / float(G**3)).reshape(3, local_x * local_y * G)


matmul = functools.partial(lax.dot_general, precision=lax.Precision.HIGHEST, preferred_element_type=jnp.float32)
PLAIN = (((1,), (0,)), ((), ()))
TURNED = (((1,), (1,)), ((), ()))


def wave_tables(n_gx, n_gy):
    share = G // 2 // n_gx
    width = G // n_gy
    grid = np.arange(G)
    turn = 2.0 * math.pi * (np.outer(grid, grid) % G) / G
    cos, sin = np.cos(turn), np.sin(turn)
    half = width // 2
    order = np.zeros(G, np.int64)
    for j in range(n_gy):
        for p in range(half):
            k = j * half + p
            order[j * width + p] = k
            order[j * width + half + p] = (G - k) % G if k else G // 2
    ahead = np.zeros((G, n_gx, 2, share))
    ahead[:, :, 0] = cos[:, : G // 2].reshape(G, n_gx, share)
    ahead[:, :, 1] = -sin[:, : G // 2].reshape(G, n_gx, share)
    back = 2.0 * ahead
    ahead[:, 0, 1, 0] = cos[:, G // 2]
    back[:, 0, 0, 0] = 1.0
    back[:, 0, 1, 0] = cos[:, G // 2]
    unit = 2.0 * math.pi / (G * grid_spacing)
    signed = np.where(grid < G // 2, grid, grid - G) * unit
    plain = np.where(grid == G // 2, 0.0, signed)
    edge = signed - plain
    lane = np.arange(128)
    across = np.zeros((n_gy, 8, 128))
    across[:, 0] = plain[order].reshape(n_gy, 1, width)[:, 0][:, lane % width]
    across[:, 1] = edge[order].reshape(n_gy, 1, width)[:, 0][:, lane % width]
    across[0, 2] = lane % half == 0
    deep = np.zeros((n_gx, 8, 128))
    per = 128 // width
    for v in range(share // per):
        deep[:, v] = (np.arange(n_gx)[:, None] * share + v * per + lane // width) * unit
    down = np.stack([np.broadcast_to(t[:, None], (G, 128)) for t in (plain, edge)])
    tables = {
        "ahead": ahead.reshape(G, G),
        "back": back.reshape(G, G).T,
        "first": np.concatenate([cos[:, order], sin[:, order]], axis=1),
        "first_back": np.concatenate([cos[:, order], sin[:, order]], axis=1),
        "second": np.concatenate([cos, sin], axis=0),
        "across": across,
        "deep": deep,
        "down": down,
    }
    return {name: np.asarray(table, np.float32) for name, table in tables.items()}


def spread(tiles, at, group, tall):
    count = 128 // group
    lane = lax.shift_right_logical(lax.broadcasted_iota(jnp.int32, (tall, 128), 1), group.bit_length() - 1)
    out = None
    for g, tile in enumerate(tiles):
        moved = pltpu.roll(tile, group * ((g - at) % count), 1) if g != at else tile
        out = moved if out is None else jnp.where(lane == g, moved, out)
    return out


def depth_kernel(field_ref, table_ref, out_ref, spec, *, n_gx, tall, wide):
    rows = tall * wide
    for c in range(3):
        spec[c * rows : (c + 1) * rows, :] = matmul(field_ref[c * rows : (c + 1) * rows, :], table_ref[...], PLAIN)
    group = G // n_gx
    count = n_gx

    @pl.loop(0, 3 * wide // count)
    def _(i):
        c = lax.div(i, jnp.int32(wide // count))
        b = (i - c * (wide // count)) * count
        tiles = [spec[pl.ds(c * rows + b + g, tall, stride=wide), :] for g in range(count)]
        for p in range(n_gx):
            out_ref[p, :, pl.ds(pl.multiple_of(i * 128, 128), 128)] = spread(tiles, p, group, tall)


def first_kernel(data_ref, table_ref, out_ref, turned, *, n_gy, share, wide):
    group = G // n_gy
    per = 128 // (2 * share)

    @pl.loop(0, 3 * wide // per)
    def _(i):
        c = lax.div(i, jnp.int32(wide // per))
        b = (i - c * (wide // per)) * per
        piece = jnp.transpose(data_ref[:, pl.ds(pl.multiple_of(i * 128, 128), 128)])
        both = matmul(piece, table_ref[...], PLAIN)
        for g in range(per):
            lo, mid, hi = g * 2 * share, (g * 2 + 1) * share, (g * 2 + 2) * share
            real = both[lo:mid, :128] + both[mid:hi, 128:]
            imag = both[mid:hi, :128] - both[lo:mid, 128:]
            turned[pl.ds(2 * c * share * wide + b + g, share, stride=wide), :] = real
            turned[pl.ds((2 * c + 1) * share * wide + b + g, share, stride=wide), :] = imag

    count = 128 // group

    @pl.loop(0, 6 * share // count)
    def _(i):
        at = i * (count * wide)
        tiles = [turned[pl.ds(pl.multiple_of(at + u * wide, 8), wide), :] for u in range(count)]
        for j in range(n_gy):
            out_ref[j, i] = spread(tiles, j, group, wide)


def second_kernel(ids, data_ref, table_ref, across_ref, deep_ref, down_ref, out_ref, flow, *, n_gy, views, wide):
    lane = lax.broadcasted_iota(jnp.int32, (G, 128), 1)
    width = G // n_gy
    half = width // 2
    across = across_ref[ids[1]]
    deep = deep_ref[ids[0]]
    alone = (lane < width) & (ids[0] == 0)
    mirror_self = across[2:3, :] > 0.5
    upper = (lane & half) != 0

    def whole(tile):
        return jnp.concatenate([data_ref[j, tile] for j in range(n_gy)], axis=0)

    def mirrored(value):
        other = jnp.where(upper, pltpu.roll(value, half, 1), pltpu.roll(value, 128 - half, 1))
        return jnp.where(mirror_self, value, other)

    def ahead(real, imag):
        one = matmul(table_ref[...], real, PLAIN)
        two = matmul(table_ref[...], imag, PLAIN)
        return one[:G] + two[G:], two[:G] - one[G:]

    def projected(spectrum, deep_plain, deep_edge):
        plain = (across[0:1, :], down_ref[0], deep_plain)
        edge = (across[1:2, :], down_ref[1], deep_edge)
        waves = [p + e for p, e in zip(plain, edge)]
        wave_sq = waves[0] * waves[0] + waves[1] * waves[1] + waves[2] * waves[2]
        live = wave_sq > 0
        inverse = 1.0 / jnp.where(live, wave_sq, 1.0)
        spread_sq = wave_sq / (4.0 * split_xi**2)
        green = (1.0 - bead_radius**2 * wave_sq / 3.0) * (1.0 + spread_sq) * jnp.exp(-spread_sq) * inverse
        green = jnp.where(live, green / float(G**3), 0.0)
        out = []
        for r in range(2):
            regular = sum(w * spectrum[c][r] for c, w in enumerate(plain)) * inverse
            nyquist = sum(w * spectrum[c][r] for c, w in enumerate(edge)) * inverse
            out.append([green * (spectrum[c][r] - plain[c] * regular - edge[c] * nyquist) for c in range(3)])
        return out

    zero = jnp.zeros((1, 128), jnp.float32)
    for v in range(views):
        spectrum = []
        apart = []
        for c in range(3):
            real = whole((2 * c) * views + v)
            imag = whole((2 * c + 1) * views + v)
            if v == 0:
                off_real = jnp.where(alone, 0.5 * (real - mirrored(real)), 0.0)
                off_imag = jnp.where(alone, 0.5 * (imag + mirrored(imag)), 0.0)
                apart.append(ahead(off_real, off_imag))
                real, imag = real - off_real, imag - off_imag
            spectrum.append(ahead(real, imag))
        found = projected(spectrum, deep[v : v + 1, :], zero)
        if v == 0:
            extra = projected(apart, zero, zero - math.pi / grid_spacing)
            found = [[a + b for a, b in zip(one, two)] for one, two in zip(found, extra)]
        for c in range(3):
            one = matmul(table_ref[...], found[0][c], PLAIN)
            two = matmul(table_ref[...], found[1][c], PLAIN)
            real, imag = one[:G] - two[G:], two[:G] + one[G:]
            for j in range(n_gy):
                out_ref[j, (2 * c) * views + v] = real[j * wide : (j + 1) * wide]
                out_ref[j, (2 * c + 1) * views + v] = imag[j * wide : (j + 1) * wide]


def first_back_kernel(data_ref, table_ref, out_ref, turned, *, n_gy, share, wide):
    group = G // n_gy
    count = n_gy
    per = 128 // (2 * share)

    @pl.loop(0, 6 * share // count)
    def _(i):
        tiles = [data_ref[j, i] for j in range(n_gy)]
        for u in range(count):
            turned[pl.ds(pl.multiple_of((i * count + u) * wide, 8), wide), :] = spread(tiles, u, group, wide)

    @pl.loop(0, 3 * wide // per)
    def _(i):
        c = lax.div(i, jnp.int32(wide // per))
        b = (i - c * (wide // per)) * per
        rows = []
        for g in range(per):
            real = turned[pl.ds(2 * c * share * wide + b + g, share, stride=wide), :]
            imag = turned[pl.ds((2 * c + 1) * share * wide + b + g, share, stride=wide), :]
            rows.append(jnp.concatenate([real, -imag], axis=1))
            rows.append(jnp.concatenate([imag, real], axis=1))
        piece = jnp.concatenate(rows, axis=0)
        out_ref[:, pl.ds(pl.multiple_of(i * 128, 128), 128)] = matmul(table_ref[...], piece, TURNED)


def depth_back_kernel(data_ref, table_ref, out_ref, spec, *, n_gx, tall, wide):
    rows = tall * wide
    group = G // n_gx
    count = n_gx

    @pl.loop(0, 3 * wide // count)
    def _(i):
        c = lax.div(i, jnp.int32(wide // count))
        b = (i - c * (wide // count)) * count
        tiles = [data_ref[p, :, pl.ds(pl.multiple_of(i * 128, 128), 128)] for p in range(n_gx)]
        for g in range(count):
            spec[pl.ds(c * rows + b + g, tall, stride=wide), :] = spread(tiles, g, group, tall)

    for c in range(3):
        out_ref[c * rows : (c + 1) * rows, :] = matmul(spec[c * rows : (c + 1) * rows, :], table_ref[...], PLAIN)


def waves(grid_data, n_gx, n_gy, fill):
    tall, wide, share = G // n_gx, G // n_gy, G // 2 // n_gx
    rows = 3 * tall * wide
    views = share * wide // 128
    tables = wave_tables(n_gx, n_gy)
    f32 = jnp.float32

    def run(name, kernel, shape, args, scratch, specs=None, after=(), **sizes):
        return pl.pallas_call(
            ignoring(functools.partial(kernel, **sizes), len(args), len(after)),
            out_shape=jax.ShapeDtypeStruct(shape, f32),
            in_specs=(specs or [VMEM_SPEC] * len(args)) + [ANY_SPEC] * len(after),
            out_specs=VMEM_SPEC,
            scratch_shapes=[pltpu.VMEM(scratch, f32)],
            compiler_params=pltpu.CompilerParams(vmem_limit_bytes=24 * 1024 * 1024),
            name=name,
            grid=(1,),
        )(*args, *after)

    def swap(value, axis):
        return lax.all_to_all(value, axis, split_axis=0, concat_axis=0, tiled=True)

    def full(shape):
        return pl.BlockSpec(shape, lambda i: (0,) * len(shape))

    force = pl.BlockSpec((rows, 128), lambda i: (1, 0))
    lanes = 6 * wide * share
    ids = jnp.stack([lax.axis_index("gx"), lax.axis_index("gy")]).astype(jnp.int32)
    value = run("depth", depth_kernel, (n_gx, tall, lanes), (grid_data, tables["ahead"]), (rows, 128),
                [force, full((G, 128))], n_gx=n_gx, tall=tall, wide=wide)
    after = fill(0, value)
    value = swap(value, "gx").reshape(G, lanes)
    value = run("first", first_kernel, (n_gy, 6 * views, wide, 128), (value, tables["first"]), (rows, 128),
                after=after, n_gy=n_gy, share=share, wide=wide)
    after = fill(1, value)
    value = swap(value.reshape(n_gy, 6 * views * wide, 128), "gy").reshape(n_gy, 6 * views, wide, 128)
    args = (ids, value, tables["second"], tables["across"], tables["deep"], tables["down"])
    value = run("second", second_kernel, (n_gy, 6 * views, wide, 128), args, (8, 128),
                [SMEM_SPEC] + [VMEM_SPEC] * 5, after, n_gy=n_gy, views=views, wide=wide)
    after = fill(2, value)
    value = swap(value.reshape(n_gy, 6 * views * wide, 128), "gy").reshape(n_gy, 6 * views, wide, 128)
    value = run("first_back", first_back_kernel, (G, lanes), (value, tables["first_back"]), (rows, 128),
                after=after, n_gy=n_gy, share=share, wide=wide)
    after = fill(3, value)
    value = swap(value.reshape(n_gx, tall, lanes), "gx")
    return run("depth_back", depth_back_kernel, (rows, 128), (value, tables["back"]), (rows, 128),
               after=after, n_gx=n_gx, tall=tall, wide=wide)


def shards(positions, noise, route, node_perm, pair_first, pair_second, pair_count):
    n_gx = lax.axis_size("gx")
    n_gy = lax.axis_size("gy")
    both = ("gx", "gy")
    peers = n_gx * n_gy
    slots = node_perm.shape[2]
    depth = slots // peers // 128
    rows = positions.shape[1] // 128
    rp = slots // 128
    swap = partial(lax.all_to_all, axis_name=both, split_axis=0, concat_axis=0, tiled=True)

    bounds = jnp.arange(peers + 1, dtype=jnp.int32) * (slots // peers)
    starts = jnp.sum(route[None, :] < bounds[:, None], axis=1, dtype=jnp.int32)
    taken = swap(slots_call(starts, route.reshape(rows, 128), depth))
    places = positions.reshape(3, rows, 128)
    data = swap(pack_call(starts, places, depth))
    counts = jnp.sum(taken >= 0, axis=(1, 2), dtype=jnp.int32)
    own_order = lax.dynamic_index_in_dim(node_perm, lax.axis_index("gx"), 0, False)
    nodes, node_lists, row_lists = nodes_call(taken, own_order.reshape(peers, depth, 128), slots)
    own_pairs, far_pairs, totals = order_call(pair_first[0], pair_second[0], pair_count, slots // CELL)
    grid_data, cells = scatter_call(node_lists, counts, data, rp, after=(totals,))

    beside = shifted(grid_data, "gx", -1)
    steps = pair_first.shape[1]
    marks = [jnp.minimum(totals[0], steps // 4), jnp.minimum(totals[0], steps * 3 // 8)]
    half = totals[1] // 16 * 8
    begin = jnp.int32(0)
    state = {"sums": jnp.zeros_like(cells), "far": jnp.zeros((3 * rp, 128), jnp.float32)}

    def within(low, high, after):
        (state["sums"],) = pair_call(own_pairs, jnp.stack([low, high]), cells, state["sums"], after=after)

    def beyond(low, high, after):
        state["sums"], state["far"] = pair_call(
            far_pairs, jnp.stack([low, high]), cells, state["sums"], beside, state["far"], after=after
        )

    def fill(n, value):
        if n == 0:
            within(begin, marks[0], (value,))
        elif n == 1:
            within(marks[0], marks[1], (value,))
        elif n == 2:
            beyond(begin, half, (value,))
        else:
            beyond(half, totals[1], (value,))
            state["far"] = shifted(state["far"], "gx", 1)
            within(marks[1], totals[0], ())
        return (state["sums"],)

    share = G // 2 // n_gx
    if share % 8 == 0 and share * (G // n_gy) % 128 == 0:
        wave_vel = waves(grid_data, n_gx, n_gy, fill)
    else:
        wave_vel = kspace_part(grid_data[3 * rp :], n_gx, n_gy).reshape(3 * rp, 128)
        for n in range(4):
            fill(n, wave_vel)
    back = swap(gather_call(row_lists, counts, nodes, state["sums"], wave_vel, state["far"]))
    moved, drift = finish_call(starts, back, places, noise.reshape(3, rows, 128))
    return (moved.reshape(positions.shape), drift.reshape(positions.shape))


def solution(mesh):
    in_specs = (
        P(None, ("gx", "gy")),
        P(None, ("gx", "gy")),
        P(("gx", "gy")),
        P(None, "gy", None),
        P(("gx", "gy"), None),
        P(("gx", "gy"), None),
        P(("gx", "gy")),
    )
    out_specs = (P(None, ("gx", "gy")), P(None, ("gx", "gy")))
    return jax.shard_map(shards, mesh=mesh, in_specs=in_specs, out_specs=out_specs, check_vma=False)
```

```python
import functools
from functools import partial
import math

import jax
import jax.numpy as jnp
import numpy as np
from jax import lax
from jax.experimental import pallas as pl
from jax.experimental.pallas import tpu as pltpu
from jax.sharding import PartitionSpec as P

G = 128
BEAD_CH = 64
CELL = 64


bead_radius = 0.5
split_xi = 0.5
time_step = 0.01
fene_k = 30.0
fene_reach = 1.5
bend_k = 2.0
grid_spacing = 4.0
pair_block = 64


def shifted(value, axis, by):
    devices = lax.axis_size(axis)
    return lax.ppermute(value, axis, [(i, (i + by) % devices) for i in range(devices)])


SPAN = 16
PARTS = (25, 37, 52)

SMEM_SPEC = pl.BlockSpec(memory_space=pltpu.SMEM)
VMEM_SPEC = pl.BlockSpec(memory_space=pltpu.VMEM)


ANY_SPEC = pl.BlockSpec(memory_space=pl.ANY)


def ignoring(kernel, inputs, extra):
    def run(*refs):
        kernel(*refs[:inputs], *refs[inputs + extra :])

    return run


def marking(kernel, inputs):
    def run(*refs):
        refs[inputs + 1][...] = jnp.zeros(refs[inputs + 1].shape, jnp.float32)
        kernel(*refs[: inputs + 1], *refs[inputs + 2 :])

    return run


def lane_index(rows):
    return lax.broadcasted_iota(jnp.int32, (rows, 128), 1)


def window(table, at, rows):
    row = lax.shift_right_logical(at, 7)
    lead = at & 127
    head = pltpu.roll(table[pl.ds(row, rows), :], (128 - lead) & 127, 1)
    tail = pltpu.roll(table[pl.ds(row + 1, rows), :], (128 - lead) & 127, 1)
    return jnp.where(lane_index(rows) < 128 - lead, head, tail)


def slots_kernel(starts, route_ref, out_ref, table, *, rows, depth):
    table[pl.ds(0, rows), :] = route_ref[...]
    table[pl.ds(rows, depth + 8), :] = jnp.zeros((depth + 8, 128), jnp.int32)
    place = lane_index(depth) + lax.broadcasted_iota(jnp.int32, (depth, 128), 0) * 128

    @pl.loop(0, out_ref.shape[0])
    def _(t):
        at = starts[t]
        slot = window(table, at, depth) - t * (depth * 128)
        out_ref[t] = jnp.where(place < starts[t + 1] - at, slot, -1)


def slots_call(starts, route, depth):
    rows = route.shape[0]
    peers = starts.shape[0] - 1
    return pl.pallas_call(
        functools.partial(slots_kernel, rows=rows, depth=depth),
        out_shape=jax.ShapeDtypeStruct((peers, depth, 128), jnp.int32),
        in_specs=[SMEM_SPEC, VMEM_SPEC],
        out_specs=VMEM_SPEC,
        scratch_shapes=[pltpu.VMEM((rows + depth + 8, 128), jnp.int32)],
        compiler_params=pltpu.CompilerParams(vmem_limit_bytes=8 * 1024 * 1024),
        name="slots",
    )(starts, route)


def chain_forces(pos):
    rows = pos[0].shape[0]
    place = lane_index(rows) & (BEAD_CH - 1)
    bonded = place < BEAD_CH - 1
    bent = place < BEAD_CH - 2
    after = (place > 0) & bonded
    bond = [jnp.where(bonded, pltpu.roll(x, 127, 1) - x, 0.5) for x in pos]
    square = bond[0] * bond[0] + bond[1] * bond[1] + bond[2] * bond[2]
    inverse = lax.rsqrt(square)
    unit = [b * inverse for b in bond]
    following = [pltpu.roll(u, 127, 1) for u in unit]
    previous = [pltpu.roll(u, 1, 1) for u in unit]
    cosine = sum(u * v for u, v in zip(unit, following))
    cosine_before = pltpu.roll(cosine, 1, 1)
    pull = fene_k / (1.0 - square / fene_reach**2)
    out = []
    for c in range(3):
        turn = jnp.where(bent, following[c] - cosine * unit[c], 0.0)
        turn = turn + jnp.where(after, previous[c] - cosine_before * unit[c], 0.0)
        slope = jnp.where(bonded, pull * bond[c] - bend_k * inverse * turn, 0.0)
        out.append(slope - pltpu.roll(slope, 1, 1))
    return out


def pack_kernel(starts, pos_ref, out_ref, table, *, rows, depth, stride):
    step = 32 if rows % 32 == 0 else 8

    @pl.loop(0, rows // step)
    def _(i):
        at = pl.multiple_of(i * step, step)
        pos = [pos_ref[c, pl.ds(at, step), :] for c in range(3)]
        for c, value in enumerate(pos + chain_forces(pos)):
            table[pl.ds(c * stride + at, step), :] = value

    for c in range(6):
        table[pl.ds(c * stride + rows, stride - rows), :] = jnp.zeros((stride - rows, 128), jnp.float32)

    @pl.loop(0, out_ref.shape[0])
    def _(t):
        at = starts[t]
        for c in range(6):
            out_ref[t, c * depth : (c + 1) * depth, :] = window(table, at + c * stride * 128, depth)


def pack_call(starts, pos, depth):
    rows = pos.shape[1]
    peers = starts.shape[0] - 1
    stride = rows + depth + 8
    stride += -stride % 8
    return pl.pallas_call(
        functools.partial(pack_kernel, rows=rows, depth=depth, stride=stride),
        out_shape=jax.ShapeDtypeStruct((peers, 6 * depth, 128), jnp.float32),
        in_specs=[SMEM_SPEC, VMEM_SPEC],
        out_specs=VMEM_SPEC,
        scratch_shapes=[pltpu.VMEM((6 * stride, 128), jnp.float32)],
        compiler_params=pltpu.CompilerParams(vmem_limit_bytes=8 * 1024 * 1024),
        name="pack",
    )(starts, pos)


def list_count(depth):
    return 8 if depth % 8 == 0 else 1


def nodes_kernel(slots_ref, perm_ref, node_ref, *list_refs, depth, spare):
    tile = list_count(depth)
    parts = depth // tile

    @pl.loop(0, slots_ref.shape[0])
    def _(t):
        rows = [jnp.broadcast_to(perm_ref[t, w : w + 1, :], (8, 128)) for w in range(depth)]
        for r in range(parts):
            slot = jnp.broadcast_to(slots_ref[t, r * tile : (r + 1) * tile, :], (8, 128))
            place = slot & 127
            which = slot >> 7
            node = jnp.full((8, 128), spare, jnp.int32)
            for w in range(depth):
                node = jnp.where(which == w, jnp.take_along_axis(rows[w], place, axis=1), node)
            packed = ((node >> 12) << 7) | (node & 127)
            node_ref[t, r * tile : (r + 1) * tile, :] = node[:tile]
            for u in range(tile):
                list_refs[u][pl.ds(t * parts + r, 1), :] = node[u : u + 1]
                list_refs[tile + u][pl.ds(t * parts + r, 1), :] = packed[u : u + 1]


def nodes_call(slots, perm, spare):
    peers, depth, _ = slots.shape
    lists = list_count(depth)
    one = jax.ShapeDtypeStruct((peers * depth // lists, 128), jnp.int32)
    found = pl.pallas_call(
        functools.partial(nodes_kernel, depth=depth, spare=spare),
        out_shape=(jax.ShapeDtypeStruct(slots.shape, jnp.int32),) + (one,) * (2 * lists),
        in_specs=[VMEM_SPEC] * 2,
        out_specs=(VMEM_SPEC,) * (1 + 2 * lists),
        compiler_params=pltpu.CompilerParams(vmem_limit_bytes=8 * 1024 * 1024),
        name="nodes",
    )(slots, perm)
    flat = [x.reshape(-1) for x in found[1:]]
    return found[0], flat[:lists], flat[lists:]


def move_rows(lists, count, t, depth, move):
    width = len(lists)
    parts = depth // width

    def part(p, carry):
        live = jnp.minimum(count - p * (width * 128), 128)
        base = (t * parts + p) * 128
        start = p * (width * 128)

        def some(i, carry):
            for k in range(SPAN):
                at = i * SPAN + k
                for u in range(width):
                    move(start + at + u * 128, lists[u][base + at])
            return carry

        return lax.fori_loop(0, lax.div(live + (SPAN - 1), jnp.int32(SPAN)), some, carry)

    whole = width * 128
    lax.fori_loop(0, lax.div(count + (whole - 1), jnp.int32(whole)), part, 0)


def scatter_kernel(counts, in_ref, *refs, depth, rp, lists):
    nodes = refs[:lists]
    out_ref, cells_ref, table, rows_ref = refs[lists:]

    @pl.loop(0, rp)
    def _(k):
        table[pl.ds(pl.multiple_of(k * 128, 128), 128), :] = jnp.zeros((128, 128), jnp.float32)

    together = 4 if depth % 4 == 0 else 1

    @pl.loop(0, in_ref.shape[0])
    def _(t):
        def turn(i, carry):
            for j in range(together):
                r = i * together + j
                piece = in_ref[t, pl.ds(r, 6, stride=depth), :]
                piece = jnp.concatenate([piece, jnp.zeros((2, 128), jnp.float32)], axis=0)
                piece = jnp.concatenate([piece] * 16, axis=0)
                rows_ref[pl.ds(pl.multiple_of(r * 128, 128), 128), :] = jnp.transpose(piece)
            return carry

        def move(at, node):
            table[pl.ds(node, 1), :] = rows_ref[pl.ds(at, 1), :]

        count = counts[t]
        part = together * 128
        lax.fori_loop(0, lax.div(count + (part - 1), jnp.int32(part)), turn, 0)
        move_rows(nodes, count, t, depth, move)

    group = lane_index(8) >> 3

    @pl.loop(0, rp // 16)
    def _(g):
        tiles = []
        for i in range(16):
            tile = table[pl.ds(pl.multiple_of(g * 2048, 2048) + 8 * i, 8), :]
            for k in range(1, 16):
                one = table[pl.ds(pl.multiple_of(g * 2048, 2048) + k * 128 + 8 * i, 8), :]
                tile = jnp.where(group == k, one, tile)
            tiles.append(tile)
        at = pl.multiple_of(g * 128, 128)
        cells_ref[pl.ds(at, 128), :] = jnp.transpose(jnp.concatenate(tiles, axis=0))
        for c in range(6):
            out_ref[pl.ds(pl.multiple_of(c * rp + g * 16, 16), 16), :] = cells_ref[pl.ds(at + c, 16, stride=8), :]


def scatter_call(nodes, counts, data, rp, after=()):
    depth = data.shape[1] // 6
    return pl.pallas_call(
        ignoring(
            functools.partial(scatter_kernel, depth=depth, rp=rp, lists=len(nodes)), 2 + len(nodes), len(after)
        ),
        out_shape=(
            jax.ShapeDtypeStruct((6 * rp, 128), jnp.float32),
            jax.ShapeDtypeStruct((8 * rp, 128), jnp.float32),
        ),
        in_specs=[SMEM_SPEC, VMEM_SPEC] + [SMEM_SPEC] * len(nodes) + [ANY_SPEC] * len(after),
        out_specs=(VMEM_SPEC,) * 2,
        scratch_shapes=[
            pltpu.VMEM((rp * 128 + 8, 128), jnp.float32),
            pltpu.VMEM((depth * 128, 128), jnp.float32),
        ],
        compiler_params=pltpu.CompilerParams(vmem_limit_bytes=40 * 1024 * 1024),
        name="scatter",
    )(counts, data, *nodes, *after)


def gather_kernel(counts, node_ref, sums_ref, one_ref, two_ref, *refs, depth, rp, lists):
    rows = refs[:lists]
    out_ref, table, found, comb = refs[lists:]
    comb[...] = jnp.zeros((128, 128), jnp.float32)

    @pl.loop(0, rp // 32)
    def _(g):
        for c in range(3):
            at = pl.ds(pl.multiple_of(c * rp + g * 32, 32), 32)
            comb[pl.ds(c, 32, stride=4), :] = one_ref[at, :] + two_ref[at, :]
        for i in range(16):
            pair = [sums_ref[pl.ds(pl.multiple_of((g * 32 + 2 * i + h) * 8, 8), 8), :] for h in range(2)]
            both = pair[0] + pltpu.roll(pair[1], 4, 0)
            comb[8 * i : 8 * i + 8, :] = comb[8 * i : 8 * i + 8, :] + both
        table[pl.ds(pl.multiple_of(g * 128, 128), 128), :] = jnp.transpose(comb[...])

    together = 4 if depth % 4 == 0 else 1

    @pl.loop(0, out_ref.shape[0])
    def _(t):
        def move(at, row):
            found[pl.ds(at, 1), :] = table[pl.ds(row, 1), :]

        def turn(i, carry):
            for j in range(together):
                r = i * together + j
                turned = jnp.transpose(found[pl.ds(pl.multiple_of(r * 128, 128), 128), :])
                place = jnp.broadcast_to(node_ref[t, pl.ds(r, 1), :], (8, 128)) >> 7
                half = (place >> 1) & 15
                value = turned[:8]
                for h in range(1, 16):
                    value = jnp.where(half == h, turned[8 * h : 8 * h + 8], value)
                value = jnp.where((place & 1) == 1, pltpu.roll(value, 4, 0), value)
                out_ref[t, pl.ds(r, 3, stride=depth), :] = value[:3]
            return carry

        count = counts[t]
        part = together * 128
        move_rows(rows, count, t, depth, move)
        lax.fori_loop(0, lax.div(count + (part - 1), jnp.int32(part)), turn, 0)


def gather_call(rows, counts, nodes, sums, one, two):
    rp = one.shape[0] // 3
    peers, depth, _ = nodes.shape
    return pl.pallas_call(
        functools.partial(gather_kernel, depth=depth, rp=rp, lists=len(rows)),
        out_shape=jax.ShapeDtypeStruct((peers, 3 * depth, 128), jnp.float32),
        in_specs=[SMEM_SPEC] + [VMEM_SPEC] * 4 + [SMEM_SPEC] * len(rows),
        out_specs=VMEM_SPEC,
        scratch_shapes=[
            pltpu.VMEM((rp * 4 + 8, 128), jnp.float32),
            pltpu.VMEM((depth * 128, 128), jnp.float32),
            pltpu.VMEM((128, 128), jnp.float32),
        ],
        compiler_params=pltpu.CompilerParams(vmem_limit_bytes=8 * 1024 * 1024),
        name="gather",
    )(counts, nodes, sums, one, two, *rows)


def finish_kernel(starts, in_ref, pos_ref, noise_ref, moved_ref, drift_ref, table, *, rows, depth, stride):
    lane = lane_index(depth)
    first = lane_index(1)

    @pl.loop(0, in_ref.shape[0])
    def _(t):
        at = starts[t]
        row = lax.shift_right_logical(at, 7)
        lead = at & 127
        for c in range(3):
            value = pltpu.roll(in_ref[t, c * depth : (c + 1) * depth, :], lead, 1)
            here = pl.ds(c * stride + row, depth)
            behind = pl.ds(c * stride + row + 1, depth)
            edge = table[pl.ds(c * stride + row, 1), :]
            table[behind, :] = value
            if depth > 1:
                body = jnp.where(lane[1:] < lead, value[:-1], value[1:])
                table[pl.ds(c * stride + row + 1, depth - 1), :] = body
            table[pl.ds(c * stride + row, 1), :] = jnp.where(first < lead, edge, value[:1])

    step = 8

    @pl.loop(0, rows // step)
    def _(i):
        at = pl.multiple_of(i * step, step)
        for c in range(3):
            drift = time_step * table[pl.ds(c * stride + at, step), :]
            drift_ref[c, pl.ds(at, step), :] = drift
            moved_ref[c, pl.ds(at, step), :] = pos_ref[c, pl.ds(at, step), :] + drift + noise_ref[c, pl.ds(at, step), :]


def finish_call(starts, data, pos, noise):
    rows = pos.shape[1]
    depth = data.shape[1] // 3
    stride = rows + depth + 8
    stride += -stride % 8
    return pl.pallas_call(
        functools.partial(finish_kernel, rows=rows, depth=depth, stride=stride),
        out_shape=(jax.ShapeDtypeStruct(pos.shape, jnp.float32),) * 2,
        in_specs=[SMEM_SPEC] + [VMEM_SPEC] * 3,
        out_specs=(VMEM_SPEC,) * 2,
        scratch_shapes=[pltpu.VMEM((3 * stride, 128), jnp.float32)],
        compiler_params=pltpu.CompilerParams(vmem_limit_bytes=8 * 1024 * 1024),
        name="finish",
    )(starts, data, pos, noise)


ERFCX_COEF = (0.06548172872398669,
    -0.3609186250151195,
    0.6338942267842493,
    -0.3384301108125971,
    0.4003704641202259,
    0.13581047899030682,
    0.2395463173952274,
    0.22417089752024144,
    7.010614160106155e-05)


def pair_math(square, coef):
    inverse = lax.rsqrt(square)
    ratio = pl.reciprocal(1.0 + 0.2 * (square * inverse))
    scaled = coef[0] * ratio + coef[1]
    for k in coef[2:]:
        scaled = scaled * ratio + k
    decay = jnp.exp(-0.25 * square)
    inverse_sq = inverse * inverse
    screen = scaled * inverse
    along = decay * (screen * (0.375 + 0.0625 * inverse_sq) + 0.125)
    across = (decay * inverse_sq) * (screen * (0.375 - 0.1875 * inverse_sq) - 0.125)
    return along, across

def order_kernel(first, second, count, own_ref, far_ref, totals, *, blocks):
    def step(p, sizes):
        own, far = sizes
        other = second[p]
        within = other < blocks
        both = first[p] * 65536 + other
        own_ref[own] = both
        far_ref[far] = both - blocks
        inside = within.astype(jnp.int32)
        return own + inside, far + 1 - inside

    own, far = lax.fori_loop(0, count[0], step, (jnp.int32(0), jnp.int32(0)))
    totals[0] = own
    totals[1] = far


def order_call(first, second, count, blocks):
    size = first.shape[0] + 8
    return pl.pallas_call(
        functools.partial(order_kernel, blocks=blocks),
        out_shape=(jax.ShapeDtypeStruct((size,), jnp.int32),) * 2 + (jax.ShapeDtypeStruct((2,), jnp.int32),),
        in_specs=[SMEM_SPEC] * 3,
        out_specs=(SMEM_SPEC,) * 3,
        compiler_params=pltpu.CompilerParams(vmem_limit_bytes=8 * 1024 * 1024),
        name="order",
    )(first, second, count)


def fill_cells(src_ref, cells, rp):
    @pl.loop(0, rp // 8)
    def _(i):
        at = pl.multiple_of(i * 8, 8)
        for c in range(6):
            cells[pl.ds(at * 8 + c, 8, stride=8), :] = src_ref[pl.ds(pl.multiple_of(c * rp + at, 8), 8), :]


def pair_kernel(pairs, bounds, cells_ref, near_in, *refs, rp, coef, unroll, beyond):
    if beyond:
        other_ref, far_in, near_ref, token, far_ref, other_cells, far_sums = refs
        fill_cells(other_ref, other_cells, rp)
        for c in range(3):
            @pl.loop(0, rp // 8)
            def _(i):
                at = pl.ds(pl.multiple_of(c * rp + i * 8, 8), 8)
                far_sums[pl.ds(i * 64 + c, 8, stride=8), :] = far_in[at, :]
    else:
        near_ref, token = refs
        other_cells, far_sums = cells_ref, near_ref
    lane = lax.broadcasted_iota(jnp.int32, (8, 128), 1)
    sub = lax.broadcasted_iota(jnp.int32, (8, 128), 0)
    left = lane < 64
    unturn = (lane + sub) & 127
    near_ref[...] = near_in[...]
    token[...] = jnp.zeros((8, 128), jnp.float32)

    def row(k):
        return pl.ds(pl.multiple_of((k >> 1) * 8, 8), 8)

    def both_halves(table, k):
        cell = table[row(k), :]
        return jnp.where(left == ((k & 1) == 0), cell, pltpu.roll(cell, 64, 1))

    def stacked(parts):
        out = jnp.zeros((8, 128), jnp.float32)
        for c, part in enumerate(parts):
            out = jnp.where(sub == c, jnp.sum(part, axis=0, keepdims=True), out)
        return out

    def one(ka, kb):
        near = both_halves(cells_ref, ka)
        near = jnp.where(left, near, pltpu.roll(near, 96, 1))
        far = both_halves(other_cells, kb)
        mine = [jnp.broadcast_to(near[c : c + 1, :], (8, 128)) for c in range(6)]
        other = [jnp.broadcast_to(far[c : c + 1, :], (8, 128)) for c in range(6)]
        near_sum = None
        far_sum = None
        for q in (3, 2, 1, 0):
            turned = [pltpu.roll(x, 8 * q, 1, stride=1, stride_axis=0) for x in other]
            gap = [mine[c] - turned[c] for c in range(3)]
            along, across = pair_math(gap[0] * gap[0] + gap[1] * gap[1] + gap[2] * gap[2] + 0.25, coef)
            to_near = across * (gap[0] * turned[3] + gap[1] * turned[4] + gap[2] * turned[5])
            to_far = across * (gap[0] * mine[3] + gap[1] * mine[4] + gap[2] * mine[5])
            near_add = [along * turned[3 + c] + to_near * gap[c] for c in range(3)]
            far_add = [along * mine[3 + c] + to_far * gap[c] for c in range(3)]
            if near_sum is None:
                near_sum, far_sum = near_add, far_add
            else:
                near_sum = [a + b for a, b in zip(near_sum, near_add)]
                far_sum = [pltpu.roll(a, 120, 1) + b for a, b in zip(far_sum, far_add)]
        far_sum = [jnp.take_along_axis(a, unturn, axis=1) for a in far_sum]
        near_vel = stacked(near_sum)
        half = jnp.where(left, pltpu.roll(near_vel, 64, 1), 0.0)
        near_vel = jnp.where(left, near_vel, 0.0) + pltpu.roll(half, 32, 1)
        near_vel = near_vel + pltpu.roll(near_vel, 64, 1)
        far_vel = stacked(far_sum)
        far_vel = far_vel + pltpu.roll(far_vel, 64, 1)
        return near_vel, far_vel

    low = bounds[0]
    high = bounds[1]

    def turn(i, carry):
        found = []
        for k in range(unroll):
            p = low + i * unroll + k
            alive = p < high
            both = jnp.where(alive, pairs[p], 0)
            ka, kb = both >> 16, both & 65535
            found.append((alive, ka, kb, one(ka, kb)))
        for alive, ka, kb, (near_vel, far_vel) in found:
            near_ref[row(ka), :] += jnp.where((left == ((ka & 1) == 0)) & alive, near_vel, 0.0)
            if not beyond:
                alive = alive & (ka != kb)
            far_sums[row(kb), :] += jnp.where((left == ((kb & 1) == 0)) & alive, far_vel, 0.0)
        return carry

    lax.fori_loop(0, lax.div(jnp.maximum(high - low, 0) + (unroll - 1), jnp.int32(unroll)), turn, 0)

    if beyond:
        for c in range(3):
            @pl.loop(0, rp // 8)
            def _(i):
                at = pl.ds(pl.multiple_of(c * rp + i * 8, 8), 8)
                far_ref[at, :] = far_sums[pl.ds(i * 64 + c, 8, stride=8), :]


def pair_call(pairs, bounds, cells, near, beside=None, far=None, after=(), coef=ERFCX_COEF, unroll=8):
    rp = cells.shape[0] // 8
    beyond = beside is not None
    extra = [beside, far] if beyond else []
    out = [jax.ShapeDtypeStruct((8 * rp, 128), jnp.float32), jax.ShapeDtypeStruct((8, 128), jnp.float32)]
    scratch = []
    if beyond:
        out.append(jax.ShapeDtypeStruct((3 * rp, 128), jnp.float32))
        scratch = [pltpu.VMEM((8 * rp, 128), jnp.float32)] * 2
    return pl.pallas_call(
        ignoring(
            functools.partial(pair_kernel, rp=rp, coef=coef, unroll=unroll, beyond=beyond),
            4 + len(extra),
            len(after),
        ),
        out_shape=tuple(out),
        in_specs=[SMEM_SPEC] * 2 + [VMEM_SPEC] * (2 + len(extra)) + [ANY_SPEC] * len(after),
        out_specs=(VMEM_SPEC,) * len(out),
        scratch_shapes=scratch,
        compiler_params=pltpu.CompilerParams(vmem_limit_bytes=8 * 1024 * 1024),
        name="beyond" if beyond else "within",
    )(pairs, bounds, cells, near, *extra, *after)


def signed_wave(grid_index):
    return jnp.where(grid_index < G // 2, grid_index, grid_index - G).astype(jnp.float32) * (
        2.0 * math.pi / (G * grid_spacing)
    )


def forward_pass(real_in, imag_in, form, cos_part, sin_part):
    contract = partial(jnp.einsum, precision=lax.Precision.HIGHEST)
    real_out = contract(form, real_in, cos_part) + contract(form, imag_in, sin_part)
    imag_out = contract(form, imag_in, cos_part) - contract(form, real_in, sin_part)
    return (real_out, imag_out)


def inverse_pass(real_in, imag_in, form, cos_part, sin_part):
    contract = partial(jnp.einsum, precision=lax.Precision.HIGHEST)
    real_out = contract(form, real_in, cos_part) - contract(form, imag_in, sin_part)
    imag_out = contract(form, imag_in, cos_part) + contract(form, real_in, sin_part)
    return (real_out, imag_out)


def project_flow(spectrum, wave_x, wave_y, wave_z):
    wave_sq = wave_x * wave_x + wave_y * wave_y + wave_z * wave_z
    wave_safe = jnp.where(wave_sq > 0, wave_sq, 1.0)
    spread_sq = wave_sq / (4.0 * split_xi**2)
    green_fn = jnp.where(
        wave_sq > 0,
        (1.0 - bead_radius**2 * wave_sq / 3.0)
        * (1.0 + spread_sq)
        * jnp.exp(-spread_sq)
        / wave_safe,
        0.0,
    )
    along_wave = (wave_x * spectrum[0] + wave_y * spectrum[1] + wave_z * spectrum[2]) / wave_safe
    return jnp.stack(
        [
            green_fn * (spectrum[0] - wave_x * along_wave),
            green_fn * (spectrum[1] - wave_y * along_wave),
            green_fn * (spectrum[2] - wave_z * along_wave),
        ]
    )


def kspace_part(force_rows, n_gx, n_gy):
    local_x = G // n_gx
    local_y = G // n_gy
    grid_index = jnp.arange(G, dtype=jnp.int32)
    phase_grid = (grid_index[:, None] * grid_index[None, :] % G).astype(jnp.float32) * (
        2.0 * math.pi / G
    )
    cosine_table = jnp.cos(phase_grid)
    sine_table = jnp.sin(phase_grid)
    contract = partial(jnp.einsum, precision=lax.Precision.HIGHEST)
    force_field = force_rows.reshape(3, local_x, local_y, G)
    wave_full = signed_wave(grid_index)
    row_gx = lax.axis_index("gx")
    row_gy = lax.axis_index("gy")
    freq_count = G
    spec_z = jnp.stack(
        [
            contract("cabz,zk->cabk", force_field, cosine_table),
            -contract("cabz,zk->cabk", force_field, sine_table),
        ]
    )
    cos_x = cosine_table.reshape(n_gx, local_x, G)
    sin_x = sine_table.reshape(n_gx, local_x, G)
    cos_y = cosine_table.reshape(n_gy, local_y, G)
    sin_y = sine_table.reshape(n_gy, local_y, G)
    depth_part = freq_count // n_gx
    width_part = G // n_gy
    slabs = lax.all_to_all(spec_z[:, :, None], "gx", split_axis=5, concat_axis=2, tiled=True)
    xr_part, xi_part = forward_pass(slabs[0], slabs[1], "ciabl,iak->cbkl", cos_x, sin_x)
    pencils = lax.all_to_all(
        jnp.stack([xr_part, xi_part])[:, :, None], "gy", split_axis=4, concat_axis=2, tiled=True
    )
    yr_part, yi_part = forward_pass(pencils[0], pencils[1], "cjbkl,jbm->ckml", cos_y, sin_y)
    wave_x = signed_wave(row_gy * width_part + jnp.arange(width_part, dtype=jnp.int32))[
        :, None, None
    ]
    wave_y = wave_full[None, :, None]
    wave_z = signed_wave(row_gx * depth_part + jnp.arange(depth_part, dtype=jnp.int32))[
        None, None, :
    ]
    flow_real = project_flow(yr_part, wave_x, wave_y, wave_z)
    flow_imag = project_flow(yi_part, wave_x, wave_y, wave_z)
    br_part, bi_part = inverse_pass(flow_real, flow_imag, "ckml,jbm->cjbkl", cos_y, sin_y)
    back = lax.all_to_all(
        jnp.stack([br_part, bi_part]), "gy", split_axis=2, concat_axis=4, tiled=True
    )[:, :, 0]
    ar_part, ai_part = inverse_pass(back[0], back[1], "cbkl,iak->ciabl", cos_x, sin_x)
    gathered = lax.all_to_all(
        jnp.stack([ar_part, ai_part]), "gx", split_axis=2, concat_axis=5, tiled=True
    )[:, :, 0]
    result = contract("cabk,zk->cabz", gathered[0], cosine_table) - contract(
        "cabk,zk->cabz", gathered[1], sine_table
    )
    return (result / float(G**3)).reshape(3, local_x * local_y * G)


matmul = functools.partial(lax.dot_general, precision=lax.Precision.HIGHEST, preferred_element_type=jnp.float32)
PLAIN = (((1,), (0,)), ((), ()))
TURNED = (((1,), (1,)), ((), ()))


def wave_tables(n_gx, n_gy):
    share = G // 2 // n_gx
    width = G // n_gy
    grid = np.arange(G)
    turn = 2.0 * math.pi * (np.outer(grid, grid) % G) / G
    cos, sin = np.cos(turn), np.sin(turn)
    half = width // 2
    order = np.zeros(G, np.int64)
    for j in range(n_gy):
        for p in range(half):
            k = j * half + p
            order[j * width + p] = k
            order[j * width + half + p] = (G - k) % G if k else G // 2
    ahead = np.zeros((G, n_gx, 2, share))
    ahead[:, :, 0] = cos[:, : G // 2].reshape(G, n_gx, share)
    ahead[:, :, 1] = -sin[:, : G // 2].reshape(G, n_gx, share)
    back = 2.0 * ahead
    ahead[:, 0, 1, 0] = cos[:, G // 2]
    back[:, 0, 0, 0] = 1.0
    back[:, 0, 1, 0] = cos[:, G // 2]
    unit = 2.0 * math.pi / (G * grid_spacing)
    signed = np.where(grid < G // 2, grid, grid - G) * unit
    plain = np.where(grid == G // 2, 0.0, signed)
    edge = signed - plain
    lane = np.arange(128)
    across = np.zeros((n_gy, 8, 128))
    across[:, 0] = plain[order].reshape(n_gy, 1, width)[:, 0][:, lane % width]
    across[:, 1] = edge[order].reshape(n_gy, 1, width)[:, 0][:, lane % width]
    across[0, 2] = lane % half == 0
    deep = np.zeros((n_gx, 8, 128))
    per = 128 // width
    for v in range(share // per):
        deep[:, v] = (np.arange(n_gx)[:, None] * share + v * per + lane // width) * unit
    down = np.stack([np.broadcast_to(t[:, None], (G, 128)) for t in (plain, edge)])
    tables = {
        "ahead": ahead.reshape(G, G),
        "back": back.reshape(G, G).T,
        "first": np.concatenate([cos[:, order], sin[:, order]], axis=1),
        "first_back": np.concatenate([cos[:, order], sin[:, order]], axis=1),
        "second": np.concatenate([cos, sin], axis=0),
        "across": across,
        "deep": deep,
        "down": down,
    }
    return {name: np.asarray(table, np.float32) for name, table in tables.items()}


def spread(tiles, at, group, tall):
    count = 128 // group
    lane = lax.shift_right_logical(lax.broadcasted_iota(jnp.int32, (tall, 128), 1), group.bit_length() - 1)
    out = None
    for g, tile in enumerate(tiles):
        moved = pltpu.roll(tile, group * ((g - at) % count), 1) if g != at else tile
        out = moved if out is None else jnp.where(lane == g, moved, out)
    return out


def depth_kernel(field_ref, table_ref, out_ref, spec, *, n_gx, tall, wide):
    rows = tall * wide
    for c in range(3):
        spec[c * rows : (c + 1) * rows, :] = matmul(field_ref[c * rows : (c + 1) * rows, :], table_ref[...], PLAIN)
    group = G // n_gx
    count = n_gx

    @pl.loop(0, 3 * wide // count)
    def _(i):
        c = lax.div(i, jnp.int32(wide // count))
        b = (i - c * (wide // count)) * count
        tiles = [spec[pl.ds(c * rows + b + g, tall, stride=wide), :] for g in range(count)]
        for p in range(n_gx):
            out_ref[p, :, pl.ds(pl.multiple_of(i * 128, 128), 128)] = spread(tiles, p, group, tall)


def first_kernel(data_ref, table_ref, out_ref, turned, *, n_gy, share, wide):
    group = G // n_gy
    per = 128 // (2 * share)

    @pl.loop(0, 3 * wide // per)
    def _(i):
        c = lax.div(i, jnp.int32(wide // per))
        b = (i - c * (wide // per)) * per
        piece = jnp.transpose(data_ref[:, pl.ds(pl.multiple_of(i * 128, 128), 128)])
        both = matmul(piece, table_ref[...], PLAIN)
        for g in range(per):
            lo, mid, hi = g * 2 * share, (g * 2 + 1) * share, (g * 2 + 2) * share
            real = both[lo:mid, :128] + both[mid:hi, 128:]
            imag = both[mid:hi, :128] - both[lo:mid, 128:]
            turned[pl.ds(2 * c * share * wide + b + g, share, stride=wide), :] = real
            turned[pl.ds((2 * c + 1) * share * wide + b + g, share, stride=wide), :] = imag

    count = 128 // group

    @pl.loop(0, 6 * share // count)
    def _(i):
        at = i * (count * wide)
        tiles = [turned[pl.ds(pl.multiple_of(at + u * wide, 8), wide), :] for u in range(count)]
        for j in range(n_gy):
            out_ref[j, i] = spread(tiles, j, group, wide)


def second_kernel(ids, data_ref, table_ref, across_ref, deep_ref, down_ref, out_ref, flow, *, n_gy, views, wide):
    lane = lax.broadcasted_iota(jnp.int32, (G, 128), 1)
    width = G // n_gy
    half = width // 2
    across = across_ref[ids[1]]
    deep = deep_ref[ids[0]]
    alone = (lane < width) & (ids[0] == 0)
    mirror_self = across[2:3, :] > 0.5
    upper = (lane & half) != 0

    def whole(tile):
        return jnp.concatenate([data_ref[j, tile] for j in range(n_gy)], axis=0)

    def mirrored(value):
        other = jnp.where(upper, pltpu.roll(value, half, 1), pltpu.roll(value, 128 - half, 1))
        return jnp.where(mirror_self, value, other)

    def ahead(real, imag):
        one = matmul(table_ref[...], real, PLAIN)
        two = matmul(table_ref[...], imag, PLAIN)
        return one[:G] + two[G:], two[:G] - one[G:]

    def projected(spectrum, deep_plain, deep_edge):
        plain = (across[0:1, :], down_ref[0], deep_plain)
        edge = (across[1:2, :], down_ref[1], deep_edge)
        waves = [p + e for p, e in zip(plain, edge)]
        wave_sq = waves[0] * waves[0] + waves[1] * waves[1] + waves[2] * waves[2]
        live = wave_sq > 0
        inverse = 1.0 / jnp.where(live, wave_sq, 1.0)
        spread_sq = wave_sq / (4.0 * split_xi**2)
        green = (1.0 - bead_radius**2 * wave_sq / 3.0) * (1.0 + spread_sq) * jnp.exp(-spread_sq) * inverse
        green = jnp.where(live, green / float(G**3), 0.0)
        out = []
        for r in range(2):
            regular = sum(w * spectrum[c][r] for c, w in enumerate(plain)) * inverse
            nyquist = sum(w * spectrum[c][r] for c, w in enumerate(edge)) * inverse
            out.append([green * (spectrum[c][r] - plain[c] * regular - edge[c] * nyquist) for c in range(3)])
        return out

    zero = jnp.zeros((1, 128), jnp.float32)
    for v in range(views):
        spectrum = []
        apart = []
        for c in range(3):
            real = whole((2 * c) * views + v)
            imag = whole((2 * c + 1) * views + v)
            if v == 0:
                off_real = jnp.where(alone, 0.5 * (real - mirrored(real)), 0.0)
                off_imag = jnp.where(alone, 0.5 * (imag + mirrored(imag)), 0.0)
                apart.append(ahead(off_real, off_imag))
                real, imag = real - off_real, imag - off_imag
            spectrum.append(ahead(real, imag))
        found = projected(spectrum, deep[v : v + 1, :], zero)
        if v == 0:
            extra = projected(apart, zero, zero - math.pi / grid_spacing)
            found = [[a + b for a, b in zip(one, two)] for one, two in zip(found, extra)]
        for c in range(3):
            one = matmul(table_ref[...], found[0][c], PLAIN)
            two = matmul(table_ref[...], found[1][c], PLAIN)
            real, imag = one[:G] - two[G:], two[:G] + one[G:]
            for j in range(n_gy):
                out_ref[j, (2 * c) * views + v] = real[j * wide : (j + 1) * wide]
                out_ref[j, (2 * c + 1) * views + v] = imag[j * wide : (j + 1) * wide]


def first_back_kernel(data_ref, table_ref, out_ref, turned, *, n_gy, share, wide):
    group = G // n_gy
    count = n_gy
    per = 128 // (2 * share)

    @pl.loop(0, 6 * share // count)
    def _(i):
        tiles = [data_ref[j, i] for j in range(n_gy)]
        for u in range(count):
            turned[pl.ds(pl.multiple_of((i * count + u) * wide, 8), wide), :] = spread(tiles, u, group, wide)

    @pl.loop(0, 3 * wide // per)
    def _(i):
        c = lax.div(i, jnp.int32(wide // per))
        b = (i - c * (wide // per)) * per
        rows = []
        for g in range(per):
            real = turned[pl.ds(2 * c * share * wide + b + g, share, stride=wide), :]
            imag = turned[pl.ds((2 * c + 1) * share * wide + b + g, share, stride=wide), :]
            rows.append(jnp.concatenate([real, -imag], axis=1))
            rows.append(jnp.concatenate([imag, real], axis=1))
        piece = jnp.concatenate(rows, axis=0)
        out_ref[:, pl.ds(pl.multiple_of(i * 128, 128), 128)] = matmul(table_ref[...], piece, TURNED)


def depth_back_kernel(data_ref, table_ref, out_ref, spec, *, n_gx, tall, wide):
    rows = tall * wide
    group = G // n_gx
    count = n_gx

    @pl.loop(0, 3 * wide // count)
    def _(i):
        c = lax.div(i, jnp.int32(wide // count))
        b = (i - c * (wide // count)) * count
        tiles = [data_ref[p, :, pl.ds(pl.multiple_of(i * 128, 128), 128)] for p in range(n_gx)]
        for g in range(count):
            spec[pl.ds(c * rows + b + g, tall, stride=wide), :] = spread(tiles, g, group, tall)

    for c in range(3):
        out_ref[c * rows : (c + 1) * rows, :] = matmul(spec[c * rows : (c + 1) * rows, :], table_ref[...], PLAIN)


def waves(grid_data, n_gx, n_gy, fill):
    tall, wide, share = G // n_gx, G // n_gy, G // 2 // n_gx
    rows = 3 * tall * wide
    views = share * wide // 128
    tables = wave_tables(n_gx, n_gy)
    f32 = jnp.float32

    def run(name, kernel, shape, args, scratch, specs=None, after=(), **sizes):
        return pl.pallas_call(
            marking(ignoring(functools.partial(kernel, **sizes), len(args), len(after)), len(args) + len(after)),
            out_shape=(jax.ShapeDtypeStruct(shape, f32), jax.ShapeDtypeStruct((8, 128), f32)),
            in_specs=(specs or [VMEM_SPEC] * len(args)) + [ANY_SPEC] * len(after),
            out_specs=(VMEM_SPEC,) * 2,
            scratch_shapes=[pltpu.VMEM(scratch, f32)],
            compiler_params=pltpu.CompilerParams(vmem_limit_bytes=8 * 1024 * 1024),
            name=name,
            grid=(1,),
        )(*args, *after)

    def swap(value, axis):
        return lax.all_to_all(value, axis, split_axis=0, concat_axis=0, tiled=True)

    def full(shape):
        return pl.BlockSpec(shape, lambda i: (0,) * len(shape))

    force = pl.BlockSpec((rows, 128), lambda i: (1, 0))
    lanes = 6 * wide * share
    ids = jnp.stack([lax.axis_index("gx"), lax.axis_index("gy")]).astype(jnp.int32)
    value, token = run("depth", depth_kernel, (n_gx, tall, lanes), (grid_data, tables["ahead"]), (rows, 128),
                [force, full((G, 128))], n_gx=n_gx, tall=tall, wide=wide)
    after = fill(0, token)
    value = swap(value, "gx").reshape(G, lanes)
    value, token = run("first", first_kernel, (n_gy, 6 * views, wide, 128), (value, tables["first"]), (rows, 128),
                after=after, n_gy=n_gy, share=share, wide=wide)
    after = fill(1, token)
    value = swap(value.reshape(n_gy, 6 * views * wide, 128), "gy").reshape(n_gy, 6 * views, wide, 128)
    args = (ids, value, tables["second"], tables["across"], tables["deep"], tables["down"])
    value, token = run("second", second_kernel, (n_gy, 6 * views, wide, 128), args, (8, 128),
                [SMEM_SPEC] + [VMEM_SPEC] * 5, after, n_gy=n_gy, views=views, wide=wide)
    after = fill(2, token)
    value = swap(value.reshape(n_gy, 6 * views * wide, 128), "gy").reshape(n_gy, 6 * views, wide, 128)
    value, token = run("first_back", first_back_kernel, (G, lanes), (value, tables["first_back"]), (rows, 128),
                after=after, n_gy=n_gy, share=share, wide=wide)
    after = fill(3, token)
    value = swap(value.reshape(n_gx, tall, lanes), "gx")
    value, _ = run("depth_back", depth_back_kernel, (rows, 128), (value, tables["back"]), (rows, 128),
               after=after, n_gx=n_gx, tall=tall, wide=wide)
    return value


def shards(positions, noise, route, node_perm, pair_first, pair_second, pair_count):
    n_gx = lax.axis_size("gx")
    n_gy = lax.axis_size("gy")
    both = ("gx", "gy")
    peers = n_gx * n_gy
    slots = node_perm.shape[2]
    depth = slots // peers // 128
    rows = positions.shape[1] // 128
    rp = slots // 128
    swap = partial(lax.all_to_all, axis_name=both, split_axis=0, concat_axis=0, tiled=True)

    bounds = jnp.arange(peers + 1, dtype=jnp.int32) * (slots // peers)
    starts = jnp.sum(route[None, :] < bounds[:, None], axis=1, dtype=jnp.int32)
    taken = swap(slots_call(starts, route.reshape(rows, 128), depth))
    places = positions.reshape(3, rows, 128)
    data = swap(pack_call(starts, places, depth))
    counts = jnp.sum(taken >= 0, axis=(1, 2), dtype=jnp.int32)
    own_order = lax.dynamic_index_in_dim(node_perm, lax.axis_index("gx"), 0, False)
    nodes, node_lists, row_lists = nodes_call(taken, own_order.reshape(peers, depth, 128), slots)
    own_pairs, far_pairs, totals = order_call(pair_first[0], pair_second[0], pair_count, slots // CELL)
    grid_data, cells = scatter_call(node_lists, counts, data, rp, after=(totals,))

    steps = pair_first.shape[1]
    marks = [jnp.int32(0)] + [jnp.minimum(totals[0], steps * part // 128) for part in PARTS] + [totals[0]]
    state = {"sums": jnp.zeros_like(cells)}

    def within(n, after):
        state["sums"], token = pair_call(own_pairs, jnp.stack(marks[n : n + 2]), cells, state["sums"], after=after)
        return token

    def fill(n, token):
        if n < 3:
            if n == 1:
                ready, _ = lax.optimization_barrier((grid_data, token))
                state["beside"] = shifted(ready, "gx", -1)
            return (within(n, (token,)),)
        bounds = jnp.stack([marks[0], totals[1]])
        none = jnp.zeros((3 * rp, 128), jnp.float32)
        state["sums"], _, far = pair_call(
            far_pairs, bounds, cells, state["sums"], state["beside"], none, after=(token,)
        )
        state["far"] = shifted(far, "gx", 1)
        return (within(3, ()),)

    share = G // 2 // n_gx
    if share % 8 == 0 and share * (G // n_gy) % 128 == 0:
        wave_vel = waves(grid_data, n_gx, n_gy, fill)
    else:
        wave_vel = kspace_part(grid_data[3 * rp :], n_gx, n_gy).reshape(3 * rp, 128)
        for n in range(4):
            fill(n, wave_vel)
    back = swap(gather_call(row_lists, counts, nodes, state["sums"], wave_vel, state["far"]))
    moved, drift = finish_call(starts, back, places, noise.reshape(3, rows, 128))
    return (moved.reshape(positions.shape), drift.reshape(positions.shape))


def solution(mesh):
    in_specs = (
        P(None, ("gx", "gy")),
        P(None, ("gx", "gy")),
        P(("gx", "gy")),
        P(None, "gy", None),
        P(("gx", "gy"), None),
        P(("gx", "gy"), None),
        P(("gx", "gy")),
    )
    out_specs = (P(None, ("gx", "gy")), P(None, ("gx", "gy")))
    return jax.shard_map(shards, mesh=mesh, in_specs=in_specs, out_specs=out_specs, check_vma=False)
```

```python
import functools
from functools import partial
import math

import jax
import jax.numpy as jnp
import numpy as np
from jax import lax
from jax.experimental import pallas as pl
from jax.experimental.pallas import tpu as pltpu
from jax.sharding import PartitionSpec as P

G = 128
BEAD_CH = 64
CELL = 64


bead_radius = 0.5
split_xi = 0.5
time_step = 0.01
fene_k = 30.0
fene_reach = 1.5
bend_k = 2.0
grid_spacing = 4.0
pair_block = 64


def shifted(value, axis, by):
    devices = lax.axis_size(axis)
    return lax.ppermute(value, axis, [(i, (i + by) % devices) for i in range(devices)])


SPAN = 16
PARTS = (25, 37, 52)

SMEM_SPEC = pl.BlockSpec(memory_space=pltpu.SMEM)
LIST_SPEC = pl.BlockSpec(memory_space=pltpu.SMEM)
VMEM_SPEC = pl.BlockSpec(memory_space=pltpu.VMEM)
MOVED_SPEC = pl.BlockSpec(memory_space=pltpu.VMEM)


ANY_SPEC = pl.BlockSpec(memory_space=pl.ANY)


def launch(kernel, *, out_shape, in_specs, out_specs, **options):
    def block(spec, value):
        shape = value.shape
        return pl.BlockSpec(shape, lambda i: (0,) * len(shape)) if spec is VMEM_SPEC or spec is MOVED_SPEC else spec

    def placed(spec, value):
        return spec is VMEM_SPEC or spec is LIST_SPEC or (spec is ANY_SPEC and value.dtype == jnp.float32)

    def run(*args):
        several = isinstance(out_shape, tuple)
        shapes = out_shape if several else (out_shape,)
        outs = out_specs if several else (out_specs,)
        found = tuple(block(s, v) for s, v in zip(outs, shapes))
        kept = tuple(pltpu.HBM(v.shape, v.dtype) if s is VMEM_SPEC else v for s, v in zip(outs, shapes))
        args = [
            pltpu.with_memory_space_constraint(jnp.asarray(v), pltpu.HBM) if placed(s, v) else v
            for s, v in zip(in_specs, args)
        ]
        return pl.pallas_call(
            kernel,
            out_shape=kept if several else kept[0],
            grid=(1,),
            in_specs=[block(s, v) for s, v in zip(in_specs, args)],
            out_specs=found if several else found[0],
            **options,
        )(*args)

    return run


def ignoring(kernel, inputs, extra):
    def run(*refs):
        kernel(*refs[:inputs], *refs[inputs + extra :])

    return run


def marking(kernel, inputs):
    def run(*refs):
        refs[inputs + 1][...] = jnp.zeros(refs[inputs + 1].shape, jnp.float32)
        kernel(*refs[: inputs + 1], *refs[inputs + 2 :])

    return run


def lane_index(rows):
    return lax.broadcasted_iota(jnp.int32, (rows, 128), 1)


def window(table, at, rows):
    row = lax.shift_right_logical(at, 7)
    lead = at & 127
    head = pltpu.roll(table[pl.ds(row, rows), :], (128 - lead) & 127, 1)
    tail = pltpu.roll(table[pl.ds(row + 1, rows), :], (128 - lead) & 127, 1)
    return jnp.where(lane_index(rows) < 128 - lead, head, tail)


def slots_kernel(starts, route_ref, out_ref, table, *, rows, depth):
    table[pl.ds(0, rows), :] = route_ref[...]
    table[pl.ds(rows, depth + 8), :] = jnp.zeros((depth + 8, 128), jnp.int32)
    place = lane_index(depth) + lax.broadcasted_iota(jnp.int32, (depth, 128), 0) * 128

    @pl.loop(0, out_ref.shape[0])
    def _(t):
        at = starts[t]
        slot = window(table, at, depth) - t * (depth * 128)
        out_ref[t] = jnp.where(place < starts[t + 1] - at, slot, -1)


def slots_call(starts, route, depth):
    rows = route.shape[0]
    peers = starts.shape[0] - 1
    return launch(
        functools.partial(slots_kernel, rows=rows, depth=depth),
        out_shape=jax.ShapeDtypeStruct((peers, depth, 128), jnp.int32),
        in_specs=[SMEM_SPEC, VMEM_SPEC],
        out_specs=VMEM_SPEC,
        scratch_shapes=[pltpu.VMEM((rows + depth + 8, 128), jnp.int32)],
        compiler_params=pltpu.CompilerParams(vmem_limit_bytes=32 * 1024 * 1024),
        name="slots",
    )(starts, route)


def chain_forces(pos):
    rows = pos[0].shape[0]
    place = lane_index(rows) & (BEAD_CH - 1)
    bonded = place < BEAD_CH - 1
    bent = place < BEAD_CH - 2
    after = (place > 0) & bonded
    bond = [jnp.where(bonded, pltpu.roll(x, 127, 1) - x, 0.5) for x in pos]
    square = bond[0] * bond[0] + bond[1] * bond[1] + bond[2] * bond[2]
    inverse = lax.rsqrt(square)
    unit = [b * inverse for b in bond]
    following = [pltpu.roll(u, 127, 1) for u in unit]
    previous = [pltpu.roll(u, 1, 1) for u in unit]
    cosine = sum(u * v for u, v in zip(unit, following))
    cosine_before = pltpu.roll(cosine, 1, 1)
    pull = fene_k / (1.0 - square / fene_reach**2)
    out = []
    for c in range(3):
        turn = jnp.where(bent, following[c] - cosine * unit[c], 0.0)
        turn = turn + jnp.where(after, previous[c] - cosine_before * unit[c], 0.0)
        slope = jnp.where(bonded, pull * bond[c] - bend_k * inverse * turn, 0.0)
        out.append(slope - pltpu.roll(slope, 1, 1))
    return out


def pack_kernel(starts, pos_ref, out_ref, table, *, rows, depth, stride):
    step = 32 if rows % 32 == 0 else 8

    @pl.loop(0, rows // step)
    def _(i):
        at = pl.multiple_of(i * step, step)
        pos = [pos_ref[c, pl.ds(at, step), :] for c in range(3)]
        for c, value in enumerate(pos + chain_forces(pos)):
            table[pl.ds(c * stride + at, step), :] = value

    for c in range(6):
        table[pl.ds(c * stride + rows, stride - rows), :] = jnp.zeros((stride - rows, 128), jnp.float32)

    @pl.loop(0, out_ref.shape[0])
    def _(t):
        at = starts[t]
        for c in range(6):
            out_ref[t, c * depth : (c + 1) * depth, :] = window(table, at + c * stride * 128, depth)


def pack_call(starts, pos, depth):
    rows = pos.shape[1]
    peers = starts.shape[0] - 1
    stride = rows + depth + 8
    stride += -stride % 8
    return launch(
        functools.partial(pack_kernel, rows=rows, depth=depth, stride=stride),
        out_shape=jax.ShapeDtypeStruct((peers, 6 * depth, 128), jnp.float32),
        in_specs=[SMEM_SPEC, VMEM_SPEC],
        out_specs=VMEM_SPEC,
        scratch_shapes=[pltpu.VMEM((6 * stride, 128), jnp.float32)],
        compiler_params=pltpu.CompilerParams(vmem_limit_bytes=32 * 1024 * 1024),
        name="pack",
    )(starts, pos)


def list_count(depth):
    return 8 if depth % 8 == 0 else 1


def nodes_kernel(slots_ref, perm_ref, node_ref, *list_refs, depth, spare):
    tile = list_count(depth)
    parts = depth // tile

    @pl.loop(0, slots_ref.shape[0])
    def _(t):
        rows = [jnp.broadcast_to(perm_ref[t, w : w + 1, :], (8, 128)) for w in range(depth)]
        for r in range(parts):
            slot = jnp.broadcast_to(slots_ref[t, r * tile : (r + 1) * tile, :], (8, 128))
            place = slot & 127
            which = slot >> 7
            node = jnp.full((8, 128), spare, jnp.int32)
            for w in range(depth):
                node = jnp.where(which == w, jnp.take_along_axis(rows[w], place, axis=1), node)
            packed = ((node >> 12) << 7) | (node & 127)
            node_ref[t, r * tile : (r + 1) * tile, :] = node[:tile]
            for u in range(tile):
                list_refs[u][pl.ds(t * parts + r, 1), :] = node[u : u + 1]
                list_refs[tile + u][pl.ds(t * parts + r, 1), :] = packed[u : u + 1]


def nodes_call(slots, perm, spare):
    peers, depth, _ = slots.shape
    lists = list_count(depth)
    one = jax.ShapeDtypeStruct((peers * depth // lists, 128), jnp.int32)
    found = launch(
        functools.partial(nodes_kernel, depth=depth, spare=spare),
        out_shape=(jax.ShapeDtypeStruct(slots.shape, jnp.int32),) + (one,) * (2 * lists),
        in_specs=[MOVED_SPEC, VMEM_SPEC],
        out_specs=(VMEM_SPEC,) * (1 + 2 * lists),
        compiler_params=pltpu.CompilerParams(vmem_limit_bytes=32 * 1024 * 1024),
        name="nodes",
    )(slots, perm)
    flat = [x.reshape(-1) for x in found[1:]]
    return found[0], flat[:lists], flat[lists:]


def move_rows(lists, count, t, depth, move):
    width = len(lists)
    parts = depth // width

    def part(p, carry):
        live = jnp.minimum(count - p * (width * 128), 128)
        base = (t * parts + p) * 128
        start = p * (width * 128)

        def some(i, carry):
            for k in range(SPAN):
                at = i * SPAN + k
                for u in range(width):
                    move(start + at + u * 128, lists[u][base + at])
            return carry

        return lax.fori_loop(0, lax.div(live + (SPAN - 1), jnp.int32(SPAN)), some, carry)

    whole = width * 128
    lax.fori_loop(0, lax.div(count + (whole - 1), jnp.int32(whole)), part, 0)


def scatter_kernel(counts, in_ref, *refs, depth, rp, lists):
    nodes = refs[:lists]
    out_ref, cells_ref, table, rows_ref = refs[lists:]

    @pl.loop(0, rp)
    def _(k):
        table[pl.ds(pl.multiple_of(k * 128, 128), 128), :] = jnp.zeros((128, 128), jnp.float32)

    together = 4 if depth % 4 == 0 else 1

    @pl.loop(0, in_ref.shape[0])
    def _(t):
        def turn(i, carry):
            for j in range(together):
                r = i * together + j
                piece = in_ref[t, pl.ds(r, 6, stride=depth), :]
                piece = jnp.concatenate([piece, jnp.zeros((2, 128), jnp.float32)], axis=0)
                piece = jnp.concatenate([piece] * 16, axis=0)
                rows_ref[pl.ds(pl.multiple_of(r * 128, 128), 128), :] = jnp.transpose(piece)
            return carry

        def move(at, node):
            table[pl.ds(node, 1), :] = rows_ref[pl.ds(at, 1), :]

        count = counts[t]
        part = together * 128
        lax.fori_loop(0, lax.div(count + (part - 1), jnp.int32(part)), turn, 0)
        move_rows(nodes, count, t, depth, move)

    group = lane_index(8) >> 3

    @pl.loop(0, rp // 16)
    def _(g):
        tiles = []
        for i in range(16):
            tile = table[pl.ds(pl.multiple_of(g * 2048, 2048) + 8 * i, 8), :]
            for k in range(1, 16):
                one = table[pl.ds(pl.multiple_of(g * 2048, 2048) + k * 128 + 8 * i, 8), :]
                tile = jnp.where(group == k, one, tile)
            tiles.append(tile)
        at = pl.multiple_of(g * 128, 128)
        cells_ref[pl.ds(at, 128), :] = jnp.transpose(jnp.concatenate(tiles, axis=0))
        for c in range(6):
            out_ref[pl.ds(pl.multiple_of(c * rp + g * 16, 16), 16), :] = cells_ref[pl.ds(at + c, 16, stride=8), :]


def scatter_call(nodes, counts, data, rp, after=()):
    depth = data.shape[1] // 6
    return launch(
        ignoring(
            functools.partial(scatter_kernel, depth=depth, rp=rp, lists=len(nodes)), 2 + len(nodes), len(after)
        ),
        out_shape=(
            jax.ShapeDtypeStruct((6 * rp, 128), jnp.float32),
            jax.ShapeDtypeStruct((8 * rp, 128), jnp.float32),
        ),
        in_specs=[SMEM_SPEC, MOVED_SPEC] + [LIST_SPEC] * len(nodes) + [ANY_SPEC] * len(after),
        out_specs=(VMEM_SPEC,) * 2,
        scratch_shapes=[
            pltpu.VMEM((rp * 128 + 8, 128), jnp.float32),
            pltpu.VMEM((depth * 128, 128), jnp.float32),
        ],
        compiler_params=pltpu.CompilerParams(vmem_limit_bytes=52 * 1024 * 1024),
        name="scatter",
    )(counts, data, *nodes, *after)


def gather_kernel(counts, node_ref, sums_ref, one_ref, two_ref, *refs, depth, rp, lists):
    rows = refs[:lists]
    out_ref, table, found, comb = refs[lists:]
    comb[...] = jnp.zeros((128, 128), jnp.float32)

    @pl.loop(0, rp // 32)
    def _(g):
        for c in range(3):
            at = pl.ds(pl.multiple_of(c * rp + g * 32, 32), 32)
            comb[pl.ds(c, 32, stride=4), :] = one_ref[at, :] + two_ref[at, :]
        for i in range(16):
            pair = [sums_ref[pl.ds(pl.multiple_of((g * 32 + 2 * i + h) * 8, 8), 8), :] for h in range(2)]
            both = pair[0] + pltpu.roll(pair[1], 4, 0)
            comb[8 * i : 8 * i + 8, :] = comb[8 * i : 8 * i + 8, :] + both
        table[pl.ds(pl.multiple_of(g * 128, 128), 128), :] = jnp.transpose(comb[...])

    together = 4 if depth % 4 == 0 else 1

    @pl.loop(0, out_ref.shape[0])
    def _(t):
        def move(at, row):
            found[pl.ds(at, 1), :] = table[pl.ds(row, 1), :]

        def turn(i, carry):
            for j in range(together):
                r = i * together + j
                turned = jnp.transpose(found[pl.ds(pl.multiple_of(r * 128, 128), 128), :])
                place = jnp.broadcast_to(node_ref[t, pl.ds(r, 1), :], (8, 128)) >> 7
                half = (place >> 1) & 15
                value = turned[:8]
                for h in range(1, 16):
                    value = jnp.where(half == h, turned[8 * h : 8 * h + 8], value)
                value = jnp.where((place & 1) == 1, pltpu.roll(value, 4, 0), value)
                out_ref[t, pl.ds(r, 3, stride=depth), :] = value[:3]
            return carry

        count = counts[t]
        part = together * 128
        move_rows(rows, count, t, depth, move)
        lax.fori_loop(0, lax.div(count + (part - 1), jnp.int32(part)), turn, 0)


def gather_call(rows, counts, nodes, sums, one, two):
    rp = one.shape[0] // 3
    peers, depth, _ = nodes.shape
    return launch(
        functools.partial(gather_kernel, depth=depth, rp=rp, lists=len(rows)),
        out_shape=jax.ShapeDtypeStruct((peers, 3 * depth, 128), jnp.float32),
        in_specs=[SMEM_SPEC] + [VMEM_SPEC] * 4 + [LIST_SPEC] * len(rows),
        out_specs=VMEM_SPEC,
        scratch_shapes=[
            pltpu.VMEM((rp * 4 + 8, 128), jnp.float32),
            pltpu.VMEM((depth * 128, 128), jnp.float32),
            pltpu.VMEM((128, 128), jnp.float32),
        ],
        compiler_params=pltpu.CompilerParams(vmem_limit_bytes=32 * 1024 * 1024),
        name="gather",
    )(counts, nodes, sums, one, two, *rows)


def finish_kernel(starts, in_ref, pos_ref, noise_ref, moved_ref, drift_ref, table, *, rows, depth, stride):
    lane = lane_index(depth)
    first = lane_index(1)

    @pl.loop(0, in_ref.shape[0])
    def _(t):
        at = starts[t]
        row = lax.shift_right_logical(at, 7)
        lead = at & 127
        for c in range(3):
            value = pltpu.roll(in_ref[t, c * depth : (c + 1) * depth, :], lead, 1)
            here = pl.ds(c * stride + row, depth)
            behind = pl.ds(c * stride + row + 1, depth)
            edge = table[pl.ds(c * stride + row, 1), :]
            table[behind, :] = value
            if depth > 1:
                body = jnp.where(lane[1:] < lead, value[:-1], value[1:])
                table[pl.ds(c * stride + row + 1, depth - 1), :] = body
            table[pl.ds(c * stride + row, 1), :] = jnp.where(first < lead, edge, value[:1])

    step = 8

    @pl.loop(0, rows // step)
    def _(i):
        at = pl.multiple_of(i * step, step)
        for c in range(3):
            drift = time_step * table[pl.ds(c * stride + at, step), :]
            drift_ref[c, pl.ds(at, step), :] = drift
            moved_ref[c, pl.ds(at, step), :] = pos_ref[c, pl.ds(at, step), :] + drift + noise_ref[c, pl.ds(at, step), :]


def finish_call(starts, data, pos, noise):
    rows = pos.shape[1]
    depth = data.shape[1] // 3
    stride = rows + depth + 8
    stride += -stride % 8
    return launch(
        functools.partial(finish_kernel, rows=rows, depth=depth, stride=stride),
        out_shape=(jax.ShapeDtypeStruct(pos.shape, jnp.float32),) * 2,
        in_specs=[SMEM_SPEC, MOVED_SPEC] + [VMEM_SPEC] * 2,
        out_specs=(VMEM_SPEC,) * 2,
        scratch_shapes=[pltpu.VMEM((3 * stride, 128), jnp.float32)],
        compiler_params=pltpu.CompilerParams(vmem_limit_bytes=32 * 1024 * 1024),
        name="finish",
    )(starts, data, pos, noise)


ERFCX_COEF = (0.06548172872398669,
    -0.3609186250151195,
    0.6338942267842493,
    -0.3384301108125971,
    0.4003704641202259,
    0.13581047899030682,
    0.2395463173952274,
    0.22417089752024144,
    7.010614160106155e-05)


def pair_math(square, coef):
    inverse = lax.rsqrt(square)
    ratio = pl.reciprocal(1.0 + 0.2 * (square * inverse))
    scaled = coef[0] * ratio + coef[1]
    for k in coef[2:]:
        scaled = scaled * ratio + k
    decay = jnp.exp(-0.25 * square)
    inverse_sq = inverse * inverse
    screen = scaled * inverse
    along = decay * (screen * (0.375 + 0.0625 * inverse_sq) + 0.125)
    across = (decay * inverse_sq) * (screen * (0.375 - 0.1875 * inverse_sq) - 0.125)
    return along, across

def order_kernel(first, second, count, own_ref, far_ref, totals, *, blocks):
    def step(p, sizes):
        own, far = sizes
        other = second[p]
        within = other < blocks
        both = first[p] * 65536 + other
        own_ref[own] = both
        far_ref[far] = both - blocks
        inside = within.astype(jnp.int32)
        return own + inside, far + 1 - inside

    own, far = lax.fori_loop(0, count[0], step, (jnp.int32(0), jnp.int32(0)))
    steps = first.shape[0]
    totals[0] = 0
    for n, part in enumerate(PARTS):
        totals[n + 1] = jnp.minimum(own, steps * part // 128)
    totals[len(PARTS) + 1] = own
    totals[len(PARTS) + 2] = 0
    totals[len(PARTS) + 3] = far


def order_call(first, second, count, blocks):
    size = first.shape[0] + 8
    return launch(
        functools.partial(order_kernel, blocks=blocks),
        out_shape=(jax.ShapeDtypeStruct((size,), jnp.int32),) * 2 + (jax.ShapeDtypeStruct((len(PARTS) + 4,), jnp.int32),),
        in_specs=[SMEM_SPEC] * 3,
        out_specs=(SMEM_SPEC,) * 3,
        compiler_params=pltpu.CompilerParams(vmem_limit_bytes=32 * 1024 * 1024),
        name="order",
    )(first, second, count)


def fill_cells(src_ref, cells, rp):
    @pl.loop(0, rp // 8)
    def _(i):
        at = pl.multiple_of(i * 8, 8)
        for c in range(6):
            cells[pl.ds(at * 8 + c, 8, stride=8), :] = src_ref[pl.ds(pl.multiple_of(c * rp + at, 8), 8), :]


def pair_kernel(pairs, bounds, cells_ref, *refs, rp, coef, unroll, beyond, part, fresh):
    if not fresh:
        near_in, *refs = refs
    if beyond:
        other_ref, near_ref, token, far_ref, other_cells, far_sums = refs
        fill_cells(other_ref, other_cells, rp)
        far_sums[...] = jnp.zeros(far_sums.shape, jnp.float32)
    else:
        near_ref, token = refs
        other_cells, far_sums = cells_ref, near_ref
    lane = lax.broadcasted_iota(jnp.int32, (8, 128), 1)
    sub = lax.broadcasted_iota(jnp.int32, (8, 128), 0)
    left = lane < 64
    unturn = (lane + sub) & 127
    near_ref[...] = jnp.zeros(near_ref.shape, jnp.float32) if fresh else near_in[...]
    token[...] = jnp.zeros((8, 128), jnp.float32)

    def row(k):
        return pl.ds(pl.multiple_of((k >> 1) * 8, 8), 8)

    def both_halves(table, k):
        cell = table[row(k), :]
        return jnp.where(left == ((k & 1) == 0), cell, pltpu.roll(cell, 64, 1))

    def stacked(parts):
        out = jnp.zeros((8, 128), jnp.float32)
        for c, part in enumerate(parts):
            out = jnp.where(sub == c, jnp.sum(part, axis=0, keepdims=True), out)
        return out

    def one(ka, kb):
        near = both_halves(cells_ref, ka)
        near = jnp.where(left, near, pltpu.roll(near, 96, 1))
        far = both_halves(other_cells, kb)
        mine = [jnp.broadcast_to(near[c : c + 1, :], (8, 128)) for c in range(6)]
        other = [jnp.broadcast_to(far[c : c + 1, :], (8, 128)) for c in range(6)]
        near_sum = None
        far_sum = None
        for q in (3, 2, 1, 0):
            turned = [pltpu.roll(x, 8 * q, 1, stride=1, stride_axis=0) for x in other]
            gap = [mine[c] - turned[c] for c in range(3)]
            along, across = pair_math(gap[0] * gap[0] + gap[1] * gap[1] + gap[2] * gap[2] + 0.25, coef)
            to_near = across * (gap[0] * turned[3] + gap[1] * turned[4] + gap[2] * turned[5])
            to_far = across * (gap[0] * mine[3] + gap[1] * mine[4] + gap[2] * mine[5])
            near_add = [along * turned[3 + c] + to_near * gap[c] for c in range(3)]
            far_add = [along * mine[3 + c] + to_far * gap[c] for c in range(3)]
            if near_sum is None:
                near_sum, far_sum = near_add, far_add
            else:
                near_sum = [a + b for a, b in zip(near_sum, near_add)]
                far_sum = [pltpu.roll(a, 120, 1) + b for a, b in zip(far_sum, far_add)]
        far_sum = [jnp.take_along_axis(a, unturn, axis=1) for a in far_sum]
        near_vel = stacked(near_sum)
        half = jnp.where(left, pltpu.roll(near_vel, 64, 1), 0.0)
        near_vel = jnp.where(left, near_vel, 0.0) + pltpu.roll(half, 32, 1)
        near_vel = near_vel + pltpu.roll(near_vel, 64, 1)
        far_vel = stacked(far_sum)
        far_vel = far_vel + pltpu.roll(far_vel, 64, 1)
        return near_vel, far_vel

    low = bounds[part]
    high = bounds[part + 1]

    def turn(i, carry):
        found = []
        for k in range(unroll):
            p = low + i * unroll + k
            alive = p < high
            both = jnp.where(alive, pairs[p], 0)
            ka, kb = both >> 16, both & 65535
            found.append((alive, ka, kb, one(ka, kb)))
        for alive, ka, kb, (near_vel, far_vel) in found:
            near_ref[row(ka), :] += jnp.where((left == ((ka & 1) == 0)) & alive, near_vel, 0.0)
            if not beyond:
                alive = alive & (ka != kb)
            far_sums[row(kb), :] += jnp.where((left == ((kb & 1) == 0)) & alive, far_vel, 0.0)
        return carry

    lax.fori_loop(0, lax.div(jnp.maximum(high - low, 0) + (unroll - 1), jnp.int32(unroll)), turn, 0)

    if beyond:
        for c in range(3):
            @pl.loop(0, rp // 8)
            def _(i):
                at = pl.ds(pl.multiple_of(c * rp + i * 8, 8), 8)
                far_ref[at, :] = far_sums[pl.ds(i * 64 + c, 8, stride=8), :]


def pair_call(pairs, bounds, part, cells, near=None, beside=None, after=(), coef=ERFCX_COEF, unroll=8):
    rp = cells.shape[0] // 8
    beyond = beside is not None
    fresh = near is None
    extra = [cells] + ([] if fresh else [near]) + ([beside] if beyond else [])
    out = [jax.ShapeDtypeStruct((8 * rp, 128), jnp.float32), jax.ShapeDtypeStruct((8, 128), jnp.float32)]
    scratch = []
    if beyond:
        out.append(jax.ShapeDtypeStruct((3 * rp, 128), jnp.float32))
        scratch = [pltpu.VMEM((8 * rp, 128), jnp.float32)] * 2
    return launch(
        ignoring(
            functools.partial(
                pair_kernel, rp=rp, coef=coef, unroll=unroll, beyond=beyond, part=part, fresh=fresh
            ),
            2 + len(extra),
            len(after),
        ),
        out_shape=tuple(out),
        in_specs=[SMEM_SPEC] * 2 + [VMEM_SPEC] * (len(extra) - beyond) + [MOVED_SPEC] * beyond + [ANY_SPEC] * len(after),
        out_specs=(VMEM_SPEC,) * len(out),
        scratch_shapes=scratch,
        compiler_params=pltpu.CompilerParams(vmem_limit_bytes=32 * 1024 * 1024),
        name="beyond" if beyond else "within",
    )(pairs, bounds, *extra, *after)


def signed_wave(grid_index):
    return jnp.where(grid_index < G // 2, grid_index, grid_index - G).astype(jnp.float32) * (
        2.0 * math.pi / (G * grid_spacing)
    )


def forward_pass(real_in, imag_in, form, cos_part, sin_part):
    contract = partial(jnp.einsum, precision=lax.Precision.HIGHEST)
    real_out = contract(form, real_in, cos_part) + contract(form, imag_in, sin_part)
    imag_out = contract(form, imag_in, cos_part) - contract(form, real_in, sin_part)
    return (real_out, imag_out)


def inverse_pass(real_in, imag_in, form, cos_part, sin_part):
    contract = partial(jnp.einsum, precision=lax.Precision.HIGHEST)
    real_out = contract(form, real_in, cos_part) - contract(form, imag_in, sin_part)
    imag_out = contract(form, imag_in, cos_part) + contract(form, real_in, sin_part)
    return (real_out, imag_out)


def project_flow(spectrum, wave_x, wave_y, wave_z):
    wave_sq = wave_x * wave_x + wave_y * wave_y + wave_z * wave_z
    wave_safe = jnp.where(wave_sq > 0, wave_sq, 1.0)
    spread_sq = wave_sq / (4.0 * split_xi**2)
    green_fn = jnp.where(
        wave_sq > 0,
        (1.0 - bead_radius**2 * wave_sq / 3.0)
        * (1.0 + spread_sq)
        * jnp.exp(-spread_sq)
        / wave_safe,
        0.0,
    )
    along_wave = (wave_x * spectrum[0] + wave_y * spectrum[1] + wave_z * spectrum[2]) / wave_safe
    return jnp.stack(
        [
            green_fn * (spectrum[0] - wave_x * along_wave),
            green_fn * (spectrum[1] - wave_y * along_wave),
            green_fn * (spectrum[2] - wave_z * along_wave),
        ]
    )


def kspace_part(force_rows, n_gx, n_gy):
    local_x = G // n_gx
    local_y = G // n_gy
    grid_index = jnp.arange(G, dtype=jnp.int32)
    phase_grid = (grid_index[:, None] * grid_index[None, :] % G).astype(jnp.float32) * (
        2.0 * math.pi / G
    )
    cosine_table = jnp.cos(phase_grid)
    sine_table = jnp.sin(phase_grid)
    contract = partial(jnp.einsum, precision=lax.Precision.HIGHEST)
    force_field = force_rows.reshape(3, local_x, local_y, G)
    wave_full = signed_wave(grid_index)
    row_gx = lax.axis_index("gx")
    row_gy = lax.axis_index("gy")
    freq_count = G
    spec_z = jnp.stack(
        [
            contract("cabz,zk->cabk", force_field, cosine_table),
            -contract("cabz,zk->cabk", force_field, sine_table),
        ]
    )
    cos_x = cosine_table.reshape(n_gx, local_x, G)
    sin_x = sine_table.reshape(n_gx, local_x, G)
    cos_y = cosine_table.reshape(n_gy, local_y, G)
    sin_y = sine_table.reshape(n_gy, local_y, G)
    depth_part = freq_count // n_gx
    width_part = G // n_gy
    slabs = lax.all_to_all(spec_z[:, :, None], "gx", split_axis=5, concat_axis=2, tiled=True)
    xr_part, xi_part = forward_pass(slabs[0], slabs[1], "ciabl,iak->cbkl", cos_x, sin_x)
    pencils = lax.all_to_all(
        jnp.stack([xr_part, xi_part])[:, :, None], "gy", split_axis=4, concat_axis=2, tiled=True
    )
    yr_part, yi_part = forward_pass(pencils[0], pencils[1], "cjbkl,jbm->ckml", cos_y, sin_y)
    wave_x = signed_wave(row_gy * width_part + jnp.arange(width_part, dtype=jnp.int32))[
        :, None, None
    ]
    wave_y = wave_full[None, :, None]
    wave_z = signed_wave(row_gx * depth_part + jnp.arange(depth_part, dtype=jnp.int32))[
        None, None, :
    ]
    flow_real = project_flow(yr_part, wave_x, wave_y, wave_z)
    flow_imag = project_flow(yi_part, wave_x, wave_y, wave_z)
    br_part, bi_part = inverse_pass(flow_real, flow_imag, "ckml,jbm->cjbkl", cos_y, sin_y)
    back = lax.all_to_all(
        jnp.stack([br_part, bi_part]), "gy", split_axis=2, concat_axis=4, tiled=True
    )[:, :, 0]
    ar_part, ai_part = inverse_pass(back[0], back[1], "cbkl,iak->ciabl", cos_x, sin_x)
    gathered = lax.all_to_all(
        jnp.stack([ar_part, ai_part]), "gx", split_axis=2, concat_axis=5, tiled=True
    )[:, :, 0]
    result = contract("cabk,zk->cabz", gathered[0], cosine_table) - contract(
        "cabk,zk->cabz", gathered[1], sine_table
    )
    return (result / float(G**3)).reshape(3, local_x * local_y * G)


matmul = functools.partial(lax.dot_general, precision=lax.Precision.HIGHEST, preferred_element_type=jnp.float32)
PLAIN = (((1,), (0,)), ((), ()))
TURNED = (((1,), (1,)), ((), ()))


def wave_tables(n_gx, n_gy):
    share = G // 2 // n_gx
    width = G // n_gy
    grid = np.arange(G)
    turn = 2.0 * math.pi * (np.outer(grid, grid) % G) / G
    cos, sin = np.cos(turn), np.sin(turn)
    half = width // 2
    order = np.zeros(G, np.int64)
    for j in range(n_gy):
        for p in range(half):
            k = j * half + p
            order[j * width + p] = k
            order[j * width + half + p] = (G - k) % G if k else G // 2
    ahead = np.zeros((G, n_gx, 2, share))
    ahead[:, :, 0] = cos[:, : G // 2].reshape(G, n_gx, share)
    ahead[:, :, 1] = -sin[:, : G // 2].reshape(G, n_gx, share)
    back = 2.0 * ahead
    ahead[:, 0, 1, 0] = cos[:, G // 2]
    back[:, 0, 0, 0] = 1.0
    back[:, 0, 1, 0] = cos[:, G // 2]
    unit = 2.0 * math.pi / (G * grid_spacing)
    signed = np.where(grid < G // 2, grid, grid - G) * unit
    plain = np.where(grid == G // 2, 0.0, signed)
    edge = signed - plain
    lane = np.arange(128)
    across = np.zeros((n_gy, 8, 128))
    across[:, 0] = plain[order].reshape(n_gy, 1, width)[:, 0][:, lane % width]
    across[:, 1] = edge[order].reshape(n_gy, 1, width)[:, 0][:, lane % width]
    across[0, 2] = lane % half == 0
    deep = np.zeros((n_gx, 8, 128))
    per = 128 // width
    for v in range(share // per):
        deep[:, v] = (np.arange(n_gx)[:, None] * share + v * per + lane // width) * unit
    down = np.stack([np.broadcast_to(t[:, None], (G, 128)) for t in (plain, edge)])
    tables = {
        "ahead": ahead.reshape(G, G),
        "back": back.reshape(G, G).T,
        "first": np.concatenate([cos[:, order], sin[:, order]], axis=1),
        "first_back": np.concatenate([cos[:, order], sin[:, order]], axis=1),
        "second": np.concatenate([cos, sin], axis=0),
        "across": across,
        "deep": deep,
        "down": down,
    }
    return {name: np.asarray(table, np.float32) for name, table in tables.items()}


def spread(tiles, at, group, tall):
    count = 128 // group
    lane = lax.shift_right_logical(lax.broadcasted_iota(jnp.int32, (tall, 128), 1), group.bit_length() - 1)
    out = None
    for g, tile in enumerate(tiles):
        moved = pltpu.roll(tile, group * ((g - at) % count), 1) if g != at else tile
        out = moved if out is None else jnp.where(lane == g, moved, out)
    return out


def depth_kernel(field_ref, table_ref, out_ref, spec, *, n_gx, tall, wide):
    rows = tall * wide
    for c in range(3):
        spec[c * rows : (c + 1) * rows, :] = matmul(field_ref[c * rows : (c + 1) * rows, :], table_ref[...], PLAIN)
    group = G // n_gx
    count = n_gx

    @pl.loop(0, 3 * wide // count)
    def _(i):
        c = lax.div(i, jnp.int32(wide // count))
        b = (i - c * (wide // count)) * count
        tiles = [spec[pl.ds(c * rows + b + g, tall, stride=wide), :] for g in range(count)]
        for p in range(n_gx):
            out_ref[p, :, pl.ds(pl.multiple_of(i * 128, 128), 128)] = spread(tiles, p, group, tall)


def first_kernel(data_ref, table_ref, out_ref, turned, *, n_gy, share, wide):
    group = G // n_gy
    per = 128 // (2 * share)

    @pl.loop(0, 3 * wide // per)
    def _(i):
        c = lax.div(i, jnp.int32(wide // per))
        b = (i - c * (wide // per)) * per
        piece = jnp.transpose(data_ref[:, pl.ds(pl.multiple_of(i * 128, 128), 128)])
        both = matmul(piece, table_ref[...], PLAIN)
        for g in range(per):
            lo, mid, hi = g * 2 * share, (g * 2 + 1) * share, (g * 2 + 2) * share
            real = both[lo:mid, :128] + both[mid:hi, 128:]
            imag = both[mid:hi, :128] - both[lo:mid, 128:]
            turned[pl.ds(2 * c * share * wide + b + g, share, stride=wide), :] = real
            turned[pl.ds((2 * c + 1) * share * wide + b + g, share, stride=wide), :] = imag

    count = 128 // group

    @pl.loop(0, 6 * share // count)
    def _(i):
        at = i * (count * wide)
        tiles = [turned[pl.ds(pl.multiple_of(at + u * wide, 8), wide), :] for u in range(count)]
        for j in range(n_gy):
            out_ref[j, i] = spread(tiles, j, group, wide)


def second_kernel(ids, data_ref, table_ref, across_ref, deep_ref, down_ref, out_ref, flow, *, n_gy, views, wide):
    lane = lax.broadcasted_iota(jnp.int32, (G, 128), 1)
    width = G // n_gy
    half = width // 2
    across = across_ref[ids[1]]
    deep = deep_ref[ids[0]]
    alone = (lane < width) & (ids[0] == 0)
    mirror_self = across[2:3, :] > 0.5
    upper = (lane & half) != 0

    def whole(tile):
        return jnp.concatenate([data_ref[j, tile] for j in range(n_gy)], axis=0)

    def mirrored(value):
        other = jnp.where(upper, pltpu.roll(value, half, 1), pltpu.roll(value, 128 - half, 1))
        return jnp.where(mirror_self, value, other)

    def ahead(real, imag):
        one = matmul(table_ref[...], real, PLAIN)
        two = matmul(table_ref[...], imag, PLAIN)
        return one[:G] + two[G:], two[:G] - one[G:]

    def projected(spectrum, deep_plain, deep_edge):
        plain = (across[0:1, :], down_ref[0], deep_plain)
        edge = (across[1:2, :], down_ref[1], deep_edge)
        waves = [p + e for p, e in zip(plain, edge)]
        wave_sq = waves[0] * waves[0] + waves[1] * waves[1] + waves[2] * waves[2]
        live = wave_sq > 0
        inverse = 1.0 / jnp.where(live, wave_sq, 1.0)
        spread_sq = wave_sq / (4.0 * split_xi**2)
        green = (1.0 - bead_radius**2 * wave_sq / 3.0) * (1.0 + spread_sq) * jnp.exp(-spread_sq) * inverse
        green = jnp.where(live, green / float(G**3), 0.0)
        out = []
        for r in range(2):
            regular = sum(w * spectrum[c][r] for c, w in enumerate(plain)) * inverse
            nyquist = sum(w * spectrum[c][r] for c, w in enumerate(edge)) * inverse
            out.append([green * (spectrum[c][r] - plain[c] * regular - edge[c] * nyquist) for c in range(3)])
        return out

    zero = jnp.zeros((1, 128), jnp.float32)
    for v in range(views):
        spectrum = []
        apart = []
        for c in range(3):
            real = whole((2 * c) * views + v)
            imag = whole((2 * c + 1) * views + v)
            if v == 0:
                off_real = jnp.where(alone, 0.5 * (real - mirrored(real)), 0.0)
                off_imag = jnp.where(alone, 0.5 * (imag + mirrored(imag)), 0.0)
                apart.append(ahead(off_real, off_imag))
                real, imag = real - off_real, imag - off_imag
            spectrum.append(ahead(real, imag))
        found = projected(spectrum, deep[v : v + 1, :], zero)
        if v == 0:
            extra = projected(apart, zero, zero - math.pi / grid_spacing)
            found = [[a + b for a, b in zip(one, two)] for one, two in zip(found, extra)]
        for c in range(3):
            one = matmul(table_ref[...], found[0][c], PLAIN)
            two = matmul(table_ref[...], found[1][c], PLAIN)
            real, imag = one[:G] - two[G:], two[:G] + one[G:]
            for j in range(n_gy):
                out_ref[j, (2 * c) * views + v] = real[j * wide : (j + 1) * wide]
                out_ref[j, (2 * c + 1) * views + v] = imag[j * wide : (j + 1) * wide]


def first_back_kernel(data_ref, table_ref, out_ref, turned, *, n_gy, share, wide):
    group = G // n_gy
    count = n_gy
    per = 128 // (2 * share)

    @pl.loop(0, 6 * share // count)
    def _(i):
        tiles = [data_ref[j, i] for j in range(n_gy)]
        for u in range(count):
            turned[pl.ds(pl.multiple_of((i * count + u) * wide, 8), wide), :] = spread(tiles, u, group, wide)

    @pl.loop(0, 3 * wide // per)
    def _(i):
        c = lax.div(i, jnp.int32(wide // per))
        b = (i - c * (wide // per)) * per
        rows = []
        for g in range(per):
            real = turned[pl.ds(2 * c * share * wide + b + g, share, stride=wide), :]
            imag = turned[pl.ds((2 * c + 1) * share * wide + b + g, share, stride=wide), :]
            rows.append(jnp.concatenate([real, -imag], axis=1))
            rows.append(jnp.concatenate([imag, real], axis=1))
        piece = jnp.concatenate(rows, axis=0)
        out_ref[:, pl.ds(pl.multiple_of(i * 128, 128), 128)] = matmul(table_ref[...], piece, TURNED)


def depth_back_kernel(data_ref, table_ref, out_ref, spec, *, n_gx, tall, wide):
    rows = tall * wide
    group = G // n_gx
    count = n_gx

    @pl.loop(0, 3 * wide // count)
    def _(i):
        c = lax.div(i, jnp.int32(wide // count))
        b = (i - c * (wide // count)) * count
        tiles = [data_ref[p, :, pl.ds(pl.multiple_of(i * 128, 128), 128)] for p in range(n_gx)]
        for g in range(count):
            spec[pl.ds(c * rows + b + g, tall, stride=wide), :] = spread(tiles, g, group, tall)

    for c in range(3):
        out_ref[c * rows : (c + 1) * rows, :] = matmul(spec[c * rows : (c + 1) * rows, :], table_ref[...], PLAIN)


def waves(grid_data, n_gx, n_gy, fill):
    tall, wide, share = G // n_gx, G // n_gy, G // 2 // n_gx
    rows = 3 * tall * wide
    views = share * wide // 128
    tables = wave_tables(n_gx, n_gy)
    f32 = jnp.float32

    def run(name, kernel, shape, args, scratch, specs=None, after=(), **sizes):
        return launch(
            marking(ignoring(functools.partial(kernel, **sizes), len(args), len(after)), len(args) + len(after)),
            out_shape=(jax.ShapeDtypeStruct(shape, f32), jax.ShapeDtypeStruct((8, 128), f32)),
            in_specs=(specs or [MOVED_SPEC] + [VMEM_SPEC] * (len(args) - 1)) + [ANY_SPEC] * len(after),
            out_specs=(VMEM_SPEC,) * 2,
            scratch_shapes=[pltpu.VMEM(scratch, f32)],
            compiler_params=pltpu.CompilerParams(vmem_limit_bytes=32 * 1024 * 1024),
            name=name,
        )(*args, *after)

    def swap(value, axis):
        return lax.all_to_all(value, axis, split_axis=0, concat_axis=0, tiled=True)

    force = pl.BlockSpec((rows, 128), lambda i: (1, 0))
    lanes = 6 * wide * share
    ids = jnp.stack([lax.axis_index("gx"), lax.axis_index("gy")]).astype(jnp.int32)
    value, token = run("depth", depth_kernel, (n_gx, tall, lanes), (pltpu.with_memory_space_constraint(grid_data, pltpu.HBM), tables["ahead"]), (rows, 128),
                [force, VMEM_SPEC], n_gx=n_gx, tall=tall, wide=wide)
    after = fill(0, token)
    value = swap(value, "gx").reshape(G, lanes)
    value, token = run("first", first_kernel, (n_gy, 6 * views, wide, 128), (value, tables["first"]), (rows, 128),
                after=after, n_gy=n_gy, share=share, wide=wide)
    after = fill(1, token)
    value = swap(value.reshape(n_gy, 6 * views * wide, 128), "gy").reshape(n_gy, 6 * views, wide, 128)
    args = (ids, value, tables["second"], tables["across"], tables["deep"], tables["down"])
    value, token = run("second", second_kernel, (n_gy, 6 * views, wide, 128), args, (8, 128),
                [SMEM_SPEC, MOVED_SPEC] + [VMEM_SPEC] * 4, after, n_gy=n_gy, views=views, wide=wide)
    after = fill(2, token)
    value = swap(value.reshape(n_gy, 6 * views * wide, 128), "gy").reshape(n_gy, 6 * views, wide, 128)
    value, token = run("first_back", first_back_kernel, (G, lanes), (value, tables["first_back"]), (rows, 128),
                after=after, n_gy=n_gy, share=share, wide=wide)
    after = fill(3, token)
    value = swap(value.reshape(n_gx, tall, lanes), "gx")
    value, _ = run("depth_back", depth_back_kernel, (rows, 128), (value, tables["back"]), (rows, 128),
               after=after, n_gx=n_gx, tall=tall, wide=wide)
    return value


def shards(positions, noise, route, node_perm, pair_first, pair_second, pair_count):
    n_gx = lax.axis_size("gx")
    n_gy = lax.axis_size("gy")
    both = ("gx", "gy")
    peers = n_gx * n_gy
    slots = node_perm.shape[2]
    depth = slots // peers // 128
    rows = positions.shape[1] // 128
    rp = slots // 128
    swap = partial(lax.all_to_all, axis_name=both, split_axis=0, concat_axis=0, tiled=True)

    bounds = jnp.arange(peers + 1, dtype=jnp.int32) * (slots // peers)
    starts = jnp.sum(route[None, :] < bounds[:, None], axis=1, dtype=jnp.int32)
    taken = swap(slots_call(starts, route.reshape(rows, 128), depth))
    places = positions.reshape(3, rows, 128)
    data = swap(pack_call(starts, places, depth))
    counts = jnp.sum(taken >= 0, axis=(1, 2), dtype=jnp.int32)
    own_order = lax.dynamic_index_in_dim(node_perm, lax.axis_index("gx"), 0, False)
    nodes, node_lists, row_lists = nodes_call(taken, own_order.reshape(peers, depth, 128), slots)
    own_pairs, far_pairs, totals = order_call(pair_first[0], pair_second[0], pair_count, slots // CELL)
    grid_data, cells = scatter_call(node_lists, counts, data, rp, after=(totals,))

    state = {"sums": None}

    def within(n, after):
        state["sums"], token = pair_call(own_pairs, totals, n, cells, state["sums"], after=after)
        return token

    def fill(n, token):
        if n < 3:
            if n == 1:
                ready, _ = lax.optimization_barrier((grid_data, token))
                state["beside"] = shifted(ready, "gx", -1)
            return (within(n, (token,)),)
        state["sums"], _, far = pair_call(
            far_pairs, totals, len(PARTS) + 2, cells, state["sums"], state["beside"], after=(token,)
        )
        state["far"] = shifted(far, "gx", 1)
        return (within(3, ()),)

    share = G // 2 // n_gx
    if share % 8 == 0 and share * (G // n_gy) % 128 == 0:
        wave_vel = waves(grid_data, n_gx, n_gy, fill)
    else:
        wave_vel = kspace_part(grid_data[3 * rp :], n_gx, n_gy).reshape(3 * rp, 128)
        for n in range(4):
            fill(n, wave_vel)
    back = swap(gather_call(row_lists, counts, nodes, state["sums"], wave_vel, state["far"]))
    moved, drift = finish_call(starts, back, places, noise.reshape(3, rows, 128))
    return (moved.reshape(positions.shape), drift.reshape(positions.shape))


def solution(mesh):
    in_specs = (
        P(None, ("gx", "gy")),
        P(None, ("gx", "gy")),
        P(("gx", "gy")),
        P(None, "gy", None),
        P(("gx", "gy"), None),
        P(("gx", "gy"), None),
        P(("gx", "gy")),
    )
    out_specs = (P(None, ("gx", "gy")), P(None, ("gx", "gy")))
    return jax.shard_map(shards, mesh=mesh, in_specs=in_specs, out_specs=out_specs, check_vma=False)
```

```python
import functools
from functools import partial
import math

import jax
import jax.numpy as jnp
import numpy as np
from jax import lax
from jax.experimental import pallas as pl
from jax.experimental.pallas import tpu as pltpu
from jax.sharding import PartitionSpec as P

G = 128
BEAD_CH = 64
CELL = 64


bead_radius = 0.5
split_xi = 0.5
time_step = 0.01
fene_k = 30.0
fene_reach = 1.5
bend_k = 2.0
grid_spacing = 4.0
pair_block = 64


def shifted(value, axis, by):
    devices = lax.axis_size(axis)
    return lax.ppermute(value, axis, [(i, (i + by) % devices) for i in range(devices)])


SPAN = 16
PARTS = (25, 37, 52)

SMEM_SPEC = pl.BlockSpec(memory_space=pltpu.SMEM)
LIST_SPEC = pl.BlockSpec(memory_space=pl.ANY)
VMEM_SPEC = pl.BlockSpec(memory_space=pltpu.VMEM)
MOVED_SPEC = pl.BlockSpec(memory_space=pltpu.VMEM)


ANY_SPEC = pl.BlockSpec(memory_space=pl.ANY)


def launch(kernel, *, out_shape, in_specs, out_specs, **options):
    def block(spec, value):
        shape = value.shape
        return pl.BlockSpec(shape, lambda i: (0,) * len(shape)) if spec is VMEM_SPEC or spec is MOVED_SPEC else spec

    def placed(spec, value):
        return spec is VMEM_SPEC or spec is LIST_SPEC or (spec is ANY_SPEC and value.dtype == jnp.float32)

    def run(*args):
        several = isinstance(out_shape, tuple)
        shapes = out_shape if several else (out_shape,)
        outs = out_specs if several else (out_specs,)
        found = tuple(block(s, v) for s, v in zip(outs, shapes))
        kept = tuple(pltpu.HBM(v.shape, v.dtype) if s is VMEM_SPEC else v for s, v in zip(outs, shapes))
        args = [
            pltpu.with_memory_space_constraint(jnp.asarray(v), pltpu.HBM) if placed(s, v) else v
            for s, v in zip(in_specs, args)
        ]
        return pl.pallas_call(
            kernel,
            out_shape=kept if several else kept[0],
            grid=(1,),
            in_specs=[block(s, v) for s, v in zip(in_specs, args)],
            out_specs=found if several else found[0],
            **options,
        )(*args)

    return run


def ignoring(kernel, inputs, extra):
    def run(*refs):
        kernel(*refs[:inputs], *refs[inputs + extra :])

    return run


def marking(kernel, inputs):
    def run(*refs):
        refs[inputs + 1][...] = jnp.zeros(refs[inputs + 1].shape, jnp.float32)
        kernel(*refs[: inputs + 1], *refs[inputs + 2 :])

    return run


def lane_index(rows):
    return lax.broadcasted_iota(jnp.int32, (rows, 128), 1)


def window(table, at, rows):
    row = lax.shift_right_logical(at, 7)
    lead = at & 127
    head = pltpu.roll(table[pl.ds(row, rows), :], (128 - lead) & 127, 1)
    tail = pltpu.roll(table[pl.ds(row + 1, rows), :], (128 - lead) & 127, 1)
    return jnp.where(lane_index(rows) < 128 - lead, head, tail)


def slots_kernel(starts, route_ref, out_ref, table, *, rows, depth):
    table[pl.ds(0, rows), :] = route_ref[...]
    table[pl.ds(rows, depth + 8), :] = jnp.zeros((depth + 8, 128), jnp.int32)
    place = lane_index(depth) + lax.broadcasted_iota(jnp.int32, (depth, 128), 0) * 128

    @pl.loop(0, out_ref.shape[0])
    def _(t):
        at = starts[t]
        slot = window(table, at, depth) - t * (depth * 128)
        out_ref[t] = jnp.where(place < starts[t + 1] - at, slot, -1)


def slots_call(starts, route, depth):
    rows = route.shape[0]
    peers = starts.shape[0] - 1
    return launch(
        functools.partial(slots_kernel, rows=rows, depth=depth),
        out_shape=jax.ShapeDtypeStruct((peers, depth, 128), jnp.int32),
        in_specs=[SMEM_SPEC, VMEM_SPEC],
        out_specs=VMEM_SPEC,
        scratch_shapes=[pltpu.VMEM((rows + depth + 8, 128), jnp.int32)],
        compiler_params=pltpu.CompilerParams(vmem_limit_bytes=32 * 1024 * 1024),
        name="slots",
    )(starts, route)


def chain_forces(pos):
    rows = pos[0].shape[0]
    place = lane_index(rows) & (BEAD_CH - 1)
    bonded = place < BEAD_CH - 1
    bent = place < BEAD_CH - 2
    after = (place > 0) & bonded
    bond = [jnp.where(bonded, pltpu.roll(x, 127, 1) - x, 0.5) for x in pos]
    square = bond[0] * bond[0] + bond[1] * bond[1] + bond[2] * bond[2]
    inverse = lax.rsqrt(square)
    unit = [b * inverse for b in bond]
    following = [pltpu.roll(u, 127, 1) for u in unit]
    previous = [pltpu.roll(u, 1, 1) for u in unit]
    cosine = sum(u * v for u, v in zip(unit, following))
    cosine_before = pltpu.roll(cosine, 1, 1)
    pull = fene_k / (1.0 - square / fene_reach**2)
    out = []
    for c in range(3):
        turn = jnp.where(bent, following[c] - cosine * unit[c], 0.0)
        turn = turn + jnp.where(after, previous[c] - cosine_before * unit[c], 0.0)
        slope = jnp.where(bonded, pull * bond[c] - bend_k * inverse * turn, 0.0)
        out.append(slope - pltpu.roll(slope, 1, 1))
    return out


def pack_kernel(starts, pos_ref, out_ref, table, *, rows, depth, stride):
    step = 32 if rows % 32 == 0 else 8

    @pl.loop(0, rows // step)
    def _(i):
        at = pl.multiple_of(i * step, step)
        pos = [pos_ref[c, pl.ds(at, step), :] for c in range(3)]
        for c, value in enumerate(pos + chain_forces(pos)):
            table[pl.ds(c * stride + at, step), :] = value

    for c in range(6):
        table[pl.ds(c * stride + rows, stride - rows), :] = jnp.zeros((stride - rows, 128), jnp.float32)

    @pl.loop(0, out_ref.shape[0])
    def _(t):
        at = starts[t]
        for c in range(6):
            out_ref[t, c * depth : (c + 1) * depth, :] = window(table, at + c * stride * 128, depth)


def pack_call(starts, pos, depth):
    rows = pos.shape[1]
    peers = starts.shape[0] - 1
    stride = rows + depth + 8
    stride += -stride % 8
    return launch(
        functools.partial(pack_kernel, rows=rows, depth=depth, stride=stride),
        out_shape=jax.ShapeDtypeStruct((peers, 6 * depth, 128), jnp.float32),
        in_specs=[SMEM_SPEC, VMEM_SPEC],
        out_specs=VMEM_SPEC,
        scratch_shapes=[pltpu.VMEM((6 * stride, 128), jnp.float32)],
        compiler_params=pltpu.CompilerParams(vmem_limit_bytes=32 * 1024 * 1024),
        name="pack",
    )(starts, pos)


def list_count(depth):
    return 8 if depth % 8 == 0 else 1


def nodes_kernel(slots_ref, perm_ref, node_ref, *list_refs, depth, spare):
    tile = list_count(depth)
    parts = depth // tile

    @pl.loop(0, slots_ref.shape[0])
    def _(t):
        rows = [jnp.broadcast_to(perm_ref[t, w : w + 1, :], (8, 128)) for w in range(depth)]
        for r in range(parts):
            slot = jnp.broadcast_to(slots_ref[t, r * tile : (r + 1) * tile, :], (8, 128))
            place = slot & 127
            which = slot >> 7
            node = jnp.full((8, 128), spare, jnp.int32)
            for w in range(depth):
                node = jnp.where(which == w, jnp.take_along_axis(rows[w], place, axis=1), node)
            packed = ((node >> 12) << 7) | (node & 127)
            node_ref[t, r * tile : (r + 1) * tile, :] = node[:tile]
            for u in range(tile):
                list_refs[u][pl.ds(t * parts + r, 1), :] = node[u : u + 1]
                list_refs[tile + u][pl.ds(t * parts + r, 1), :] = packed[u : u + 1]


def nodes_call(slots, perm, spare):
    peers, depth, _ = slots.shape
    lists = list_count(depth)
    one = jax.ShapeDtypeStruct((peers * depth // lists, 128), jnp.int32)
    found = launch(
        functools.partial(nodes_kernel, depth=depth, spare=spare),
        out_shape=(jax.ShapeDtypeStruct(slots.shape, jnp.int32),) + (one,) * (2 * lists),
        in_specs=[MOVED_SPEC, VMEM_SPEC],
        out_specs=(VMEM_SPEC,) * (1 + 2 * lists),
        compiler_params=pltpu.CompilerParams(vmem_limit_bytes=32 * 1024 * 1024),
        name="nodes",
    )(slots, perm)
    flat = [x.reshape(-1) for x in found[1:]]
    return found[0], flat[:lists], flat[lists:]


def move_rows(lists, count, t, depth, move):
    width = len(lists)
    parts = depth // width

    def part(p, carry):
        live = jnp.minimum(count - p * (width * 128), 128)
        base = (t * parts + p) * 128
        start = p * (width * 128)

        def some(i, carry):
            for k in range(SPAN):
                at = i * SPAN + k
                for u in range(width):
                    move(start + at + u * 128, lists[u][base + at])
            return carry

        return lax.fori_loop(0, lax.div(live + (SPAN - 1), jnp.int32(SPAN)), some, carry)

    whole = width * 128
    lax.fori_loop(0, lax.div(count + (whole - 1), jnp.int32(whole)), part, 0)


def fetching(lists, kept, arrived):
    copies = [pltpu.make_async_copy(a, b, arrived.at[k]) for k, (a, b) in enumerate(zip(lists, kept))]
    for copy in copies:
        copy.start()
    return copies


def list_scratch(lists):
    kept = [pltpu.SMEM(x.shape, jnp.int32) for x in lists]
    return kept + [pltpu.SemaphoreType.DMA((len(lists),))]


def scatter_kernel(counts, in_ref, *refs, depth, rp, lists):
    out_ref, cells_ref, table, rows_ref, *nodes, arrived = refs[lists:]
    copies = fetching(refs[:lists], nodes, arrived)

    @pl.loop(0, rp)
    def _(k):
        table[pl.ds(pl.multiple_of(k * 128, 128), 128), :] = jnp.zeros((128, 128), jnp.float32)

    for copy in copies:
        copy.wait()

    together = 4 if depth % 4 == 0 else 1

    @pl.loop(0, in_ref.shape[0])
    def _(t):
        def turn(i, carry):
            for j in range(together):
                r = i * together + j
                piece = in_ref[t, pl.ds(r, 6, stride=depth), :]
                piece = jnp.concatenate([piece, jnp.zeros((2, 128), jnp.float32)], axis=0)
                piece = jnp.concatenate([piece] * 16, axis=0)
                rows_ref[pl.ds(pl.multiple_of(r * 128, 128), 128), :] = jnp.transpose(piece)
            return carry

        def move(at, node):
            table[pl.ds(node, 1), :] = rows_ref[pl.ds(at, 1), :]

        count = counts[t]
        part = together * 128
        lax.fori_loop(0, lax.div(count + (part - 1), jnp.int32(part)), turn, 0)
        move_rows(nodes, count, t, depth, move)

    group = lane_index(8) >> 3

    @pl.loop(0, rp // 16)
    def _(g):
        tiles = []
        for i in range(16):
            tile = table[pl.ds(pl.multiple_of(g * 2048, 2048) + 8 * i, 8), :]
            for k in range(1, 16):
                one = table[pl.ds(pl.multiple_of(g * 2048, 2048) + k * 128 + 8 * i, 8), :]
                tile = jnp.where(group == k, one, tile)
            tiles.append(tile)
        at = pl.multiple_of(g * 128, 128)
        cells_ref[pl.ds(at, 128), :] = jnp.transpose(jnp.concatenate(tiles, axis=0))
        for c in range(6):
            out_ref[pl.ds(pl.multiple_of(c * rp + g * 16, 16), 16), :] = cells_ref[pl.ds(at + c, 16, stride=8), :]


def scatter_call(nodes, counts, data, rp, after=()):
    depth = data.shape[1] // 6
    return launch(
        ignoring(
            functools.partial(scatter_kernel, depth=depth, rp=rp, lists=len(nodes)), 2 + len(nodes), len(after)
        ),
        out_shape=(
            jax.ShapeDtypeStruct((6 * rp, 128), jnp.float32),
            jax.ShapeDtypeStruct((8 * rp, 128), jnp.float32),
        ),
        in_specs=[SMEM_SPEC, MOVED_SPEC] + [LIST_SPEC] * len(nodes) + [ANY_SPEC] * len(after),
        out_specs=(VMEM_SPEC,) * 2,
        scratch_shapes=[
            pltpu.VMEM((rp * 128 + 8, 128), jnp.float32),
            pltpu.VMEM((depth * 128, 128), jnp.float32),
        ]
        + list_scratch(nodes),
        compiler_params=pltpu.CompilerParams(vmem_limit_bytes=52 * 1024 * 1024),
        name="scatter",
    )(counts, data, *nodes, *after)


def gather_kernel(counts, node_ref, sums_ref, one_ref, two_ref, *refs, depth, rp, lists):
    out_ref, table, found, comb, *rows, arrived = refs[lists:]
    copies = fetching(refs[:lists], rows, arrived)
    comb[...] = jnp.zeros((128, 128), jnp.float32)

    @pl.loop(0, rp // 32)
    def _(g):
        for c in range(3):
            at = pl.ds(pl.multiple_of(c * rp + g * 32, 32), 32)
            comb[pl.ds(c, 32, stride=4), :] = one_ref[at, :] + two_ref[at, :]
        for i in range(16):
            pair = [sums_ref[pl.ds(pl.multiple_of((g * 32 + 2 * i + h) * 8, 8), 8), :] for h in range(2)]
            both = pair[0] + pltpu.roll(pair[1], 4, 0)
            comb[8 * i : 8 * i + 8, :] = comb[8 * i : 8 * i + 8, :] + both
        table[pl.ds(pl.multiple_of(g * 128, 128), 128), :] = jnp.transpose(comb[...])

    for copy in copies:
        copy.wait()
    together = 4 if depth % 4 == 0 else 1

    @pl.loop(0, out_ref.shape[0])
    def _(t):
        def move(at, row):
            found[pl.ds(at, 1), :] = table[pl.ds(row, 1), :]

        def turn(i, carry):
            for j in range(together):
                r = i * together + j
                turned = jnp.transpose(found[pl.ds(pl.multiple_of(r * 128, 128), 128), :])
                place = jnp.broadcast_to(node_ref[t, pl.ds(r, 1), :], (8, 128)) >> 7
                half = (place >> 1) & 15
                value = turned[:8]
                for h in range(1, 16):
                    value = jnp.where(half == h, turned[8 * h : 8 * h + 8], value)
                value = jnp.where((place & 1) == 1, pltpu.roll(value, 4, 0), value)
                out_ref[t, pl.ds(r, 3, stride=depth), :] = value[:3]
            return carry

        count = counts[t]
        part = together * 128
        move_rows(rows, count, t, depth, move)
        lax.fori_loop(0, lax.div(count + (part - 1), jnp.int32(part)), turn, 0)


def gather_call(rows, counts, nodes, sums, one, two):
    rp = one.shape[0] // 3
    peers, depth, _ = nodes.shape
    return launch(
        functools.partial(gather_kernel, depth=depth, rp=rp, lists=len(rows)),
        out_shape=jax.ShapeDtypeStruct((peers, 3 * depth, 128), jnp.float32),
        in_specs=[SMEM_SPEC] + [VMEM_SPEC] * 4 + [LIST_SPEC] * len(rows),
        out_specs=VMEM_SPEC,
        scratch_shapes=[
            pltpu.VMEM((rp * 4 + 8, 128), jnp.float32),
            pltpu.VMEM((depth * 128, 128), jnp.float32),
            pltpu.VMEM((128, 128), jnp.float32),
        ]
        + list_scratch(rows),
        compiler_params=pltpu.CompilerParams(vmem_limit_bytes=32 * 1024 * 1024),
        name="gather",
    )(counts, nodes, sums, one, two, *rows)


def finish_kernel(starts, in_ref, pos_ref, noise_ref, moved_ref, drift_ref, table, *, rows, depth, stride):
    lane = lane_index(depth)
    first = lane_index(1)

    @pl.loop(0, in_ref.shape[0])
    def _(t):
        at = starts[t]
        row = lax.shift_right_logical(at, 7)
        lead = at & 127
        for c in range(3):
            value = pltpu.roll(in_ref[t, c * depth : (c + 1) * depth, :], lead, 1)
            here = pl.ds(c * stride + row, depth)
            behind = pl.ds(c * stride + row + 1, depth)
            edge = table[pl.ds(c * stride + row, 1), :]
            table[behind, :] = value
            if depth > 1:
                body = jnp.where(lane[1:] < lead, value[:-1], value[1:])
                table[pl.ds(c * stride + row + 1, depth - 1), :] = body
            table[pl.ds(c * stride + row, 1), :] = jnp.where(first < lead, edge, value[:1])

    step = 8

    @pl.loop(0, rows // step)
    def _(i):
        at = pl.multiple_of(i * step, step)
        for c in range(3):
            drift = time_step * table[pl.ds(c * stride + at, step), :]
            drift_ref[c, pl.ds(at, step), :] = drift
            moved_ref[c, pl.ds(at, step), :] = pos_ref[c, pl.ds(at, step), :] + drift + noise_ref[c, pl.ds(at, step), :]


def finish_call(starts, data, pos, noise):
    rows = pos.shape[1]
    depth = data.shape[1] // 3
    stride = rows + depth + 8
    stride += -stride % 8
    return launch(
        functools.partial(finish_kernel, rows=rows, depth=depth, stride=stride),
        out_shape=(jax.ShapeDtypeStruct(pos.shape, jnp.float32),) * 2,
        in_specs=[SMEM_SPEC, MOVED_SPEC] + [VMEM_SPEC] * 2,
        out_specs=(VMEM_SPEC,) * 2,
        scratch_shapes=[pltpu.VMEM((3 * stride, 128), jnp.float32)],
        compiler_params=pltpu.CompilerParams(vmem_limit_bytes=32 * 1024 * 1024),
        name="finish",
    )(starts, data, pos, noise)


ERFCX_COEF = (0.06548172872398669,
    -0.3609186250151195,
    0.6338942267842493,
    -0.3384301108125971,
    0.4003704641202259,
    0.13581047899030682,
    0.2395463173952274,
    0.22417089752024144,
    7.010614160106155e-05)


def pair_math(square, coef):
    inverse = lax.rsqrt(square)
    ratio = pl.reciprocal(1.0 + 0.2 * (square * inverse))
    scaled = coef[0] * ratio + coef[1]
    for k in coef[2:]:
        scaled = scaled * ratio + k
    decay = jnp.exp(-0.25 * square)
    inverse_sq = inverse * inverse
    screen = scaled * inverse
    along = decay * (screen * (0.375 + 0.0625 * inverse_sq) + 0.125)
    across = (decay * inverse_sq) * (screen * (0.375 - 0.1875 * inverse_sq) - 0.125)
    return along, across

def order_kernel(first, second, count, own_ref, far_ref, totals, *, blocks):
    def step(p, sizes):
        own, far = sizes
        other = second[p]
        within = other < blocks
        both = first[p] * 65536 + other
        own_ref[own] = both
        far_ref[far] = both - blocks
        inside = within.astype(jnp.int32)
        return own + inside, far + 1 - inside

    own, far = lax.fori_loop(0, count[0], step, (jnp.int32(0), jnp.int32(0)))
    steps = first.shape[0]
    totals[0] = 0
    for n, part in enumerate(PARTS):
        totals[n + 1] = jnp.minimum(own, steps * part // 128)
    totals[len(PARTS) + 1] = own
    totals[len(PARTS) + 2] = 0
    totals[len(PARTS) + 3] = far


def order_call(first, second, count, blocks):
    size = first.shape[0] + 8
    return launch(
        functools.partial(order_kernel, blocks=blocks),
        out_shape=(jax.ShapeDtypeStruct((size,), jnp.int32),) * 2 + (jax.ShapeDtypeStruct((len(PARTS) + 4,), jnp.int32),),
        in_specs=[SMEM_SPEC] * 3,
        out_specs=(SMEM_SPEC,) * 3,
        compiler_params=pltpu.CompilerParams(vmem_limit_bytes=32 * 1024 * 1024),
        name="order",
    )(first, second, count)


def fill_cells(src_ref, cells, rp):
    @pl.loop(0, rp // 8)
    def _(i):
        at = pl.multiple_of(i * 8, 8)
        for c in range(6):
            cells[pl.ds(at * 8 + c, 8, stride=8), :] = src_ref[pl.ds(pl.multiple_of(c * rp + at, 8), 8), :]


def pair_kernel(pairs, bounds, cells_ref, *refs, rp, coef, unroll, beyond, part, fresh):
    if not fresh:
        near_in, *refs = refs
    if beyond:
        other_ref, near_ref, token, far_ref, other_cells, far_sums = refs
        fill_cells(other_ref, other_cells, rp)
        far_sums[...] = jnp.zeros(far_sums.shape, jnp.float32)
    else:
        near_ref, token = refs
        other_cells, far_sums = cells_ref, near_ref
    lane = lax.broadcasted_iota(jnp.int32, (8, 128), 1)
    sub = lax.broadcasted_iota(jnp.int32, (8, 128), 0)
    left = lane < 64
    unturn = (lane + sub) & 127
    near_ref[...] = jnp.zeros(near_ref.shape, jnp.float32) if fresh else near_in[...]
    token[...] = jnp.zeros((8, 128), jnp.float32)

    def row(k):
        return pl.ds(pl.multiple_of((k >> 1) * 8, 8), 8)

    def both_halves(table, k):
        cell = table[row(k), :]
        return jnp.where(left == ((k & 1) == 0), cell, pltpu.roll(cell, 64, 1))

    def stacked(parts):
        out = jnp.zeros((8, 128), jnp.float32)
        for c, part in enumerate(parts):
            out = jnp.where(sub == c, jnp.sum(part, axis=0, keepdims=True), out)
        return out

    def one(ka, kb):
        near = both_halves(cells_ref, ka)
        near = jnp.where(left, near, pltpu.roll(near, 96, 1))
        far = both_halves(other_cells, kb)
        mine = [jnp.broadcast_to(near[c : c + 1, :], (8, 128)) for c in range(6)]
        other = [jnp.broadcast_to(far[c : c + 1, :], (8, 128)) for c in range(6)]
        near_sum = None
        far_sum = None
        for q in (3, 2, 1, 0):
            turned = [pltpu.roll(x, 8 * q, 1, stride=1, stride_axis=0) for x in other]
            gap = [mine[c] - turned[c] for c in range(3)]
            along, across = pair_math(gap[0] * gap[0] + gap[1] * gap[1] + gap[2] * gap[2] + 0.25, coef)
            to_near = across * (gap[0] * turned[3] + gap[1] * turned[4] + gap[2] * turned[5])
            to_far = across * (gap[0] * mine[3] + gap[1] * mine[4] + gap[2] * mine[5])
            near_add = [along * turned[3 + c] + to_near * gap[c] for c in range(3)]
            far_add = [along * mine[3 + c] + to_far * gap[c] for c in range(3)]
            if near_sum is None:
                near_sum, far_sum = near_add, far_add
            else:
                near_sum = [a + b for a, b in zip(near_sum, near_add)]
                far_sum = [pltpu.roll(a, 120, 1) + b for a, b in zip(far_sum, far_add)]
        far_sum = [jnp.take_along_axis(a, unturn, axis=1) for a in far_sum]
        near_vel = stacked(near_sum)
        half = jnp.where(left, pltpu.roll(near_vel, 64, 1), 0.0)
        near_vel = jnp.where(left, near_vel, 0.0) + pltpu.roll(half, 32, 1)
        near_vel = near_vel + pltpu.roll(near_vel, 64, 1)
        far_vel = stacked(far_sum)
        far_vel = far_vel + pltpu.roll(far_vel, 64, 1)
        return near_vel, far_vel

    low = bounds[part]
    high = bounds[part + 1]

    def turn(i, carry):
        found = []
        for k in range(unroll):
            p = low + i * unroll + k
            alive = p < high
            both = jnp.where(alive, pairs[p], 0)
            ka, kb = both >> 16, both & 65535
            found.append((alive, ka, kb, one(ka, kb)))
        for alive, ka, kb, (near_vel, far_vel) in found:
            near_ref[row(ka), :] += jnp.where((left == ((ka & 1) == 0)) & alive, near_vel, 0.0)
            if not beyond:
                alive = alive & (ka != kb)
            far_sums[row(kb), :] += jnp.where((left == ((kb & 1) == 0)) & alive, far_vel, 0.0)
        return carry

    lax.fori_loop(0, lax.div(jnp.maximum(high - low, 0) + (unroll - 1), jnp.int32(unroll)), turn, 0)

    if beyond:
        for c in range(3):
            @pl.loop(0, rp // 8)
            def _(i):
                at = pl.ds(pl.multiple_of(c * rp + i * 8, 8), 8)
                far_ref[at, :] = far_sums[pl.ds(i * 64 + c, 8, stride=8), :]


def pair_call(pairs, bounds, part, cells, near=None, beside=None, after=(), coef=ERFCX_COEF, unroll=8):
    rp = cells.shape[0] // 8
    beyond = beside is not None
    fresh = near is None
    extra = [cells] + ([] if fresh else [near]) + ([beside] if beyond else [])
    out = [jax.ShapeDtypeStruct((8 * rp, 128), jnp.float32), jax.ShapeDtypeStruct((8, 128), jnp.float32)]
    scratch = []
    if beyond:
        out.append(jax.ShapeDtypeStruct((3 * rp, 128), jnp.float32))
        scratch = [pltpu.VMEM((8 * rp, 128), jnp.float32)] * 2
    return launch(
        ignoring(
            functools.partial(
                pair_kernel, rp=rp, coef=coef, unroll=unroll, beyond=beyond, part=part, fresh=fresh
            ),
            2 + len(extra),
            len(after),
        ),
        out_shape=tuple(out),
        in_specs=[SMEM_SPEC] * 2 + [VMEM_SPEC] * (len(extra) - beyond) + [MOVED_SPEC] * beyond + [ANY_SPEC] * len(after),
        out_specs=(VMEM_SPEC,) * len(out),
        scratch_shapes=scratch,
        compiler_params=pltpu.CompilerParams(vmem_limit_bytes=32 * 1024 * 1024),
        name="beyond" if beyond else "within",
    )(pairs, bounds, *extra, *after)


def signed_wave(grid_index):
    return jnp.where(grid_index < G // 2, grid_index, grid_index - G).astype(jnp.float32) * (
        2.0 * math.pi / (G * grid_spacing)
    )


def forward_pass(real_in, imag_in, form, cos_part, sin_part):
    contract = partial(jnp.einsum, precision=lax.Precision.HIGHEST)
    real_out = contract(form, real_in, cos_part) + contract(form, imag_in, sin_part)
    imag_out = contract(form, imag_in, cos_part) - contract(form, real_in, sin_part)
    return (real_out, imag_out)


def inverse_pass(real_in, imag_in, form, cos_part, sin_part):
    contract = partial(jnp.einsum, precision=lax.Precision.HIGHEST)
    real_out = contract(form, real_in, cos_part) - contract(form, imag_in, sin_part)
    imag_out = contract(form, imag_in, cos_part) + contract(form, real_in, sin_part)
    return (real_out, imag_out)


def project_flow(spectrum, wave_x, wave_y, wave_z):
    wave_sq = wave_x * wave_x + wave_y * wave_y + wave_z * wave_z
    wave_safe = jnp.where(wave_sq > 0, wave_sq, 1.0)
    spread_sq = wave_sq / (4.0 * split_xi**2)
    green_fn = jnp.where(
        wave_sq > 0,
        (1.0 - bead_radius**2 * wave_sq / 3.0)
        * (1.0 + spread_sq)
        * jnp.exp(-spread_sq)
        / wave_safe,
        0.0,
    )
    along_wave = (wave_x * spectrum[0] + wave_y * spectrum[1] + wave_z * spectrum[2]) / wave_safe
    return jnp.stack(
        [
            green_fn * (spectrum[0] - wave_x * along_wave),
            green_fn * (spectrum[1] - wave_y * along_wave),
            green_fn * (spectrum[2] - wave_z * along_wave),
        ]
    )


def kspace_part(force_rows, n_gx, n_gy):
    local_x = G // n_gx
    local_y = G // n_gy
    grid_index = jnp.arange(G, dtype=jnp.int32)
    phase_grid = (grid_index[:, None] * grid_index[None, :] % G).astype(jnp.float32) * (
        2.0 * math.pi / G
    )
    cosine_table = jnp.cos(phase_grid)
    sine_table = jnp.sin(phase_grid)
    contract = partial(jnp.einsum, precision=lax.Precision.HIGHEST)
    force_field = force_rows.reshape(3, local_x, local_y, G)
    wave_full = signed_wave(grid_index)
    row_gx = lax.axis_index("gx")
    row_gy = lax.axis_index("gy")
    freq_count = G
    spec_z = jnp.stack(
        [
            contract("cabz,zk->cabk", force_field, cosine_table),
            -contract("cabz,zk->cabk", force_field, sine_table),
        ]
    )
    cos_x = cosine_table.reshape(n_gx, local_x, G)
    sin_x = sine_table.reshape(n_gx, local_x, G)
    cos_y = cosine_table.reshape(n_gy, local_y, G)
    sin_y = sine_table.reshape(n_gy, local_y, G)
    depth_part = freq_count // n_gx
    width_part = G // n_gy
    slabs = lax.all_to_all(spec_z[:, :, None], "gx", split_axis=5, concat_axis=2, tiled=True)
    xr_part, xi_part = forward_pass(slabs[0], slabs[1], "ciabl,iak->cbkl", cos_x, sin_x)
    pencils = lax.all_to_all(
        jnp.stack([xr_part, xi_part])[:, :, None], "gy", split_axis=4, concat_axis=2, tiled=True
    )
    yr_part, yi_part = forward_pass(pencils[0], pencils[1], "cjbkl,jbm->ckml", cos_y, sin_y)
    wave_x = signed_wave(row_gy * width_part + jnp.arange(width_part, dtype=jnp.int32))[
        :, None, None
    ]
    wave_y = wave_full[None, :, None]
    wave_z = signed_wave(row_gx * depth_part + jnp.arange(depth_part, dtype=jnp.int32))[
        None, None, :
    ]
    flow_real = project_flow(yr_part, wave_x, wave_y, wave_z)
    flow_imag = project_flow(yi_part, wave_x, wave_y, wave_z)
    br_part, bi_part = inverse_pass(flow_real, flow_imag, "ckml,jbm->cjbkl", cos_y, sin_y)
    back = lax.all_to_all(
        jnp.stack([br_part, bi_part]), "gy", split_axis=2, concat_axis=4, tiled=True
    )[:, :, 0]
    ar_part, ai_part = inverse_pass(back[0], back[1], "cbkl,iak->ciabl", cos_x, sin_x)
    gathered = lax.all_to_all(
        jnp.stack([ar_part, ai_part]), "gx", split_axis=2, concat_axis=5, tiled=True
    )[:, :, 0]
    result = contract("cabk,zk->cabz", gathered[0], cosine_table) - contract(
        "cabk,zk->cabz", gathered[1], sine_table
    )
    return (result / float(G**3)).reshape(3, local_x * local_y * G)


matmul = functools.partial(lax.dot_general, precision=lax.Precision.HIGHEST, preferred_element_type=jnp.float32)
PLAIN = (((1,), (0,)), ((), ()))
TURNED = (((1,), (1,)), ((), ()))


def wave_tables(n_gx, n_gy):
    share = G // 2 // n_gx
    width = G // n_gy
    grid = np.arange(G)
    turn = 2.0 * math.pi * (np.outer(grid, grid) % G) / G
    cos, sin = np.cos(turn), np.sin(turn)
    half = width // 2
    order = np.zeros(G, np.int64)
    for j in range(n_gy):
        for p in range(half):
            k = j * half + p
            order[j * width + p] = k
            order[j * width + half + p] = (G - k) % G if k else G // 2
    ahead = np.zeros((G, n_gx, 2, share))
    ahead[:, :, 0] = cos[:, : G // 2].reshape(G, n_gx, share)
    ahead[:, :, 1] = -sin[:, : G // 2].reshape(G, n_gx, share)
    back = 2.0 * ahead
    ahead[:, 0, 1, 0] = cos[:, G // 2]
    back[:, 0, 0, 0] = 1.0
    back[:, 0, 1, 0] = cos[:, G // 2]
    unit = 2.0 * math.pi / (G * grid_spacing)
    signed = np.where(grid < G // 2, grid, grid - G) * unit
    plain = np.where(grid == G // 2, 0.0, signed)
    edge = signed - plain
    lane = np.arange(128)
    across = np.zeros((n_gy, 8, 128))
    across[:, 0] = plain[order].reshape(n_gy, 1, width)[:, 0][:, lane % width]
    across[:, 1] = edge[order].reshape(n_gy, 1, width)[:, 0][:, lane % width]
    across[0, 2] = lane % half == 0
    deep = np.zeros((n_gx, 8, 128))
    per = 128 // width
    for v in range(share // per):
        deep[:, v] = (np.arange(n_gx)[:, None] * share + v * per + lane // width) * unit
    down = np.stack([np.broadcast_to(t[:, None], (G, 128)) for t in (plain, edge)])
    tables = {
        "ahead": ahead.reshape(G, G),
        "back": back.reshape(G, G).T,
        "first": np.concatenate([cos[:, order], sin[:, order]], axis=1),
        "first_back": np.concatenate([cos[:, order], sin[:, order]], axis=1),
        "second": np.concatenate([cos, sin], axis=0),
        "across": across,
        "deep": deep,
        "down": down,
    }
    return {name: np.asarray(table, np.float32) for name, table in tables.items()}


def spread(tiles, at, group, tall):
    count = 128 // group
    lane = lax.shift_right_logical(lax.broadcasted_iota(jnp.int32, (tall, 128), 1), group.bit_length() - 1)
    out = None
    for g, tile in enumerate(tiles):
        moved = pltpu.roll(tile, group * ((g - at) % count), 1) if g != at else tile
        out = moved if out is None else jnp.where(lane == g, moved, out)
    return out


def depth_kernel(field_ref, table_ref, out_ref, spec, *, n_gx, tall, wide):
    rows = tall * wide
    for c in range(3):
        spec[c * rows : (c + 1) * rows, :] = matmul(field_ref[c * rows : (c + 1) * rows, :], table_ref[...], PLAIN)
    group = G // n_gx
    count = n_gx

    @pl.loop(0, 3 * wide // count)
    def _(i):
        c = lax.div(i, jnp.int32(wide // count))
        b = (i - c * (wide // count)) * count
        tiles = [spec[pl.ds(c * rows + b + g, tall, stride=wide), :] for g in range(count)]
        for p in range(n_gx):
            out_ref[p, :, pl.ds(pl.multiple_of(i * 128, 128), 128)] = spread(tiles, p, group, tall)


def first_kernel(data_ref, table_ref, out_ref, turned, *, n_gy, share, wide):
    group = G // n_gy
    per = 128 // (2 * share)

    @pl.loop(0, 3 * wide // per)
    def _(i):
        c = lax.div(i, jnp.int32(wide // per))
        b = (i - c * (wide // per)) * per
        piece = jnp.transpose(data_ref[:, pl.ds(pl.multiple_of(i * 128, 128), 128)])
        both = matmul(piece, table_ref[...], PLAIN)
        for g in range(per):
            lo, mid, hi = g * 2 * share, (g * 2 + 1) * share, (g * 2 + 2) * share
            real = both[lo:mid, :128] + both[mid:hi, 128:]
            imag = both[mid:hi, :128] - both[lo:mid, 128:]
            turned[pl.ds(2 * c * share * wide + b + g, share, stride=wide), :] = real
            turned[pl.ds((2 * c + 1) * share * wide + b + g, share, stride=wide), :] = imag

    count = 128 // group

    @pl.loop(0, 6 * share // count)
    def _(i):
        at = i * (count * wide)
        tiles = [turned[pl.ds(pl.multiple_of(at + u * wide, 8), wide), :] for u in range(count)]
        for j in range(n_gy):
            out_ref[j, i] = spread(tiles, j, group, wide)


def second_kernel(ids, data_ref, table_ref, across_ref, deep_ref, down_ref, out_ref, flow, *, n_gy, views, wide):
    lane = lax.broadcasted_iota(jnp.int32, (G, 128), 1)
    width = G // n_gy
    half = width // 2
    across = across_ref[ids[1]]
    deep = deep_ref[ids[0]]
    alone = (lane < width) & (ids[0] == 0)
    mirror_self = across[2:3, :] > 0.5
    upper = (lane & half) != 0

    def whole(tile):
        return jnp.concatenate([data_ref[j, tile] for j in range(n_gy)], axis=0)

    def mirrored(value):
        other = jnp.where(upper, pltpu.roll(value, half, 1), pltpu.roll(value, 128 - half, 1))
        return jnp.where(mirror_self, value, other)

    def ahead(real, imag):
        one = matmul(table_ref[...], real, PLAIN)
        two = matmul(table_ref[...], imag, PLAIN)
        return one[:G] + two[G:], two[:G] - one[G:]

    def projected(spectrum, deep_plain, deep_edge):
        plain = (across[0:1, :], down_ref[0], deep_plain)
        edge = (across[1:2, :], down_ref[1], deep_edge)
        waves = [p + e for p, e in zip(plain, edge)]
        wave_sq = waves[0] * waves[0] + waves[1] * waves[1] + waves[2] * waves[2]
        live = wave_sq > 0
        inverse = 1.0 / jnp.where(live, wave_sq, 1.0)
        spread_sq = wave_sq / (4.0 * split_xi**2)
        green = (1.0 - bead_radius**2 * wave_sq / 3.0) * (1.0 + spread_sq) * jnp.exp(-spread_sq) * inverse
        green = jnp.where(live, green / float(G**3), 0.0)
        out = []
        for r in range(2):
            regular = sum(w * spectrum[c][r] for c, w in enumerate(plain)) * inverse
            nyquist = sum(w * spectrum[c][r] for c, w in enumerate(edge)) * inverse
            out.append([green * (spectrum[c][r] - plain[c] * regular - edge[c] * nyquist) for c in range(3)])
        return out

    zero = jnp.zeros((1, 128), jnp.float32)
    for v in range(views):
        spectrum = []
        apart = []
        for c in range(3):
            real = whole((2 * c) * views + v)
            imag = whole((2 * c + 1) * views + v)
            if v == 0:
                off_real = jnp.where(alone, 0.5 * (real - mirrored(real)), 0.0)
                off_imag = jnp.where(alone, 0.5 * (imag + mirrored(imag)), 0.0)
                apart.append(ahead(off_real, off_imag))
                real, imag = real - off_real, imag - off_imag
            spectrum.append(ahead(real, imag))
        found = projected(spectrum, deep[v : v + 1, :], zero)
        if v == 0:
            extra = projected(apart, zero, zero - math.pi / grid_spacing)
            found = [[a + b for a, b in zip(one, two)] for one, two in zip(found, extra)]
        for c in range(3):
            one = matmul(table_ref[...], found[0][c], PLAIN)
            two = matmul(table_ref[...], found[1][c], PLAIN)
            real, imag = one[:G] - two[G:], two[:G] + one[G:]
            for j in range(n_gy):
                out_ref[j, (2 * c) * views + v] = real[j * wide : (j + 1) * wide]
                out_ref[j, (2 * c + 1) * views + v] = imag[j * wide : (j + 1) * wide]


def first_back_kernel(data_ref, table_ref, out_ref, turned, *, n_gy, share, wide):
    group = G // n_gy
    count = n_gy
    per = 128 // (2 * share)

    @pl.loop(0, 6 * share // count)
    def _(i):
        tiles = [data_ref[j, i] for j in range(n_gy)]
        for u in range(count):
            turned[pl.ds(pl.multiple_of((i * count + u) * wide, 8), wide), :] = spread(tiles, u, group, wide)

    @pl.loop(0, 3 * wide // per)
    def _(i):
        c = lax.div(i, jnp.int32(wide // per))
        b = (i - c * (wide // per)) * per
        rows = []
        for g in range(per):
            real = turned[pl.ds(2 * c * share * wide + b + g, share, stride=wide), :]
            imag = turned[pl.ds((2 * c + 1) * share * wide + b + g, share, stride=wide), :]
            rows.append(jnp.concatenate([real, -imag], axis=1))
            rows.append(jnp.concatenate([imag, real], axis=1))
        piece = jnp.concatenate(rows, axis=0)
        out_ref[:, pl.ds(pl.multiple_of(i * 128, 128), 128)] = matmul(table_ref[...], piece, TURNED)


def depth_back_kernel(data_ref, table_ref, out_ref, spec, *, n_gx, tall, wide):
    rows = tall * wide
    group = G // n_gx
    count = n_gx

    @pl.loop(0, 3 * wide // count)
    def _(i):
        c = lax.div(i, jnp.int32(wide // count))
        b = (i - c * (wide // count)) * count
        tiles = [data_ref[p, :, pl.ds(pl.multiple_of(i * 128, 128), 128)] for p in range(n_gx)]
        for g in range(count):
            spec[pl.ds(c * rows + b + g, tall, stride=wide), :] = spread(tiles, g, group, tall)

    for c in range(3):
        out_ref[c * rows : (c + 1) * rows, :] = matmul(spec[c * rows : (c + 1) * rows, :], table_ref[...], PLAIN)


def waves(grid_data, n_gx, n_gy, fill):
    tall, wide, share = G // n_gx, G // n_gy, G // 2 // n_gx
    rows = 3 * tall * wide
    views = share * wide // 128
    tables = wave_tables(n_gx, n_gy)
    f32 = jnp.float32

    def run(name, kernel, shape, args, scratch, specs=None, after=(), **sizes):
        return launch(
            marking(ignoring(functools.partial(kernel, **sizes), len(args), len(after)), len(args) + len(after)),
            out_shape=(jax.ShapeDtypeStruct(shape, f32), jax.ShapeDtypeStruct((8, 128), f32)),
            in_specs=(specs or [MOVED_SPEC] + [VMEM_SPEC] * (len(args) - 1)) + [ANY_SPEC] * len(after),
            out_specs=(VMEM_SPEC,) * 2,
            scratch_shapes=[pltpu.VMEM(scratch, f32)],
            compiler_params=pltpu.CompilerParams(vmem_limit_bytes=32 * 1024 * 1024),
            name=name,
        )(*args, *after)

    def swap(value, axis):
        return lax.all_to_all(value, axis, split_axis=0, concat_axis=0, tiled=True)

    force = pl.BlockSpec((rows, 128), lambda i: (1, 0))
    lanes = 6 * wide * share
    ids = jnp.stack([lax.axis_index("gx"), lax.axis_index("gy")]).astype(jnp.int32)
    value, token = run("depth", depth_kernel, (n_gx, tall, lanes), (pltpu.with_memory_space_constraint(grid_data, pltpu.HBM), tables["ahead"]), (rows, 128),
                [force, VMEM_SPEC], n_gx=n_gx, tall=tall, wide=wide)
    after = fill(0, token)
    value = swap(value, "gx").reshape(G, lanes)
    value, token = run("first", first_kernel, (n_gy, 6 * views, wide, 128), (value, tables["first"]), (rows, 128),
                after=after, n_gy=n_gy, share=share, wide=wide)
    after = fill(1, token)
    value = swap(value.reshape(n_gy, 6 * views * wide, 128), "gy").reshape(n_gy, 6 * views, wide, 128)
    args = (ids, value, tables["second"], tables["across"], tables["deep"], tables["down"])
    value, token = run("second", second_kernel, (n_gy, 6 * views, wide, 128), args, (8, 128),
                [SMEM_SPEC, MOVED_SPEC] + [VMEM_SPEC] * 4, after, n_gy=n_gy, views=views, wide=wide)
    after = fill(2, token)
    value = swap(value.reshape(n_gy, 6 * views * wide, 128), "gy").reshape(n_gy, 6 * views, wide, 128)
    value, token = run("first_back", first_back_kernel, (G, lanes), (value, tables["first_back"]), (rows, 128),
                after=after, n_gy=n_gy, share=share, wide=wide)
    after = fill(3, token)
    value = swap(value.reshape(n_gx, tall, lanes), "gx")
    value, _ = run("depth_back", depth_back_kernel, (rows, 128), (value, tables["back"]), (rows, 128),
               after=after, n_gx=n_gx, tall=tall, wide=wide)
    return value


def shards(positions, noise, route, node_perm, pair_first, pair_second, pair_count):
    n_gx = lax.axis_size("gx")
    n_gy = lax.axis_size("gy")
    both = ("gx", "gy")
    peers = n_gx * n_gy
    slots = node_perm.shape[2]
    depth = slots // peers // 128
    rows = positions.shape[1] // 128
    rp = slots // 128
    swap = partial(lax.all_to_all, axis_name=both, split_axis=0, concat_axis=0, tiled=True)

    bounds = jnp.arange(peers + 1, dtype=jnp.int32) * (slots // peers)
    starts = jnp.sum(route[None, :] < bounds[:, None], axis=1, dtype=jnp.int32)
    taken = swap(slots_call(starts, route.reshape(rows, 128), depth))
    places = positions.reshape(3, rows, 128)
    data = swap(pack_call(starts, places, depth))
    counts = jnp.sum(taken >= 0, axis=(1, 2), dtype=jnp.int32)
    own_order = lax.dynamic_index_in_dim(node_perm, lax.axis_index("gx"), 0, False)
    nodes, node_lists, row_lists = nodes_call(taken, own_order.reshape(peers, depth, 128), slots)
    own_pairs, far_pairs, totals = order_call(pair_first[0], pair_second[0], pair_count, slots // CELL)
    grid_data, cells = scatter_call(node_lists, counts, data, rp, after=(totals,))

    state = {"sums": None}

    def within(n, after):
        state["sums"], token = pair_call(own_pairs, totals, n, cells, state["sums"], after=after)
        return token

    def fill(n, token):
        if n < 3:
            if n == 1:
                ready, _ = lax.optimization_barrier((grid_data, token))
                state["beside"] = shifted(ready, "gx", -1)
            return (within(n, (token,)),)
        state["sums"], _, far = pair_call(
            far_pairs, totals, len(PARTS) + 2, cells, state["sums"], state["beside"], after=(token,)
        )
        state["far"] = shifted(far, "gx", 1)
        return (within(3, ()),)

    share = G // 2 // n_gx
    if share % 8 == 0 and share * (G // n_gy) % 128 == 0:
        wave_vel = waves(grid_data, n_gx, n_gy, fill)
    else:
        wave_vel = kspace_part(grid_data[3 * rp :], n_gx, n_gy).reshape(3 * rp, 128)
        for n in range(4):
            fill(n, wave_vel)
    back = swap(gather_call(row_lists, counts, nodes, state["sums"], wave_vel, state["far"]))
    moved, drift = finish_call(starts, back, places, noise.reshape(3, rows, 128))
    return (moved.reshape(positions.shape), drift.reshape(positions.shape))


def solution(mesh):
    in_specs = (
        P(None, ("gx", "gy")),
        P(None, ("gx", "gy")),
        P(("gx", "gy")),
        P(None, "gy", None),
        P(("gx", "gy"), None),
        P(("gx", "gy"), None),
        P(("gx", "gy")),
    )
    out_specs = (P(None, ("gx", "gy")), P(None, ("gx", "gy")))
    return jax.shard_map(shards, mesh=mesh, in_specs=in_specs, out_specs=out_specs, check_vma=False)
```

```python
import functools
from functools import partial
import math

import jax
import jax.numpy as jnp
import numpy as np
from jax import lax
from jax.experimental import pallas as pl
from jax.experimental.pallas import tpu as pltpu
from jax.sharding import PartitionSpec as P

G = 128
BEAD_CH = 64
CELL = 64


bead_radius = 0.5
split_xi = 0.5
time_step = 0.01
fene_k = 30.0
fene_reach = 1.5
bend_k = 2.0
grid_spacing = 4.0
pair_block = 64


def shifted(value, axis, by):
    devices = lax.axis_size(axis)
    return lax.ppermute(value, axis, [(i, (i + by) % devices) for i in range(devices)])


SPAN = 32
PARTS = (25, 37, 52)

SMEM_SPEC = pl.BlockSpec(memory_space=pltpu.SMEM)
LIST_SPEC = pl.BlockSpec(memory_space=pltpu.SMEM)
VMEM_SPEC = pl.BlockSpec(memory_space=pltpu.VMEM)
MOVED_SPEC = pl.BlockSpec(memory_space=pltpu.VMEM)


ANY_SPEC = pl.BlockSpec(memory_space=pl.ANY)


def launch(kernel, *, out_shape, in_specs, out_specs, **options):
    def block(spec, value):
        shape = value.shape
        return pl.BlockSpec(shape, lambda i: (0,) * len(shape)) if spec is VMEM_SPEC or spec is MOVED_SPEC else spec

    def placed(spec, value):
        return spec is VMEM_SPEC or spec is LIST_SPEC or (spec is ANY_SPEC and value.dtype == jnp.float32)

    def run(*args):
        several = isinstance(out_shape, tuple)
        shapes = out_shape if several else (out_shape,)
        outs = out_specs if several else (out_specs,)
        found = tuple(block(s, v) for s, v in zip(outs, shapes))
        kept = tuple(pltpu.HBM(v.shape, v.dtype) if s is VMEM_SPEC else v for s, v in zip(outs, shapes))
        args = [
            pltpu.with_memory_space_constraint(jnp.asarray(v), pltpu.HBM) if placed(s, v) else v
            for s, v in zip(in_specs, args)
        ]
        return pl.pallas_call(
            kernel,
            out_shape=kept if several else kept[0],
            grid=(1,),
            in_specs=[block(s, v) for s, v in zip(in_specs, args)],
            out_specs=found if several else found[0],
            **options,
        )(*args)

    return run


def ignoring(kernel, inputs, extra):
    def run(*refs):
        kernel(*refs[:inputs], *refs[inputs + extra :])

    return run


def marking(kernel, inputs):
    def run(*refs):
        refs[inputs + 1][...] = jnp.zeros(refs[inputs + 1].shape, jnp.float32)
        kernel(*refs[: inputs + 1], *refs[inputs + 2 :])

    return run


def lane_index(rows):
    return lax.broadcasted_iota(jnp.int32, (rows, 128), 1)


def window(table, at, rows):
    row = lax.shift_right_logical(at, 7)
    lead = at & 127
    head = pltpu.roll(table[pl.ds(row, rows), :], (128 - lead) & 127, 1)
    tail = pltpu.roll(table[pl.ds(row + 1, rows), :], (128 - lead) & 127, 1)
    return jnp.where(lane_index(rows) < 128 - lead, head, tail)


def slots_kernel(starts, route_ref, out_ref, table, *, rows, depth):
    table[pl.ds(0, rows), :] = route_ref[...]
    table[pl.ds(rows, depth + 8), :] = jnp.zeros((depth + 8, 128), jnp.int32)
    place = lane_index(depth) + lax.broadcasted_iota(jnp.int32, (depth, 128), 0) * 128

    @pl.loop(0, out_ref.shape[0])
    def _(t):
        at = starts[t]
        slot = window(table, at, depth) - t * (depth * 128)
        out_ref[t] = jnp.where(place < starts[t + 1] - at, slot, -1)


def slots_call(starts, route, depth):
    rows = route.shape[0]
    peers = starts.shape[0] - 1
    return launch(
        functools.partial(slots_kernel, rows=rows, depth=depth),
        out_shape=jax.ShapeDtypeStruct((peers, depth, 128), jnp.int32),
        in_specs=[SMEM_SPEC, VMEM_SPEC],
        out_specs=VMEM_SPEC,
        scratch_shapes=[pltpu.VMEM((rows + depth + 8, 128), jnp.int32)],
        compiler_params=pltpu.CompilerParams(vmem_limit_bytes=32 * 1024 * 1024),
        name="slots",
    )(starts, route)


def chain_forces(pos):
    rows = pos[0].shape[0]
    place = lane_index(rows) & (BEAD_CH - 1)
    bonded = place < BEAD_CH - 1
    bent = place < BEAD_CH - 2
    after = (place > 0) & bonded
    bond = [jnp.where(bonded, pltpu.roll(x, 127, 1) - x, 0.5) for x in pos]
    square = bond[0] * bond[0] + bond[1] * bond[1] + bond[2] * bond[2]
    inverse = lax.rsqrt(square)
    unit = [b * inverse for b in bond]
    following = [pltpu.roll(u, 127, 1) for u in unit]
    previous = [pltpu.roll(u, 1, 1) for u in unit]
    cosine = sum(u * v for u, v in zip(unit, following))
    cosine_before = pltpu.roll(cosine, 1, 1)
    pull = fene_k / (1.0 - square / fene_reach**2)
    out = []
    for c in range(3):
        turn = jnp.where(bent, following[c] - cosine * unit[c], 0.0)
        turn = turn + jnp.where(after, previous[c] - cosine_before * unit[c], 0.0)
        slope = jnp.where(bonded, pull * bond[c] - bend_k * inverse * turn, 0.0)
        out.append(slope - pltpu.roll(slope, 1, 1))
    return out


def pack_kernel(starts, pos_ref, out_ref, table, *, rows, depth, stride):
    step = 32 if rows % 32 == 0 else 8

    @pl.loop(0, rows // step)
    def _(i):
        at = pl.multiple_of(i * step, step)
        pos = [pos_ref[c, pl.ds(at, step), :] for c in range(3)]
        for c, value in enumerate(pos + chain_forces(pos)):
            table[pl.ds(c * stride + at, step), :] = value

    for c in range(6):
        table[pl.ds(c * stride + rows, stride - rows), :] = jnp.zeros((stride - rows, 128), jnp.float32)

    @pl.loop(0, out_ref.shape[0])
    def _(t):
        at = starts[t]
        for c in range(6):
            out_ref[t, c * depth : (c + 1) * depth, :] = window(table, at + c * stride * 128, depth)


def pack_call(starts, pos, depth):
    rows = pos.shape[1]
    peers = starts.shape[0] - 1
    stride = rows + depth + 8
    stride += -stride % 8
    return launch(
        functools.partial(pack_kernel, rows=rows, depth=depth, stride=stride),
        out_shape=jax.ShapeDtypeStruct((peers, 6 * depth, 128), jnp.float32),
        in_specs=[SMEM_SPEC, VMEM_SPEC],
        out_specs=VMEM_SPEC,
        scratch_shapes=[pltpu.VMEM((6 * stride, 128), jnp.float32)],
        compiler_params=pltpu.CompilerParams(vmem_limit_bytes=32 * 1024 * 1024),
        name="pack",
    )(starts, pos)


def list_count(depth):
    return 8 if depth % 8 == 0 else 1


def nodes_kernel(slots_ref, perm_ref, node_ref, *list_refs, depth, spare):
    tile = list_count(depth)
    parts = depth // tile

    @pl.loop(0, slots_ref.shape[0])
    def _(t):
        rows = [jnp.broadcast_to(perm_ref[t, w : w + 1, :], (8, 128)) for w in range(depth)]
        for r in range(parts):
            slot = jnp.broadcast_to(slots_ref[t, r * tile : (r + 1) * tile, :], (8, 128))
            place = slot & 127
            which = slot >> 7
            node = jnp.full((8, 128), spare, jnp.int32)
            for w in range(depth):
                node = jnp.where(which == w, jnp.take_along_axis(rows[w], place, axis=1), node)
            packed = ((node >> 12) << 7) | (node & 127)
            node_ref[t, r * tile : (r + 1) * tile, :] = node[:tile]
            for u in range(tile):
                list_refs[u][pl.ds(t * parts + r, 1), :] = node[u : u + 1]
                list_refs[tile + u][pl.ds(t * parts + r, 1), :] = packed[u : u + 1]


def nodes_call(slots, perm, spare):
    peers, depth, _ = slots.shape
    lists = list_count(depth)
    one = jax.ShapeDtypeStruct((peers * depth // lists, 128), jnp.int32)
    found = launch(
        functools.partial(nodes_kernel, depth=depth, spare=spare),
        out_shape=(jax.ShapeDtypeStruct(slots.shape, jnp.int32),) + (one,) * (2 * lists),
        in_specs=[MOVED_SPEC, VMEM_SPEC],
        out_specs=(VMEM_SPEC,) * (1 + 2 * lists),
        compiler_params=pltpu.CompilerParams(vmem_limit_bytes=32 * 1024 * 1024),
        name="nodes",
    )(slots, perm)
    flat = [x.reshape(-1) for x in found[1:]]
    return found[0], flat[:lists], flat[lists:]


def move_rows(lists, count, t, depth, move):
    width = len(lists)
    parts = depth // width

    def part(p, carry):
        live = jnp.minimum(count - p * (width * 128), 128)
        base = (t * parts + p) * 128
        start = p * (width * 128)

        def some(i, carry):
            for k in range(SPAN):
                at = i * SPAN + k
                for u in range(width):
                    move(start + at + u * 128, lists[u][base + at])
            return carry

        return lax.fori_loop(0, lax.div(live + (SPAN - 1), jnp.int32(SPAN)), some, carry)

    whole = width * 128
    lax.fori_loop(0, lax.div(count + (whole - 1), jnp.int32(whole)), part, 0)


def scatter_kernel(counts, in_ref, *refs, depth, rp, lists):
    nodes = refs[:lists]
    out_ref, cells_ref, table, rows_ref = refs[lists:]

    @pl.loop(0, rp)
    def _(k):
        table[pl.ds(pl.multiple_of(k * 128, 128), 128), :] = jnp.zeros((128, 128), jnp.float32)

    together = 8 if depth % 8 == 0 else 1

    @pl.loop(0, in_ref.shape[0])
    def _(t):
        def turn(i, carry):
            for j in range(together):
                r = i * together + j
                piece = in_ref[t, pl.ds(r, 6, stride=depth), :]
                piece = jnp.concatenate([piece, jnp.zeros((2, 128), jnp.float32)], axis=0)
                piece = jnp.concatenate([piece] * 16, axis=0)
                rows_ref[pl.ds(pl.multiple_of(r * 128, 128), 128), :] = jnp.transpose(piece)
            return carry

        def move(at, node):
            table[pl.ds(node, 1), :] = rows_ref[pl.ds(at, 1), :]

        count = counts[t]
        part = together * 128
        lax.fori_loop(0, lax.div(count + (part - 1), jnp.int32(part)), turn, 0)
        move_rows(nodes, count, t, depth, move)

    group = lane_index(8) >> 3

    @pl.loop(0, rp // 16)
    def _(g):
        tiles = []
        for i in range(16):
            tile = table[pl.ds(pl.multiple_of(g * 2048, 2048) + 8 * i, 8), :]
            for k in range(1, 16):
                one = table[pl.ds(pl.multiple_of(g * 2048, 2048) + k * 128 + 8 * i, 8), :]
                tile = jnp.where(group == k, one, tile)
            tiles.append(tile)
        at = pl.multiple_of(g * 128, 128)
        cells_ref[pl.ds(at, 128), :] = jnp.transpose(jnp.concatenate(tiles, axis=0))
        for c in range(6):
            out_ref[pl.ds(pl.multiple_of(c * rp + g * 16, 16), 16), :] = cells_ref[pl.ds(at + c, 16, stride=8), :]


def scatter_call(nodes, counts, data, rp, after=()):
    depth = data.shape[1] // 6
    return launch(
        ignoring(
            functools.partial(scatter_kernel, depth=depth, rp=rp, lists=len(nodes)), 2 + len(nodes), len(after)
        ),
        out_shape=(
            jax.ShapeDtypeStruct((6 * rp, 128), jnp.float32),
            jax.ShapeDtypeStruct((8 * rp, 128), jnp.float32),
        ),
        in_specs=[SMEM_SPEC, MOVED_SPEC] + [LIST_SPEC] * len(nodes) + [ANY_SPEC] * len(after),
        out_specs=(VMEM_SPEC,) * 2,
        scratch_shapes=[
            pltpu.VMEM((rp * 128 + 8, 128), jnp.float32),
            pltpu.VMEM((depth * 128, 128), jnp.float32),
        ],
        compiler_params=pltpu.CompilerParams(vmem_limit_bytes=52 * 1024 * 1024),
        name="scatter",
    )(counts, data, *nodes, *after)


def gather_kernel(counts, node_ref, sums_ref, one_ref, two_ref, *refs, depth, rp, lists):
    rows = refs[:lists]
    out_ref, table, found, comb = refs[lists:]
    comb[...] = jnp.zeros((128, 128), jnp.float32)

    @pl.loop(0, rp // 32)
    def _(g):
        for c in range(3):
            at = pl.ds(pl.multiple_of(c * rp + g * 32, 32), 32)
            comb[pl.ds(c, 32, stride=4), :] = one_ref[at, :] + two_ref[at, :]
        for i in range(16):
            pair = [sums_ref[pl.ds(pl.multiple_of((g * 32 + 2 * i + h) * 8, 8), 8), :] for h in range(2)]
            both = pair[0] + pltpu.roll(pair[1], 4, 0)
            comb[8 * i : 8 * i + 8, :] = comb[8 * i : 8 * i + 8, :] + both
        table[pl.ds(pl.multiple_of(g * 128, 128), 128), :] = jnp.transpose(comb[...])

    together = 8 if depth % 8 == 0 else 1

    @pl.loop(0, out_ref.shape[0])
    def _(t):
        def move(at, row):
            found[pl.ds(at, 1), :] = table[pl.ds(row, 1), :]

        def turn(i, carry):
            for j in range(together):
                r = i * together + j
                turned = jnp.transpose(found[pl.ds(pl.multiple_of(r * 128, 128), 128), :])
                place = jnp.broadcast_to(node_ref[t, pl.ds(r, 1), :], (8, 128)) >> 7
                half = (place >> 1) & 15
                value = turned[:8]
                for h in range(1, 16):
                    value = jnp.where(half == h, turned[8 * h : 8 * h + 8], value)
                value = jnp.where((place & 1) == 1, pltpu.roll(value, 4, 0), value)
                out_ref[t, pl.ds(r, 3, stride=depth), :] = value[:3]
            return carry

        count = counts[t]
        part = together * 128
        move_rows(rows, count, t, depth, move)
        lax.fori_loop(0, lax.div(count + (part - 1), jnp.int32(part)), turn, 0)


def gather_call(rows, counts, nodes, sums, one, two):
    rp = one.shape[0] // 3
    peers, depth, _ = nodes.shape
    return launch(
        functools.partial(gather_kernel, depth=depth, rp=rp, lists=len(rows)),
        out_shape=jax.ShapeDtypeStruct((peers, 3 * depth, 128), jnp.float32),
        in_specs=[SMEM_SPEC] + [VMEM_SPEC] * 4 + [LIST_SPEC] * len(rows),
        out_specs=VMEM_SPEC,
        scratch_shapes=[
            pltpu.VMEM((rp * 4 + 8, 128), jnp.float32),
            pltpu.VMEM((depth * 128, 128), jnp.float32),
            pltpu.VMEM((128, 128), jnp.float32),
        ],
        compiler_params=pltpu.CompilerParams(vmem_limit_bytes=32 * 1024 * 1024),
        name="gather",
    )(counts, nodes, sums, one, two, *rows)


def finish_kernel(starts, in_ref, pos_ref, noise_ref, moved_ref, drift_ref, table, *, rows, depth, stride):
    lane = lane_index(depth)
    first = lane_index(1)

    @pl.loop(0, in_ref.shape[0])
    def _(t):
        at = starts[t]
        row = lax.shift_right_logical(at, 7)
        lead = at & 127
        for c in range(3):
            value = pltpu.roll(in_ref[t, c * depth : (c + 1) * depth, :], lead, 1)
            here = pl.ds(c * stride + row, depth)
            behind = pl.ds(c * stride + row + 1, depth)
            edge = table[pl.ds(c * stride + row, 1), :]
            table[behind, :] = value
            if depth > 1:
                body = jnp.where(lane[1:] < lead, value[:-1], value[1:])
                table[pl.ds(c * stride + row + 1, depth - 1), :] = body
            table[pl.ds(c * stride + row, 1), :] = jnp.where(first < lead, edge, value[:1])

    step = 8

    @pl.loop(0, rows // step)
    def _(i):
        at = pl.multiple_of(i * step, step)
        for c in range(3):
            drift = time_step * table[pl.ds(c * stride + at, step), :]
            drift_ref[c, pl.ds(at, step), :] = drift
            moved_ref[c, pl.ds(at, step), :] = pos_ref[c, pl.ds(at, step), :] + drift + noise_ref[c, pl.ds(at, step), :]


def finish_call(starts, data, pos, noise):
    rows = pos.shape[1]
    depth = data.shape[1] // 3
    stride = rows + depth + 8
    stride += -stride % 8
    return launch(
        functools.partial(finish_kernel, rows=rows, depth=depth, stride=stride),
        out_shape=(jax.ShapeDtypeStruct(pos.shape, jnp.float32),) * 2,
        in_specs=[SMEM_SPEC, MOVED_SPEC] + [VMEM_SPEC] * 2,
        out_specs=(VMEM_SPEC,) * 2,
        scratch_shapes=[pltpu.VMEM((3 * stride, 128), jnp.float32)],
        compiler_params=pltpu.CompilerParams(vmem_limit_bytes=32 * 1024 * 1024),
        name="finish",
    )(starts, data, pos, noise)


ERFCX_COEF = (0.06548172872398669,
    -0.3609186250151195,
    0.6338942267842493,
    -0.3384301108125971,
    0.4003704641202259,
    0.13581047899030682,
    0.2395463173952274,
    0.22417089752024144,
    7.010614160106155e-05)


def pair_math(square, coef):
    inverse = lax.rsqrt(square)
    ratio = pl.reciprocal(1.0 + 0.2 * (square * inverse))
    scaled = coef[0] * ratio + coef[1]
    for k in coef[2:]:
        scaled = scaled * ratio + k
    decay = jnp.exp(-0.25 * square)
    inverse_sq = inverse * inverse
    screen = scaled * inverse
    along = decay * (screen * (0.375 + 0.0625 * inverse_sq) + 0.125)
    across = (decay * inverse_sq) * (screen * (0.375 - 0.1875 * inverse_sq) - 0.125)
    return along, across

def order_kernel(first, second, count, own_ref, far_ref, totals, *, blocks):
    def step(p, sizes):
        own, far = sizes
        other = second[p]
        within = other < blocks
        both = first[p] * 65536 + other
        own_ref[own] = both
        far_ref[far] = both - blocks
        inside = within.astype(jnp.int32)
        return own + inside, far + 1 - inside

    own, far = lax.fori_loop(0, count[0], step, (jnp.int32(0), jnp.int32(0)))
    steps = first.shape[0]
    totals[0] = 0
    for n, part in enumerate(PARTS):
        totals[n + 1] = jnp.minimum(own, steps * part // 128)
    totals[len(PARTS) + 1] = own
    totals[len(PARTS) + 2] = 0
    totals[len(PARTS) + 3] = far


def order_call(first, second, count, blocks):
    size = first.shape[0] + 8
    return launch(
        functools.partial(order_kernel, blocks=blocks),
        out_shape=(jax.ShapeDtypeStruct((size,), jnp.int32),) * 2 + (jax.ShapeDtypeStruct((len(PARTS) + 4,), jnp.int32),),
        in_specs=[SMEM_SPEC] * 3,
        out_specs=(SMEM_SPEC,) * 3,
        compiler_params=pltpu.CompilerParams(vmem_limit_bytes=32 * 1024 * 1024),
        name="order",
    )(first, second, count)


def fill_cells(src_ref, cells, rp):
    @pl.loop(0, rp // 8)
    def _(i):
        at = pl.multiple_of(i * 8, 8)
        for c in range(6):
            cells[pl.ds(at * 8 + c, 8, stride=8), :] = src_ref[pl.ds(pl.multiple_of(c * rp + at, 8), 8), :]


def pair_kernel(pairs, bounds, cells_ref, *refs, rp, coef, unroll, beyond, part, fresh):
    if not fresh:
        near_in, *refs = refs
    if beyond:
        other_ref, near_ref, token, far_ref, other_cells, far_sums = refs
        fill_cells(other_ref, other_cells, rp)
        far_sums[...] = jnp.zeros(far_sums.shape, jnp.float32)
    else:
        near_ref, token = refs
        other_cells, far_sums = cells_ref, near_ref
    lane = lax.broadcasted_iota(jnp.int32, (8, 128), 1)
    sub = lax.broadcasted_iota(jnp.int32, (8, 128), 0)
    left = lane < 64
    unturn = (lane + sub) & 127
    near_ref[...] = jnp.zeros(near_ref.shape, jnp.float32) if fresh else near_in[...]
    token[...] = jnp.zeros((8, 128), jnp.float32)

    def row(k):
        return pl.ds(pl.multiple_of((k >> 1) * 8, 8), 8)

    def both_halves(table, k):
        cell = table[row(k), :]
        return jnp.where(left == ((k & 1) == 0), cell, pltpu.roll(cell, 64, 1))

    def stacked(parts):
        out = jnp.zeros((8, 128), jnp.float32)
        for c, part in enumerate(parts):
            out = jnp.where(sub == c, jnp.sum(part, axis=0, keepdims=True), out)
        return out

    def one(ka, kb):
        near = both_halves(cells_ref, ka)
        near = jnp.where(left, near, pltpu.roll(near, 96, 1))
        far = both_halves(other_cells, kb)
        mine = [jnp.broadcast_to(near[c : c + 1, :], (8, 128)) for c in range(6)]
        other = [jnp.broadcast_to(far[c : c + 1, :], (8, 128)) for c in range(6)]
        near_sum = None
        far_sum = None
        for q in (3, 2, 1, 0):
            turned = [pltpu.roll(x, 8 * q, 1, stride=1, stride_axis=0) for x in other]
            gap = [mine[c] - turned[c] for c in range(3)]
            along, across = pair_math(gap[0] * gap[0] + gap[1] * gap[1] + gap[2] * gap[2] + 0.25, coef)
            to_near = across * (gap[0] * turned[3] + gap[1] * turned[4] + gap[2] * turned[5])
            to_far = across * (gap[0] * mine[3] + gap[1] * mine[4] + gap[2] * mine[5])
            near_add = [along * turned[3 + c] + to_near * gap[c] for c in range(3)]
            far_add = [along * mine[3 + c] + to_far * gap[c] for c in range(3)]
            if near_sum is None:
                near_sum, far_sum = near_add, far_add
            else:
                near_sum = [a + b for a, b in zip(near_sum, near_add)]
                far_sum = [pltpu.roll(a, 120, 1) + b for a, b in zip(far_sum, far_add)]
        far_sum = [jnp.take_along_axis(a, unturn, axis=1) for a in far_sum]
        near_vel = stacked(near_sum)
        half = jnp.where(left, pltpu.roll(near_vel, 64, 1), 0.0)
        near_vel = jnp.where(left, near_vel, 0.0) + pltpu.roll(half, 32, 1)
        near_vel = near_vel + pltpu.roll(near_vel, 64, 1)
        far_vel = stacked(far_sum)
        far_vel = far_vel + pltpu.roll(far_vel, 64, 1)
        return near_vel, far_vel

    low = bounds[part]
    high = bounds[part + 1]

    def turn(i, carry):
        found = []
        for k in range(unroll):
            p = low + i * unroll + k
            alive = p < high
            both = jnp.where(alive, pairs[p], 0)
            ka, kb = both >> 16, both & 65535
            found.append((alive, ka, kb, one(ka, kb)))
        for alive, ka, kb, (near_vel, far_vel) in found:
            near_ref[row(ka), :] += jnp.where((left == ((ka & 1) == 0)) & alive, near_vel, 0.0)
            if not beyond:
                alive = alive & (ka != kb)
            far_sums[row(kb), :] += jnp.where((left == ((kb & 1) == 0)) & alive, far_vel, 0.0)
        return carry

    lax.fori_loop(0, lax.div(jnp.maximum(high - low, 0) + (unroll - 1), jnp.int32(unroll)), turn, 0)

    if beyond:
        for c in range(3):
            @pl.loop(0, rp // 8)
            def _(i):
                at = pl.ds(pl.multiple_of(c * rp + i * 8, 8), 8)
                far_ref[at, :] = far_sums[pl.ds(i * 64 + c, 8, stride=8), :]


def pair_call(pairs, bounds, part, cells, near=None, beside=None, after=(), coef=ERFCX_COEF, unroll=8):
    rp = cells.shape[0] // 8
    beyond = beside is not None
    fresh = near is None
    extra = [cells] + ([] if fresh else [near]) + ([beside] if beyond else [])
    out = [jax.ShapeDtypeStruct((8 * rp, 128), jnp.float32), jax.ShapeDtypeStruct((8, 128), jnp.float32)]
    scratch = []
    if beyond:
        out.append(jax.ShapeDtypeStruct((3 * rp, 128), jnp.float32))
        scratch = [pltpu.VMEM((8 * rp, 128), jnp.float32)] * 2
    return launch(
        ignoring(
            functools.partial(
                pair_kernel, rp=rp, coef=coef, unroll=unroll, beyond=beyond, part=part, fresh=fresh
            ),
            2 + len(extra),
            len(after),
        ),
        out_shape=tuple(out),
        in_specs=[SMEM_SPEC] * 2 + [VMEM_SPEC] * (len(extra) - beyond) + [MOVED_SPEC] * beyond + [ANY_SPEC] * len(after),
        out_specs=(VMEM_SPEC,) * len(out),
        scratch_shapes=scratch,
        compiler_params=pltpu.CompilerParams(vmem_limit_bytes=32 * 1024 * 1024),
        name="beyond" if beyond else "within",
    )(pairs, bounds, *extra, *after)


def signed_wave(grid_index):
    return jnp.where(grid_index < G // 2, grid_index, grid_index - G).astype(jnp.float32) * (
        2.0 * math.pi / (G * grid_spacing)
    )


def forward_pass(real_in, imag_in, form, cos_part, sin_part):
    contract = partial(jnp.einsum, precision=lax.Precision.HIGHEST)
    real_out = contract(form, real_in, cos_part) + contract(form, imag_in, sin_part)
    imag_out = contract(form, imag_in, cos_part) - contract(form, real_in, sin_part)
    return (real_out, imag_out)


def inverse_pass(real_in, imag_in, form, cos_part, sin_part):
    contract = partial(jnp.einsum, precision=lax.Precision.HIGHEST)
    real_out = contract(form, real_in, cos_part) - contract(form, imag_in, sin_part)
    imag_out = contract(form, imag_in, cos_part) + contract(form, real_in, sin_part)
    return (real_out, imag_out)


def project_flow(spectrum, wave_x, wave_y, wave_z):
    wave_sq = wave_x * wave_x + wave_y * wave_y + wave_z * wave_z
    wave_safe = jnp.where(wave_sq > 0, wave_sq, 1.0)
    spread_sq = wave_sq / (4.0 * split_xi**2)
    green_fn = jnp.where(
        wave_sq > 0,
        (1.0 - bead_radius**2 * wave_sq / 3.0)
        * (1.0 + spread_sq)
        * jnp.exp(-spread_sq)
        / wave_safe,
        0.0,
    )
    along_wave = (wave_x * spectrum[0] + wave_y * spectrum[1] + wave_z * spectrum[2]) / wave_safe
    return jnp.stack(
        [
            green_fn * (spectrum[0] - wave_x * along_wave),
            green_fn * (spectrum[1] - wave_y * along_wave),
            green_fn * (spectrum[2] - wave_z * along_wave),
        ]
    )


def kspace_part(force_rows, n_gx, n_gy):
    local_x = G // n_gx
    local_y = G // n_gy
    grid_index = jnp.arange(G, dtype=jnp.int32)
    phase_grid = (grid_index[:, None] * grid_index[None, :] % G).astype(jnp.float32) * (
        2.0 * math.pi / G
    )
    cosine_table = jnp.cos(phase_grid)
    sine_table = jnp.sin(phase_grid)
    contract = partial(jnp.einsum, precision=lax.Precision.HIGHEST)
    force_field = force_rows.reshape(3, local_x, local_y, G)
    wave_full = signed_wave(grid_index)
    row_gx = lax.axis_index("gx")
    row_gy = lax.axis_index("gy")
    freq_count = G
    spec_z = jnp.stack(
        [
            contract("cabz,zk->cabk", force_field, cosine_table),
            -contract("cabz,zk->cabk", force_field, sine_table),
        ]
    )
    cos_x = cosine_table.reshape(n_gx, local_x, G)
    sin_x = sine_table.reshape(n_gx, local_x, G)
    cos_y = cosine_table.reshape(n_gy, local_y, G)
    sin_y = sine_table.reshape(n_gy, local_y, G)
    depth_part = freq_count // n_gx
    width_part = G // n_gy
    slabs = lax.all_to_all(spec_z[:, :, None], "gx", split_axis=5, concat_axis=2, tiled=True)
    xr_part, xi_part = forward_pass(slabs[0], slabs[1], "ciabl,iak->cbkl", cos_x, sin_x)
    pencils = lax.all_to_all(
        jnp.stack([xr_part, xi_part])[:, :, None], "gy", split_axis=4, concat_axis=2, tiled=True
    )
    yr_part, yi_part = forward_pass(pencils[0], pencils[1], "cjbkl,jbm->ckml", cos_y, sin_y)
    wave_x = signed_wave(row_gy * width_part + jnp.arange(width_part, dtype=jnp.int32))[
        :, None, None
    ]
    wave_y = wave_full[None, :, None]
    wave_z = signed_wave(row_gx * depth_part + jnp.arange(depth_part, dtype=jnp.int32))[
        None, None, :
    ]
    flow_real = project_flow(yr_part, wave_x, wave_y, wave_z)
    flow_imag = project_flow(yi_part, wave_x, wave_y, wave_z)
    br_part, bi_part = inverse_pass(flow_real, flow_imag, "ckml,jbm->cjbkl", cos_y, sin_y)
    back = lax.all_to_all(
        jnp.stack([br_part, bi_part]), "gy", split_axis=2, concat_axis=4, tiled=True
    )[:, :, 0]
    ar_part, ai_part = inverse_pass(back[0], back[1], "cbkl,iak->ciabl", cos_x, sin_x)
    gathered = lax.all_to_all(
        jnp.stack([ar_part, ai_part]), "gx", split_axis=2, concat_axis=5, tiled=True
    )[:, :, 0]
    result = contract("cabk,zk->cabz", gathered[0], cosine_table) - contract(
        "cabk,zk->cabz", gathered[1], sine_table
    )
    return (result / float(G**3)).reshape(3, local_x * local_y * G)


matmul = functools.partial(lax.dot_general, precision=lax.Precision.HIGHEST, preferred_element_type=jnp.float32)
PLAIN = (((1,), (0,)), ((), ()))
TURNED = (((1,), (1,)), ((), ()))


def wave_tables(n_gx, n_gy):
    share = G // 2 // n_gx
    width = G // n_gy
    grid = np.arange(G)
    turn = 2.0 * math.pi * (np.outer(grid, grid) % G) / G
    cos, sin = np.cos(turn), np.sin(turn)
    half = width // 2
    order = np.zeros(G, np.int64)
    for j in range(n_gy):
        for p in range(half):
            k = j * half + p
            order[j * width + p] = k
            order[j * width + half + p] = (G - k) % G if k else G // 2
    ahead = np.zeros((G, n_gx, 2, share))
    ahead[:, :, 0] = cos[:, : G // 2].reshape(G, n_gx, share)
    ahead[:, :, 1] = -sin[:, : G // 2].reshape(G, n_gx, share)
    back = 2.0 * ahead
    ahead[:, 0, 1, 0] = cos[:, G // 2]
    back[:, 0, 0, 0] = 1.0
    back[:, 0, 1, 0] = cos[:, G // 2]
    unit = 2.0 * math.pi / (G * grid_spacing)
    signed = np.where(grid < G // 2, grid, grid - G) * unit
    plain = np.where(grid == G // 2, 0.0, signed)
    edge = signed - plain
    lane = np.arange(128)
    across = np.zeros((n_gy, 8, 128))
    across[:, 0] = plain[order].reshape(n_gy, 1, width)[:, 0][:, lane % width]
    across[:, 1] = edge[order].reshape(n_gy, 1, width)[:, 0][:, lane % width]
    across[0, 2] = lane % half == 0
    deep = np.zeros((n_gx, 8, 128))
    per = 128 // width
    for v in range(share // per):
        deep[:, v] = (np.arange(n_gx)[:, None] * share + v * per + lane // width) * unit
    down = np.stack([np.broadcast_to(t[:, None], (G, 128)) for t in (plain, edge)])
    tables = {
        "ahead": ahead.reshape(G, G),
        "back": back.reshape(G, G).T,
        "first": np.concatenate([cos[:, order], sin[:, order]], axis=1),
        "first_back": np.concatenate([cos[:, order], sin[:, order]], axis=1),
        "second": np.concatenate([cos, sin], axis=0),
        "across": across,
        "deep": deep,
        "down": down,
    }
    return {name: np.asarray(table, np.float32) for name, table in tables.items()}


def spread(tiles, at, group, tall):
    count = 128 // group
    lane = lax.shift_right_logical(lax.broadcasted_iota(jnp.int32, (tall, 128), 1), group.bit_length() - 1)
    out = None
    for g, tile in enumerate(tiles):
        moved = pltpu.roll(tile, group * ((g - at) % count), 1) if g != at else tile
        out = moved if out is None else jnp.where(lane == g, moved, out)
    return out


def depth_kernel(field_ref, table_ref, out_ref, spec, *, n_gx, tall, wide):
    rows = tall * wide
    for c in range(3):
        spec[c * rows : (c + 1) * rows, :] = matmul(field_ref[c * rows : (c + 1) * rows, :], table_ref[...], PLAIN)
    group = G // n_gx
    count = n_gx

    @pl.loop(0, 3 * wide // count)
    def _(i):
        c = lax.div(i, jnp.int32(wide // count))
        b = (i - c * (wide // count)) * count
        tiles = [spec[pl.ds(c * rows + b + g, tall, stride=wide), :] for g in range(count)]
        for p in range(n_gx):
            out_ref[p, :, pl.ds(pl.multiple_of(i * 128, 128), 128)] = spread(tiles, p, group, tall)


def first_kernel(data_ref, table_ref, out_ref, turned, *, n_gy, share, wide):
    group = G // n_gy
    per = 128 // (2 * share)

    @pl.loop(0, 3 * wide // per)
    def _(i):
        c = lax.div(i, jnp.int32(wide // per))
        b = (i - c * (wide // per)) * per
        piece = jnp.transpose(data_ref[:, pl.ds(pl.multiple_of(i * 128, 128), 128)])
        both = matmul(piece, table_ref[...], PLAIN)
        for g in range(per):
            lo, mid, hi = g * 2 * share, (g * 2 + 1) * share, (g * 2 + 2) * share
            real = both[lo:mid, :128] + both[mid:hi, 128:]
            imag = both[mid:hi, :128] - both[lo:mid, 128:]
            turned[pl.ds(2 * c * share * wide + b + g, share, stride=wide), :] = real
            turned[pl.ds((2 * c + 1) * share * wide + b + g, share, stride=wide), :] = imag

    count = 128 // group

    @pl.loop(0, 6 * share // count)
    def _(i):
        at = i * (count * wide)
        tiles = [turned[pl.ds(pl.multiple_of(at + u * wide, 8), wide), :] for u in range(count)]
        for j in range(n_gy):
            out_ref[j, i] = spread(tiles, j, group, wide)


def second_kernel(ids, data_ref, table_ref, across_ref, deep_ref, down_ref, out_ref, flow, *, n_gy, views, wide):
    lane = lax.broadcasted_iota(jnp.int32, (G, 128), 1)
    width = G // n_gy
    half = width // 2
    across = across_ref[ids[1]]
    deep = deep_ref[ids[0]]
    alone = (lane < width) & (ids[0] == 0)
    mirror_self = across[2:3, :] > 0.5
    upper = (lane & half) != 0

    def whole(tile):
        return jnp.concatenate([data_ref[j, tile] for j in range(n_gy)], axis=0)

    def mirrored(value):
        other = jnp.where(upper, pltpu.roll(value, half, 1), pltpu.roll(value, 128 - half, 1))
        return jnp.where(mirror_self, value, other)

    def ahead(real, imag):
        one = matmul(table_ref[...], real, PLAIN)
        two = matmul(table_ref[...], imag, PLAIN)
        return one[:G] + two[G:], two[:G] - one[G:]

    def projected(spectrum, deep_plain, deep_edge):
        plain = (across[0:1, :], down_ref[0], deep_plain)
        edge = (across[1:2, :], down_ref[1], deep_edge)
        waves = [p + e for p, e in zip(plain, edge)]
        wave_sq = waves[0] * waves[0] + waves[1] * waves[1] + waves[2] * waves[2]
        live = wave_sq > 0
        inverse = 1.0 / jnp.where(live, wave_sq, 1.0)
        spread_sq = wave_sq / (4.0 * split_xi**2)
        green = (1.0 - bead_radius**2 * wave_sq / 3.0) * (1.0 + spread_sq) * jnp.exp(-spread_sq) * inverse
        green = jnp.where(live, green / float(G**3), 0.0)
        out = []
        for r in range(2):
            regular = sum(w * spectrum[c][r] for c, w in enumerate(plain)) * inverse
            nyquist = sum(w * spectrum[c][r] for c, w in enumerate(edge)) * inverse
            out.append([green * (spectrum[c][r] - plain[c] * regular - edge[c] * nyquist) for c in range(3)])
        return out

    zero = jnp.zeros((1, 128), jnp.float32)
    for v in range(views):
        spectrum = []
        apart = []
        for c in range(3):
            real = whole((2 * c) * views + v)
            imag = whole((2 * c + 1) * views + v)
            if v == 0:
                off_real = jnp.where(alone, 0.5 * (real - mirrored(real)), 0.0)
                off_imag = jnp.where(alone, 0.5 * (imag + mirrored(imag)), 0.0)
                apart.append(ahead(off_real, off_imag))
                real, imag = real - off_real, imag - off_imag
            spectrum.append(ahead(real, imag))
        found = projected(spectrum, deep[v : v + 1, :], zero)
        if v == 0:
            extra = projected(apart, zero, zero - math.pi / grid_spacing)
            found = [[a + b for a, b in zip(one, two)] for one, two in zip(found, extra)]
        for c in range(3):
            one = matmul(table_ref[...], found[0][c], PLAIN)
            two = matmul(table_ref[...], found[1][c], PLAIN)
            real, imag = one[:G] - two[G:], two[:G] + one[G:]
            for j in range(n_gy):
                out_ref[j, (2 * c) * views + v] = real[j * wide : (j + 1) * wide]
                out_ref[j, (2 * c + 1) * views + v] = imag[j * wide : (j + 1) * wide]


def first_back_kernel(data_ref, table_ref, out_ref, turned, *, n_gy, share, wide):
    group = G // n_gy
    count = n_gy
    per = 128 // (2 * share)

    @pl.loop(0, 6 * share // count)
    def _(i):
        tiles = [data_ref[j, i] for j in range(n_gy)]
        for u in range(count):
            turned[pl.ds(pl.multiple_of((i * count + u) * wide, 8), wide), :] = spread(tiles, u, group, wide)

    @pl.loop(0, 3 * wide // per)
    def _(i):
        c = lax.div(i, jnp.int32(wide // per))
        b = (i - c * (wide // per)) * per
        rows = []
        for g in range(per):
            real = turned[pl.ds(2 * c * share * wide + b + g, share, stride=wide), :]
            imag = turned[pl.ds((2 * c + 1) * share * wide + b + g, share, stride=wide), :]
            rows.append(jnp.concatenate([real, -imag], axis=1))
            rows.append(jnp.concatenate([imag, real], axis=1))
        piece = jnp.concatenate(rows, axis=0)
        out_ref[:, pl.ds(pl.multiple_of(i * 128, 128), 128)] = matmul(table_ref[...], piece, TURNED)


def depth_back_kernel(data_ref, table_ref, out_ref, spec, *, n_gx, tall, wide):
    rows = tall * wide
    group = G // n_gx
    count = n_gx

    @pl.loop(0, 3 * wide // count)
    def _(i):
        c = lax.div(i, jnp.int32(wide // count))
        b = (i - c * (wide // count)) * count
        tiles = [data_ref[p, :, pl.ds(pl.multiple_of(i * 128, 128), 128)] for p in range(n_gx)]
        for g in range(count):
            spec[pl.ds(c * rows + b + g, tall, stride=wide), :] = spread(tiles, g, group, tall)

    for c in range(3):
        out_ref[c * rows : (c + 1) * rows, :] = matmul(spec[c * rows : (c + 1) * rows, :], table_ref[...], PLAIN)


def waves(grid_data, n_gx, n_gy, fill):
    tall, wide, share = G // n_gx, G // n_gy, G // 2 // n_gx
    rows = 3 * tall * wide
    views = share * wide // 128
    tables = wave_tables(n_gx, n_gy)
    f32 = jnp.float32

    def run(name, kernel, shape, args, scratch, specs=None, after=(), **sizes):
        return launch(
            marking(ignoring(functools.partial(kernel, **sizes), len(args), len(after)), len(args) + len(after)),
            out_shape=(jax.ShapeDtypeStruct(shape, f32), jax.ShapeDtypeStruct((8, 128), f32)),
            in_specs=(specs or [MOVED_SPEC] + [VMEM_SPEC] * (len(args) - 1)) + [ANY_SPEC] * len(after),
            out_specs=(VMEM_SPEC,) * 2,
            scratch_shapes=[pltpu.VMEM(scratch, f32)],
            compiler_params=pltpu.CompilerParams(vmem_limit_bytes=32 * 1024 * 1024),
            name=name,
        )(*args, *after)

    def swap(value, axis):
        return lax.all_to_all(value, axis, split_axis=0, concat_axis=0, tiled=True)

    force = pl.BlockSpec((rows, 128), lambda i: (1, 0))
    lanes = 6 * wide * share
    ids = jnp.stack([lax.axis_index("gx"), lax.axis_index("gy")]).astype(jnp.int32)
    value, token = run("depth", depth_kernel, (n_gx, tall, lanes), (pltpu.with_memory_space_constraint(grid_data, pltpu.HBM), tables["ahead"]), (rows, 128),
                [force, VMEM_SPEC], n_gx=n_gx, tall=tall, wide=wide)
    after = fill(0, token)
    value = swap(value, "gx").reshape(G, lanes)
    value, token = run("first", first_kernel, (n_gy, 6 * views, wide, 128), (value, tables["first"]), (rows, 128),
                after=after, n_gy=n_gy, share=share, wide=wide)
    after = fill(1, token)
    value = swap(value.reshape(n_gy, 6 * views * wide, 128), "gy").reshape(n_gy, 6 * views, wide, 128)
    args = (ids, value, tables["second"], tables["across"], tables["deep"], tables["down"])
    value, token = run("second", second_kernel, (n_gy, 6 * views, wide, 128), args, (8, 128),
                [SMEM_SPEC, MOVED_SPEC] + [VMEM_SPEC] * 4, after, n_gy=n_gy, views=views, wide=wide)
    after = fill(2, token)
    value = swap(value.reshape(n_gy, 6 * views * wide, 128), "gy").reshape(n_gy, 6 * views, wide, 128)
    value, token = run("first_back", first_back_kernel, (G, lanes), (value, tables["first_back"]), (rows, 128),
                after=after, n_gy=n_gy, share=share, wide=wide)
    after = fill(3, token)
    value = swap(value.reshape(n_gx, tall, lanes), "gx")
    value, _ = run("depth_back", depth_back_kernel, (rows, 128), (value, tables["back"]), (rows, 128),
               after=after, n_gx=n_gx, tall=tall, wide=wide)
    return value


def shards(positions, noise, route, node_perm, pair_first, pair_second, pair_count):
    n_gx = lax.axis_size("gx")
    n_gy = lax.axis_size("gy")
    both = ("gx", "gy")
    peers = n_gx * n_gy
    slots = node_perm.shape[2]
    depth = slots // peers // 128
    rows = positions.shape[1] // 128
    rp = slots // 128
    swap = partial(lax.all_to_all, axis_name=both, split_axis=0, concat_axis=0, tiled=True)

    bounds = jnp.arange(peers + 1, dtype=jnp.int32) * (slots // peers)
    starts = jnp.sum(route[None, :] < bounds[:, None], axis=1, dtype=jnp.int32)
    taken = swap(slots_call(starts, route.reshape(rows, 128), depth))
    places = positions.reshape(3, rows, 128)
    data = swap(pack_call(starts, places, depth))
    counts = jnp.sum(taken >= 0, axis=(1, 2), dtype=jnp.int32)
    own_order = lax.dynamic_index_in_dim(node_perm, lax.axis_index("gx"), 0, False)
    nodes, node_lists, row_lists = nodes_call(taken, own_order.reshape(peers, depth, 128), slots)
    own_pairs, far_pairs, totals = order_call(pair_first[0], pair_second[0], pair_count, slots // CELL)
    grid_data, cells = scatter_call(node_lists, counts, data, rp, after=(totals,))

    state = {"sums": None}

    def within(n, after):
        state["sums"], token = pair_call(own_pairs, totals, n, cells, state["sums"], after=after)
        return token

    def fill(n, token):
        if n < 3:
            if n == 1:
                ready, _ = lax.optimization_barrier((grid_data, token))
                state["beside"] = shifted(ready, "gx", -1)
            return (within(n, (token,)),)
        state["sums"], _, far = pair_call(
            far_pairs, totals, len(PARTS) + 2, cells, state["sums"], state["beside"], after=(token,)
        )
        state["far"] = shifted(far, "gx", 1)
        return (within(3, ()),)

    share = G // 2 // n_gx
    if share % 8 == 0 and share * (G // n_gy) % 128 == 0:
        wave_vel = waves(grid_data, n_gx, n_gy, fill)
    else:
        wave_vel = kspace_part(grid_data[3 * rp :], n_gx, n_gy).reshape(3 * rp, 128)
        for n in range(4):
            fill(n, wave_vel)
    back = swap(gather_call(row_lists, counts, nodes, state["sums"], wave_vel, state["far"]))
    moved, drift = finish_call(starts, back, places, noise.reshape(3, rows, 128))
    return (moved.reshape(positions.shape), drift.reshape(positions.shape))


def solution(mesh):
    in_specs = (
        P(None, ("gx", "gy")),
        P(None, ("gx", "gy")),
        P(("gx", "gy")),
        P(None, "gy", None),
        P(("gx", "gy"), None),
        P(("gx", "gy"), None),
        P(("gx", "gy")),
    )
    out_specs = (P(None, ("gx", "gy")), P(None, ("gx", "gy")))
    return jax.shard_map(shards, mesh=mesh, in_specs=in_specs, out_specs=out_specs, check_vma=False)
```

```python
import functools
from functools import partial
import math

import jax
import jax.numpy as jnp
import numpy as np
from jax import lax
from jax.experimental import pallas as pl
from jax.experimental.pallas import tpu as pltpu
from jax.sharding import PartitionSpec as P

G = 128
BEAD_CH = 64
CELL = 64


bead_radius = 0.5
split_xi = 0.5
time_step = 0.01
fene_k = 30.0
fene_reach = 1.5
bend_k = 2.0
grid_spacing = 4.0
pair_block = 64


def shifted(value, axis, by):
    devices = lax.axis_size(axis)
    return lax.ppermute(value, axis, [(i, (i + by) % devices) for i in range(devices)])


SPAN = 64
PARTS = (25, 37, 52)

SMEM_SPEC = pl.BlockSpec(memory_space=pltpu.SMEM)
LIST_SPEC = pl.BlockSpec(memory_space=pltpu.SMEM)
VMEM_SPEC = pl.BlockSpec(memory_space=pltpu.VMEM)
MOVED_SPEC = pl.BlockSpec(memory_space=pltpu.VMEM)


ANY_SPEC = pl.BlockSpec(memory_space=pl.ANY)


def launch(kernel, *, out_shape, in_specs, out_specs, **options):
    def block(spec, value):
        shape = value.shape
        return pl.BlockSpec(shape, lambda i: (0,) * len(shape)) if spec is VMEM_SPEC or spec is MOVED_SPEC else spec

    def placed(spec, value):
        return spec is VMEM_SPEC or spec is LIST_SPEC or (spec is ANY_SPEC and value.dtype == jnp.float32)

    def run(*args):
        several = isinstance(out_shape, tuple)
        shapes = out_shape if several else (out_shape,)
        outs = out_specs if several else (out_specs,)
        found = tuple(block(s, v) for s, v in zip(outs, shapes))
        kept = tuple(pltpu.HBM(v.shape, v.dtype) if s is VMEM_SPEC else v for s, v in zip(outs, shapes))
        args = [
            pltpu.with_memory_space_constraint(jnp.asarray(v), pltpu.HBM) if placed(s, v) else v
            for s, v in zip(in_specs, args)
        ]
        return pl.pallas_call(
            kernel,
            out_shape=kept if several else kept[0],
            grid=(1,),
            in_specs=[block(s, v) for s, v in zip(in_specs, args)],
            out_specs=found if several else found[0],
            **options,
        )(*args)

    return run


def ignoring(kernel, inputs, extra):
    def run(*refs):
        kernel(*refs[:inputs], *refs[inputs + extra :])

    return run


def marking(kernel, inputs):
    def run(*refs):
        refs[inputs + 1][...] = jnp.zeros(refs[inputs + 1].shape, jnp.float32)
        kernel(*refs[: inputs + 1], *refs[inputs + 2 :])

    return run


def lane_index(rows):
    return lax.broadcasted_iota(jnp.int32, (rows, 128), 1)


def window(table, at, rows):
    row = lax.shift_right_logical(at, 7)
    lead = at & 127
    head = pltpu.roll(table[pl.ds(row, rows), :], (128 - lead) & 127, 1)
    tail = pltpu.roll(table[pl.ds(row + 1, rows), :], (128 - lead) & 127, 1)
    return jnp.where(lane_index(rows) < 128 - lead, head, tail)


def slots_kernel(starts, route_ref, out_ref, table, *, rows, depth):
    table[pl.ds(0, rows), :] = route_ref[...]
    table[pl.ds(rows, depth + 8), :] = jnp.zeros((depth + 8, 128), jnp.int32)
    place = lane_index(depth) + lax.broadcasted_iota(jnp.int32, (depth, 128), 0) * 128

    @pl.loop(0, out_ref.shape[0])
    def _(t):
        at = starts[t]
        slot = window(table, at, depth) - t * (depth * 128)
        out_ref[t] = jnp.where(place < starts[t + 1] - at, slot, -1)


def slots_call(starts, route, depth):
    rows = route.shape[0]
    peers = starts.shape[0] - 1
    return launch(
        functools.partial(slots_kernel, rows=rows, depth=depth),
        out_shape=jax.ShapeDtypeStruct((peers, depth, 128), jnp.int32),
        in_specs=[SMEM_SPEC, VMEM_SPEC],
        out_specs=VMEM_SPEC,
        scratch_shapes=[pltpu.VMEM((rows + depth + 8, 128), jnp.int32)],
        compiler_params=pltpu.CompilerParams(vmem_limit_bytes=32 * 1024 * 1024),
        name="slots",
    )(starts, route)


def chain_forces(pos):
    rows = pos[0].shape[0]
    place = lane_index(rows) & (BEAD_CH - 1)
    bonded = place < BEAD_CH - 1
    bent = place < BEAD_CH - 2
    after = (place > 0) & bonded
    bond = [jnp.where(bonded, pltpu.roll(x, 127, 1) - x, 0.5) for x in pos]
    square = bond[0] * bond[0] + bond[1] * bond[1] + bond[2] * bond[2]
    inverse = lax.rsqrt(square)
    unit = [b * inverse for b in bond]
    following = [pltpu.roll(u, 127, 1) for u in unit]
    previous = [pltpu.roll(u, 1, 1) for u in unit]
    cosine = sum(u * v for u, v in zip(unit, following))
    cosine_before = pltpu.roll(cosine, 1, 1)
    pull = fene_k / (1.0 - square / fene_reach**2)
    out = []
    for c in range(3):
        turn = jnp.where(bent, following[c] - cosine * unit[c], 0.0)
        turn = turn + jnp.where(after, previous[c] - cosine_before * unit[c], 0.0)
        slope = jnp.where(bonded, pull * bond[c] - bend_k * inverse * turn, 0.0)
        out.append(slope - pltpu.roll(slope, 1, 1))
    return out


def pack_kernel(starts, pos_ref, out_ref, table, *, rows, depth, stride):
    step = 32 if rows % 32 == 0 else 8

    @pl.loop(0, rows // step)
    def _(i):
        at = pl.multiple_of(i * step, step)
        pos = [pos_ref[c, pl.ds(at, step), :] for c in range(3)]
        for c, value in enumerate(pos + chain_forces(pos)):
            table[pl.ds(c * stride + at, step), :] = value

    for c in range(6):
        table[pl.ds(c * stride + rows, stride - rows), :] = jnp.zeros((stride - rows, 128), jnp.float32)

    @pl.loop(0, out_ref.shape[0])
    def _(t):
        at = starts[t]
        for c in range(6):
            out_ref[t, c * depth : (c + 1) * depth, :] = window(table, at + c * stride * 128, depth)


def pack_call(starts, pos, depth):
    rows = pos.shape[1]
    peers = starts.shape[0] - 1
    stride = rows + depth + 8
    stride += -stride % 8
    return launch(
        functools.partial(pack_kernel, rows=rows, depth=depth, stride=stride),
        out_shape=jax.ShapeDtypeStruct((peers, 6 * depth, 128), jnp.float32),
        in_specs=[SMEM_SPEC, VMEM_SPEC],
        out_specs=VMEM_SPEC,
        scratch_shapes=[pltpu.VMEM((6 * stride, 128), jnp.float32)],
        compiler_params=pltpu.CompilerParams(vmem_limit_bytes=32 * 1024 * 1024),
        name="pack",
    )(starts, pos)


def list_count(depth):
    return 8 if depth % 8 == 0 else 1


def nodes_kernel(slots_ref, perm_ref, node_ref, *list_refs, depth, spare):
    tile = list_count(depth)
    parts = depth // tile

    @pl.loop(0, slots_ref.shape[0])
    def _(t):
        rows = [jnp.broadcast_to(perm_ref[t, w : w + 1, :], (8, 128)) for w in range(depth)]
        for r in range(parts):
            slot = jnp.broadcast_to(slots_ref[t, r * tile : (r + 1) * tile, :], (8, 128))
            place = slot & 127
            which = slot >> 7
            node = jnp.full((8, 128), spare, jnp.int32)
            for w in range(depth):
                node = jnp.where(which == w, jnp.take_along_axis(rows[w], place, axis=1), node)
            packed = ((node >> 12) << 7) | (node & 127)
            node_ref[t, r * tile : (r + 1) * tile, :] = node[:tile]
            for u in range(tile):
                list_refs[u][pl.ds(t * parts + r, 1), :] = node[u : u + 1]
                list_refs[tile + u][pl.ds(t * parts + r, 1), :] = packed[u : u + 1]


def nodes_call(slots, perm, spare):
    peers, depth, _ = slots.shape
    lists = list_count(depth)
    one = jax.ShapeDtypeStruct((peers * depth // lists, 128), jnp.int32)
    found = launch(
        functools.partial(nodes_kernel, depth=depth, spare=spare),
        out_shape=(jax.ShapeDtypeStruct(slots.shape, jnp.int32),) + (one,) * (2 * lists),
        in_specs=[MOVED_SPEC, VMEM_SPEC],
        out_specs=(VMEM_SPEC,) * (1 + 2 * lists),
        compiler_params=pltpu.CompilerParams(vmem_limit_bytes=32 * 1024 * 1024),
        name="nodes",
    )(slots, perm)
    flat = [x.reshape(-1) for x in found[1:]]
    return found[0], flat[:lists], flat[lists:]


def move_rows(lists, count, t, depth, move):
    width = len(lists)
    parts = depth // width

    def part(p, carry):
        live = jnp.minimum(count - p * (width * 128), 128)
        base = (t * parts + p) * 128
        start = p * (width * 128)

        def some(i, carry):
            for k in range(SPAN):
                at = i * SPAN + k
                for u in range(width):
                    move(start + at + u * 128, lists[u][base + at])
            return carry

        return lax.fori_loop(0, lax.div(live + (SPAN - 1), jnp.int32(SPAN)), some, carry)

    whole = width * 128
    lax.fori_loop(0, lax.div(count + (whole - 1), jnp.int32(whole)), part, 0)


def scatter_kernel(counts, in_ref, *refs, depth, rp, lists):
    nodes = refs[:lists]
    out_ref, cells_ref, table, rows_ref = refs[lists:]

    @pl.loop(0, rp)
    def _(k):
        table[pl.ds(pl.multiple_of(k * 128, 128), 128), :] = jnp.zeros((128, 128), jnp.float32)

    together = 8 if depth % 8 == 0 else 1

    @pl.loop(0, in_ref.shape[0])
    def _(t):
        def turn(i, carry):
            for j in range(together):
                r = i * together + j
                piece = in_ref[t, pl.ds(r, 6, stride=depth), :]
                piece = jnp.concatenate([piece, jnp.zeros((2, 128), jnp.float32)], axis=0)
                piece = jnp.concatenate([piece] * 16, axis=0)
                rows_ref[pl.ds(pl.multiple_of(r * 128, 128), 128), :] = jnp.transpose(piece)
            return carry

        def move(at, node):
            table[pl.ds(node, 1), :] = rows_ref[pl.ds(at, 1), :]

        count = counts[t]
        part = together * 128
        lax.fori_loop(0, lax.div(count + (part - 1), jnp.int32(part)), turn, 0)
        move_rows(nodes, count, t, depth, move)

    group = lane_index(8) >> 3

    @pl.loop(0, rp // 16)
    def _(g):
        tiles = []
        for i in range(16):
            tile = table[pl.ds(pl.multiple_of(g * 2048, 2048) + 8 * i, 8), :]
            for k in range(1, 16):
                one = table[pl.ds(pl.multiple_of(g * 2048, 2048) + k * 128 + 8 * i, 8), :]
                tile = jnp.where(group == k, one, tile)
            tiles.append(tile)
        at = pl.multiple_of(g * 128, 128)
        cells_ref[pl.ds(at, 128), :] = jnp.transpose(jnp.concatenate(tiles, axis=0))
        for c in range(6):
            out_ref[pl.ds(pl.multiple_of(c * rp + g * 16, 16), 16), :] = cells_ref[pl.ds(at + c, 16, stride=8), :]


def scatter_call(nodes, counts, data, rp, after=()):
    depth = data.shape[1] // 6
    return launch(
        ignoring(
            functools.partial(scatter_kernel, depth=depth, rp=rp, lists=len(nodes)), 2 + len(nodes), len(after)
        ),
        out_shape=(
            jax.ShapeDtypeStruct((6 * rp, 128), jnp.float32),
            jax.ShapeDtypeStruct((8 * rp, 128), jnp.float32),
        ),
        in_specs=[SMEM_SPEC, MOVED_SPEC] + [LIST_SPEC] * len(nodes) + [ANY_SPEC] * len(after),
        out_specs=(VMEM_SPEC,) * 2,
        scratch_shapes=[
            pltpu.VMEM((rp * 128 + 8, 128), jnp.float32),
            pltpu.VMEM((depth * 128, 128), jnp.float32),
        ],
        compiler_params=pltpu.CompilerParams(vmem_limit_bytes=52 * 1024 * 1024),
        name="scatter",
    )(counts, data, *nodes, *after)


def gather_kernel(counts, node_ref, sums_ref, one_ref, two_ref, *refs, depth, rp, lists):
    rows = refs[:lists]
    out_ref, table, found, comb = refs[lists:]
    comb[...] = jnp.zeros((128, 128), jnp.float32)

    @pl.loop(0, rp // 32)
    def _(g):
        for c in range(3):
            at = pl.ds(pl.multiple_of(c * rp + g * 32, 32), 32)
            comb[pl.ds(c, 32, stride=4), :] = one_ref[at, :] + two_ref[at, :]
        for i in range(16):
            pair = [sums_ref[pl.ds(pl.multiple_of((g * 32 + 2 * i + h) * 8, 8), 8), :] for h in range(2)]
            both = pair[0] + pltpu.roll(pair[1], 4, 0)
            comb[8 * i : 8 * i + 8, :] = comb[8 * i : 8 * i + 8, :] + both
        table[pl.ds(pl.multiple_of(g * 128, 128), 128), :] = jnp.transpose(comb[...])

    together = 8 if depth % 8 == 0 else 1

    @pl.loop(0, out_ref.shape[0])
    def _(t):
        def move(at, row):
            found[pl.ds(at, 1), :] = table[pl.ds(row, 1), :]

        def turn(i, carry):
            for j in range(together):
                r = i * together + j
                turned = jnp.transpose(found[pl.ds(pl.multiple_of(r * 128, 128), 128), :])
                place = jnp.broadcast_to(node_ref[t, pl.ds(r, 1), :], (8, 128)) >> 7
                half = (place >> 1) & 15
                value = turned[:8]
                for h in range(1, 16):
                    value = jnp.where(half == h, turned[8 * h : 8 * h + 8], value)
                value = jnp.where((place & 1) == 1, pltpu.roll(value, 4, 0), value)
                out_ref[t, pl.ds(r, 3, stride=depth), :] = value[:3]
            return carry

        count = counts[t]
        part = together * 128
        move_rows(rows, count, t, depth, move)
        lax.fori_loop(0, lax.div(count + (part - 1), jnp.int32(part)), turn, 0)


def gather_call(rows, counts, nodes, sums, one, two):
    rp = one.shape[0] // 3
    peers, depth, _ = nodes.shape
    return launch(
        functools.partial(gather_kernel, depth=depth, rp=rp, lists=len(rows)),
        out_shape=jax.ShapeDtypeStruct((peers, 3 * depth, 128), jnp.float32),
        in_specs=[SMEM_SPEC] + [VMEM_SPEC] * 4 + [LIST_SPEC] * len(rows),
        out_specs=VMEM_SPEC,
        scratch_shapes=[
            pltpu.VMEM((rp * 4 + 8, 128), jnp.float32),
            pltpu.VMEM((depth * 128, 128), jnp.float32),
            pltpu.VMEM((128, 128), jnp.float32),
        ],
        compiler_params=pltpu.CompilerParams(vmem_limit_bytes=32 * 1024 * 1024),
        name="gather",
    )(counts, nodes, sums, one, two, *rows)


def finish_kernel(starts, in_ref, pos_ref, noise_ref, moved_ref, drift_ref, table, *, rows, depth, stride):
    lane = lane_index(depth)
    first = lane_index(1)

    @pl.loop(0, in_ref.shape[0])
    def _(t):
        at = starts[t]
        row = lax.shift_right_logical(at, 7)
        lead = at & 127
        for c in range(3):
            value = pltpu.roll(in_ref[t, c * depth : (c + 1) * depth, :], lead, 1)
            here = pl.ds(c * stride + row, depth)
            behind = pl.ds(c * stride + row + 1, depth)
            edge = table[pl.ds(c * stride + row, 1), :]
            table[behind, :] = value
            if depth > 1:
                body = jnp.where(lane[1:] < lead, value[:-1], value[1:])
                table[pl.ds(c * stride + row + 1, depth - 1), :] = body
            table[pl.ds(c * stride + row, 1), :] = jnp.where(first < lead, edge, value[:1])

    step = 8

    @pl.loop(0, rows // step)
    def _(i):
        at = pl.multiple_of(i * step, step)
        for c in range(3):
            drift = time_step * table[pl.ds(c * stride + at, step), :]
            drift_ref[c, pl.ds(at, step), :] = drift
            moved_ref[c, pl.ds(at, step), :] = pos_ref[c, pl.ds(at, step), :] + drift + noise_ref[c, pl.ds(at, step), :]


def finish_call(starts, data, pos, noise):
    rows = pos.shape[1]
    depth = data.shape[1] // 3
    stride = rows + depth + 8
    stride += -stride % 8
    return launch(
        functools.partial(finish_kernel, rows=rows, depth=depth, stride=stride),
        out_shape=(jax.ShapeDtypeStruct(pos.shape, jnp.float32),) * 2,
        in_specs=[SMEM_SPEC, MOVED_SPEC] + [VMEM_SPEC] * 2,
        out_specs=(VMEM_SPEC,) * 2,
        scratch_shapes=[pltpu.VMEM((3 * stride, 128), jnp.float32)],
        compiler_params=pltpu.CompilerParams(vmem_limit_bytes=32 * 1024 * 1024),
        name="finish",
    )(starts, data, pos, noise)


ERFCX_COEF = (0.06548172872398669,
    -0.3609186250151195,
    0.6338942267842493,
    -0.3384301108125971,
    0.4003704641202259,
    0.13581047899030682,
    0.2395463173952274,
    0.22417089752024144,
    7.010614160106155e-05)


def pair_math(square, coef):
    inverse = lax.rsqrt(square)
    ratio = pl.reciprocal(1.0 + 0.2 * (square * inverse))
    scaled = coef[0] * ratio + coef[1]
    for k in coef[2:]:
        scaled = scaled * ratio + k
    decay = jnp.exp(-0.25 * square)
    inverse_sq = inverse * inverse
    screen = scaled * inverse
    along = decay * (screen * (0.375 + 0.0625 * inverse_sq) + 0.125)
    across = (decay * inverse_sq) * (screen * (0.375 - 0.1875 * inverse_sq) - 0.125)
    return along, across

def order_kernel(first, second, count, own_ref, far_ref, totals, *, blocks):
    def step(p, sizes):
        own, far = sizes
        other = second[p]
        within = other < blocks
        both = first[p] * 65536 + other
        own_ref[own] = both
        far_ref[far] = both - blocks
        inside = within.astype(jnp.int32)
        return own + inside, far + 1 - inside

    own, far = lax.fori_loop(0, count[0], step, (jnp.int32(0), jnp.int32(0)))
    steps = first.shape[0]
    totals[0] = 0
    for n, part in enumerate(PARTS):
        totals[n + 1] = jnp.minimum(own, steps * part // 128)
    totals[len(PARTS) + 1] = own
    totals[len(PARTS) + 2] = 0
    totals[len(PARTS) + 3] = far


def order_call(first, second, count, blocks):
    size = first.shape[0] + 8
    return launch(
        functools.partial(order_kernel, blocks=blocks),
        out_shape=(jax.ShapeDtypeStruct((size,), jnp.int32),) * 2 + (jax.ShapeDtypeStruct((len(PARTS) + 4,), jnp.int32),),
        in_specs=[SMEM_SPEC] * 3,
        out_specs=(SMEM_SPEC,) * 3,
        compiler_params=pltpu.CompilerParams(vmem_limit_bytes=32 * 1024 * 1024),
        name="order",
    )(first, second, count)


def fill_cells(src_ref, cells, rp):
    @pl.loop(0, rp // 8)
    def _(i):
        at = pl.multiple_of(i * 8, 8)
        for c in range(6):
            cells[pl.ds(at * 8 + c, 8, stride=8), :] = src_ref[pl.ds(pl.multiple_of(c * rp + at, 8), 8), :]


def pair_kernel(pairs, bounds, cells_ref, *refs, rp, coef, unroll, beyond, part, fresh):
    if not fresh:
        near_in, *refs = refs
    if beyond:
        other_ref, near_ref, token, far_ref, other_cells, far_sums = refs
        fill_cells(other_ref, other_cells, rp)
        far_sums[...] = jnp.zeros(far_sums.shape, jnp.float32)
    else:
        near_ref, token = refs
        other_cells, far_sums = cells_ref, near_ref
    lane = lax.broadcasted_iota(jnp.int32, (8, 128), 1)
    sub = lax.broadcasted_iota(jnp.int32, (8, 128), 0)
    left = lane < 64
    unturn = (lane + sub) & 127
    near_ref[...] = jnp.zeros(near_ref.shape, jnp.float32) if fresh else near_in[...]
    token[...] = jnp.zeros((8, 128), jnp.float32)

    def row(k):
        return pl.ds(pl.multiple_of((k >> 1) * 8, 8), 8)

    def both_halves(table, k):
        cell = table[row(k), :]
        return jnp.where(left == ((k & 1) == 0), cell, pltpu.roll(cell, 64, 1))

    def stacked(parts):
        out = jnp.zeros((8, 128), jnp.float32)
        for c, part in enumerate(parts):
            out = jnp.where(sub == c, jnp.sum(part, axis=0, keepdims=True), out)
        return out

    def one(ka, kb):
        near = both_halves(cells_ref, ka)
        near = jnp.where(left, near, pltpu.roll(near, 96, 1))
        far = both_halves(other_cells, kb)
        mine = [jnp.broadcast_to(near[c : c + 1, :], (8, 128)) for c in range(6)]
        other = [jnp.broadcast_to(far[c : c + 1, :], (8, 128)) for c in range(6)]
        near_sum = None
        far_sum = None
        for q in (3, 2, 1, 0):
            turned = [pltpu.roll(x, 8 * q, 1, stride=1, stride_axis=0) for x in other]
            gap = [mine[c] - turned[c] for c in range(3)]
            along, across = pair_math(gap[0] * gap[0] + gap[1] * gap[1] + gap[2] * gap[2] + 0.25, coef)
            to_near = across * (gap[0] * turned[3] + gap[1] * turned[4] + gap[2] * turned[5])
            to_far = across * (gap[0] * mine[3] + gap[1] * mine[4] + gap[2] * mine[5])
            near_add = [along * turned[3 + c] + to_near * gap[c] for c in range(3)]
            far_add = [along * mine[3 + c] + to_far * gap[c] for c in range(3)]
            if near_sum is None:
                near_sum, far_sum = near_add, far_add
            else:
                near_sum = [a + b for a, b in zip(near_sum, near_add)]
                far_sum = [pltpu.roll(a, 120, 1) + b for a, b in zip(far_sum, far_add)]
        far_sum = [jnp.take_along_axis(a, unturn, axis=1) for a in far_sum]
        near_vel = stacked(near_sum)
        half = jnp.where(left, pltpu.roll(near_vel, 64, 1), 0.0)
        near_vel = jnp.where(left, near_vel, 0.0) + pltpu.roll(half, 32, 1)
        near_vel = near_vel + pltpu.roll(near_vel, 64, 1)
        far_vel = stacked(far_sum)
        far_vel = far_vel + pltpu.roll(far_vel, 64, 1)
        return near_vel, far_vel

    low = bounds[part]
    high = bounds[part + 1]

    def turn(i, carry):
        found = []
        for k in range(unroll):
            p = low + i * unroll + k
            alive = p < high
            both = jnp.where(alive, pairs[p], 0)
            ka, kb = both >> 16, both & 65535
            found.append((alive, ka, kb, one(ka, kb)))
        for alive, ka, kb, (near_vel, far_vel) in found:
            near_ref[row(ka), :] += jnp.where((left == ((ka & 1) == 0)) & alive, near_vel, 0.0)
            if not beyond:
                alive = alive & (ka != kb)
            far_sums[row(kb), :] += jnp.where((left == ((kb & 1) == 0)) & alive, far_vel, 0.0)
        return carry

    lax.fori_loop(0, lax.div(jnp.maximum(high - low, 0) + (unroll - 1), jnp.int32(unroll)), turn, 0)

    if beyond:
        for c in range(3):
            @pl.loop(0, rp // 8)
            def _(i):
                at = pl.ds(pl.multiple_of(c * rp + i * 8, 8), 8)
                far_ref[at, :] = far_sums[pl.ds(i * 64 + c, 8, stride=8), :]


def pair_call(pairs, bounds, part, cells, near=None, beside=None, after=(), coef=ERFCX_COEF, unroll=8):
    rp = cells.shape[0] // 8
    beyond = beside is not None
    fresh = near is None
    extra = [cells] + ([] if fresh else [near]) + ([beside] if beyond else [])
    out = [jax.ShapeDtypeStruct((8 * rp, 128), jnp.float32), jax.ShapeDtypeStruct((8, 128), jnp.float32)]
    scratch = []
    if beyond:
        out.append(jax.ShapeDtypeStruct((3 * rp, 128), jnp.float32))
        scratch = [pltpu.VMEM((8 * rp, 128), jnp.float32)] * 2
    return launch(
        ignoring(
            functools.partial(
                pair_kernel, rp=rp, coef=coef, unroll=unroll, beyond=beyond, part=part, fresh=fresh
            ),
            2 + len(extra),
            len(after),
        ),
        out_shape=tuple(out),
        in_specs=[SMEM_SPEC] * 2 + [VMEM_SPEC] * (len(extra) - beyond) + [MOVED_SPEC] * beyond + [ANY_SPEC] * len(after),
        out_specs=(VMEM_SPEC,) * len(out),
        scratch_shapes=scratch,
        compiler_params=pltpu.CompilerParams(vmem_limit_bytes=32 * 1024 * 1024),
        name="beyond" if beyond else "within",
    )(pairs, bounds, *extra, *after)


def signed_wave(grid_index):
    return jnp.where(grid_index < G // 2, grid_index, grid_index - G).astype(jnp.float32) * (
        2.0 * math.pi / (G * grid_spacing)
    )


def forward_pass(real_in, imag_in, form, cos_part, sin_part):
    contract = partial(jnp.einsum, precision=lax.Precision.HIGHEST)
    real_out = contract(form, real_in, cos_part) + contract(form, imag_in, sin_part)
    imag_out = contract(form, imag_in, cos_part) - contract(form, real_in, sin_part)
    return (real_out, imag_out)


def inverse_pass(real_in, imag_in, form, cos_part, sin_part):
    contract = partial(jnp.einsum, precision=lax.Precision.HIGHEST)
    real_out = contract(form, real_in, cos_part) - contract(form, imag_in, sin_part)
    imag_out = contract(form, imag_in, cos_part) + contract(form, real_in, sin_part)
    return (real_out, imag_out)


def project_flow(spectrum, wave_x, wave_y, wave_z):
    wave_sq = wave_x * wave_x + wave_y * wave_y + wave_z * wave_z
    wave_safe = jnp.where(wave_sq > 0, wave_sq, 1.0)
    spread_sq = wave_sq / (4.0 * split_xi**2)
    green_fn = jnp.where(
        wave_sq > 0,
        (1.0 - bead_radius**2 * wave_sq / 3.0)
        * (1.0 + spread_sq)
        * jnp.exp(-spread_sq)
        / wave_safe,
        0.0,
    )
    along_wave = (wave_x * spectrum[0] + wave_y * spectrum[1] + wave_z * spectrum[2]) / wave_safe
    return jnp.stack(
        [
            green_fn * (spectrum[0] - wave_x * along_wave),
            green_fn * (spectrum[1] - wave_y * along_wave),
            green_fn * (spectrum[2] - wave_z * along_wave),
        ]
    )


def kspace_part(force_rows, n_gx, n_gy):
    local_x = G // n_gx
    local_y = G // n_gy
    grid_index = jnp.arange(G, dtype=jnp.int32)
    phase_grid = (grid_index[:, None] * grid_index[None, :] % G).astype(jnp.float32) * (
        2.0 * math.pi / G
    )
    cosine_table = jnp.cos(phase_grid)
    sine_table = jnp.sin(phase_grid)
    contract = partial(jnp.einsum, precision=lax.Precision.HIGHEST)
    force_field = force_rows.reshape(3, local_x, local_y, G)
    wave_full = signed_wave(grid_index)
    row_gx = lax.axis_index("gx")
    row_gy = lax.axis_index("gy")
    freq_count = G
    spec_z = jnp.stack(
        [
            contract("cabz,zk->cabk", force_field, cosine_table),
            -contract("cabz,zk->cabk", force_field, sine_table),
        ]
    )
    cos_x = cosine_table.reshape(n_gx, local_x, G)
    sin_x = sine_table.reshape(n_gx, local_x, G)
    cos_y = cosine_table.reshape(n_gy, local_y, G)
    sin_y = sine_table.reshape(n_gy, local_y, G)
    depth_part = freq_count // n_gx
    width_part = G // n_gy
    slabs = lax.all_to_all(spec_z[:, :, None], "gx", split_axis=5, concat_axis=2, tiled=True)
    xr_part, xi_part = forward_pass(slabs[0], slabs[1], "ciabl,iak->cbkl", cos_x, sin_x)
    pencils = lax.all_to_all(
        jnp.stack([xr_part, xi_part])[:, :, None], "gy", split_axis=4, concat_axis=2, tiled=True
    )
    yr_part, yi_part = forward_pass(pencils[0], pencils[1], "cjbkl,jbm->ckml", cos_y, sin_y)
    wave_x = signed_wave(row_gy * width_part + jnp.arange(width_part, dtype=jnp.int32))[
        :, None, None
    ]
    wave_y = wave_full[None, :, None]
    wave_z = signed_wave(row_gx * depth_part + jnp.arange(depth_part, dtype=jnp.int32))[
        None, None, :
    ]
    flow_real = project_flow(yr_part, wave_x, wave_y, wave_z)
    flow_imag = project_flow(yi_part, wave_x, wave_y, wave_z)
    br_part, bi_part = inverse_pass(flow_real, flow_imag, "ckml,jbm->cjbkl", cos_y, sin_y)
    back = lax.all_to_all(
        jnp.stack([br_part, bi_part]), "gy", split_axis=2, concat_axis=4, tiled=True
    )[:, :, 0]
    ar_part, ai_part = inverse_pass(back[0], back[1], "cbkl,iak->ciabl", cos_x, sin_x)
    gathered = lax.all_to_all(
        jnp.stack([ar_part, ai_part]), "gx", split_axis=2, concat_axis=5, tiled=True
    )[:, :, 0]
    result = contract("cabk,zk->cabz", gathered[0], cosine_table) - contract(
        "cabk,zk->cabz", gathered[1], sine_table
    )
    return (result / float(G**3)).reshape(3, local_x * local_y * G)


matmul = functools.partial(lax.dot_general, precision=lax.Precision.HIGHEST, preferred_element_type=jnp.float32)
PLAIN = (((1,), (0,)), ((), ()))
TURNED = (((1,), (1,)), ((), ()))


def wave_tables(n_gx, n_gy):
    share = G // 2 // n_gx
    width = G // n_gy
    grid = np.arange(G)
    turn = 2.0 * math.pi * (np.outer(grid, grid) % G) / G
    cos, sin = np.cos(turn), np.sin(turn)
    half = width // 2
    order = np.zeros(G, np.int64)
    for j in range(n_gy):
        for p in range(half):
            k = j * half + p
            order[j * width + p] = k
            order[j * width + half + p] = (G - k) % G if k else G // 2
    ahead = np.zeros((G, n_gx, 2, share))
    ahead[:, :, 0] = cos[:, : G // 2].reshape(G, n_gx, share)
    ahead[:, :, 1] = -sin[:, : G // 2].reshape(G, n_gx, share)
    back = 2.0 * ahead
    ahead[:, 0, 1, 0] = cos[:, G // 2]
    back[:, 0, 0, 0] = 1.0
    back[:, 0, 1, 0] = cos[:, G // 2]
    unit = 2.0 * math.pi / (G * grid_spacing)
    signed = np.where(grid < G // 2, grid, grid - G) * unit
    plain = np.where(grid == G // 2, 0.0, signed)
    edge = signed - plain
    lane = np.arange(128)
    across = np.zeros((n_gy, 8, 128))
    across[:, 0] = plain[order].reshape(n_gy, 1, width)[:, 0][:, lane % width]
    across[:, 1] = edge[order].reshape(n_gy, 1, width)[:, 0][:, lane % width]
    across[0, 2] = lane % half == 0
    deep = np.zeros((n_gx, 8, 128))
    per = 128 // width
    for v in range(share // per):
        deep[:, v] = (np.arange(n_gx)[:, None] * share + v * per + lane // width) * unit
    down = np.stack([np.broadcast_to(t[:, None], (G, 128)) for t in (plain, edge)])
    tables = {
        "ahead": ahead.reshape(G, G),
        "back": back.reshape(G, G).T,
        "first": np.concatenate([cos[:, order], sin[:, order]], axis=1),
        "first_back": np.concatenate([cos[:, order], sin[:, order]], axis=1),
        "second": np.concatenate([cos, sin], axis=0),
        "across": across,
        "deep": deep,
        "down": down,
    }
    return {name: np.asarray(table, np.float32) for name, table in tables.items()}


def spread(tiles, at, group, tall):
    count = 128 // group
    lane = lax.shift_right_logical(lax.broadcasted_iota(jnp.int32, (tall, 128), 1), group.bit_length() - 1)
    out = None
    for g, tile in enumerate(tiles):
        moved = pltpu.roll(tile, group * ((g - at) % count), 1) if g != at else tile
        out = moved if out is None else jnp.where(lane == g, moved, out)
    return out


def depth_kernel(field_ref, table_ref, out_ref, spec, *, n_gx, tall, wide):
    rows = tall * wide
    for c in range(3):
        spec[c * rows : (c + 1) * rows, :] = matmul(field_ref[c * rows : (c + 1) * rows, :], table_ref[...], PLAIN)
    group = G // n_gx
    count = n_gx

    @pl.loop(0, 3 * wide // count)
    def _(i):
        c = lax.div(i, jnp.int32(wide // count))
        b = (i - c * (wide // count)) * count
        tiles = [spec[pl.ds(c * rows + b + g, tall, stride=wide), :] for g in range(count)]
        for p in range(n_gx):
            out_ref[p, :, pl.ds(pl.multiple_of(i * 128, 128), 128)] = spread(tiles, p, group, tall)


def first_kernel(data_ref, table_ref, out_ref, turned, *, n_gy, share, wide):
    group = G // n_gy
    per = 128 // (2 * share)

    @pl.loop(0, 3 * wide // per)
    def _(i):
        c = lax.div(i, jnp.int32(wide // per))
        b = (i - c * (wide // per)) * per
        piece = jnp.transpose(data_ref[:, pl.ds(pl.multiple_of(i * 128, 128), 128)])
        both = matmul(piece, table_ref[...], PLAIN)
        for g in range(per):
            lo, mid, hi = g * 2 * share, (g * 2 + 1) * share, (g * 2 + 2) * share
            real = both[lo:mid, :128] + both[mid:hi, 128:]
            imag = both[mid:hi, :128] - both[lo:mid, 128:]
            turned[pl.ds(2 * c * share * wide + b + g, share, stride=wide), :] = real
            turned[pl.ds((2 * c + 1) * share * wide + b + g, share, stride=wide), :] = imag

    count = 128 // group

    @pl.loop(0, 6 * share // count)
    def _(i):
        at = i * (count * wide)
        tiles = [turned[pl.ds(pl.multiple_of(at + u * wide, 8), wide), :] for u in range(count)]
        for j in range(n_gy):
            out_ref[j, i] = spread(tiles, j, group, wide)


def second_kernel(ids, data_ref, table_ref, across_ref, deep_ref, down_ref, out_ref, flow, *, n_gy, views, wide):
    lane = lax.broadcasted_iota(jnp.int32, (G, 128), 1)
    width = G // n_gy
    half = width // 2
    across = across_ref[ids[1]]
    deep = deep_ref[ids[0]]
    alone = (lane < width) & (ids[0] == 0)
    mirror_self = across[2:3, :] > 0.5
    upper = (lane & half) != 0

    def whole(tile):
        return jnp.concatenate([data_ref[j, tile] for j in range(n_gy)], axis=0)

    def mirrored(value):
        other = jnp.where(upper, pltpu.roll(value, half, 1), pltpu.roll(value, 128 - half, 1))
        return jnp.where(mirror_self, value, other)

    def ahead(real, imag):
        one = matmul(table_ref[...], real, PLAIN)
        two = matmul(table_ref[...], imag, PLAIN)
        return one[:G] + two[G:], two[:G] - one[G:]

    def projected(spectrum, deep_plain, deep_edge):
        plain = (across[0:1, :], down_ref[0], deep_plain)
        edge = (across[1:2, :], down_ref[1], deep_edge)
        waves = [p + e for p, e in zip(plain, edge)]
        wave_sq = waves[0] * waves[0] + waves[1] * waves[1] + waves[2] * waves[2]
        live = wave_sq > 0
        inverse = 1.0 / jnp.where(live, wave_sq, 1.0)
        spread_sq = wave_sq / (4.0 * split_xi**2)
        green = (1.0 - bead_radius**2 * wave_sq / 3.0) * (1.0 + spread_sq) * jnp.exp(-spread_sq) * inverse
        green = jnp.where(live, green / float(G**3), 0.0)
        out = []
        for r in range(2):
            regular = sum(w * spectrum[c][r] for c, w in enumerate(plain)) * inverse
            nyquist = sum(w * spectrum[c][r] for c, w in enumerate(edge)) * inverse
            out.append([green * (spectrum[c][r] - plain[c] * regular - edge[c] * nyquist) for c in range(3)])
        return out

    zero = jnp.zeros((1, 128), jnp.float32)
    for v in range(views):
        spectrum = []
        apart = []
        for c in range(3):
            real = whole((2 * c) * views + v)
            imag = whole((2 * c + 1) * views + v)
            if v == 0:
                off_real = jnp.where(alone, 0.5 * (real - mirrored(real)), 0.0)
                off_imag = jnp.where(alone, 0.5 * (imag + mirrored(imag)), 0.0)
                apart.append(ahead(off_real, off_imag))
                real, imag = real - off_real, imag - off_imag
            spectrum.append(ahead(real, imag))
        found = projected(spectrum, deep[v : v + 1, :], zero)
        if v == 0:
            extra = projected(apart, zero, zero - math.pi / grid_spacing)
            found = [[a + b for a, b in zip(one, two)] for one, two in zip(found, extra)]
        for c in range(3):
            one = matmul(table_ref[...], found[0][c], PLAIN)
            two = matmul(table_ref[...], found[1][c], PLAIN)
            real, imag = one[:G] - two[G:], two[:G] + one[G:]
            for j in range(n_gy):
                out_ref[j, (2 * c) * views + v] = real[j * wide : (j + 1) * wide]
                out_ref[j, (2 * c + 1) * views + v] = imag[j * wide : (j + 1) * wide]


def first_back_kernel(data_ref, table_ref, out_ref, turned, *, n_gy, share, wide):
    group = G // n_gy
    count = n_gy
    per = 128 // (2 * share)

    @pl.loop(0, 6 * share // count)
    def _(i):
        tiles = [data_ref[j, i] for j in range(n_gy)]
        for u in range(count):
            turned[pl.ds(pl.multiple_of((i * count + u) * wide, 8), wide), :] = spread(tiles, u, group, wide)

    @pl.loop(0, 3 * wide // per)
    def _(i):
        c = lax.div(i, jnp.int32(wide // per))
        b = (i - c * (wide // per)) * per
        rows = []
        for g in range(per):
            real = turned[pl.ds(2 * c * share * wide + b + g, share, stride=wide), :]
            imag = turned[pl.ds((2 * c + 1) * share * wide + b + g, share, stride=wide), :]
            rows.append(jnp.concatenate([real, -imag], axis=1))
            rows.append(jnp.concatenate([imag, real], axis=1))
        piece = jnp.concatenate(rows, axis=0)
        out_ref[:, pl.ds(pl.multiple_of(i * 128, 128), 128)] = matmul(table_ref[...], piece, TURNED)


def depth_back_kernel(data_ref, table_ref, out_ref, spec, *, n_gx, tall, wide):
    rows = tall * wide
    group = G // n_gx
    count = n_gx

    @pl.loop(0, 3 * wide // count)
    def _(i):
        c = lax.div(i, jnp.int32(wide // count))
        b = (i - c * (wide // count)) * count
        tiles = [data_ref[p, :, pl.ds(pl.multiple_of(i * 128, 128), 128)] for p in range(n_gx)]
        for g in range(count):
            spec[pl.ds(c * rows + b + g, tall, stride=wide), :] = spread(tiles, g, group, tall)

    for c in range(3):
        out_ref[c * rows : (c + 1) * rows, :] = matmul(spec[c * rows : (c + 1) * rows, :], table_ref[...], PLAIN)


def waves(grid_data, n_gx, n_gy, fill):
    tall, wide, share = G // n_gx, G // n_gy, G // 2 // n_gx
    rows = 3 * tall * wide
    views = share * wide // 128
    tables = wave_tables(n_gx, n_gy)
    f32 = jnp.float32

    def run(name, kernel, shape, args, scratch, specs=None, after=(), **sizes):
        return launch(
            marking(ignoring(functools.partial(kernel, **sizes), len(args), len(after)), len(args) + len(after)),
            out_shape=(jax.ShapeDtypeStruct(shape, f32), jax.ShapeDtypeStruct((8, 128), f32)),
            in_specs=(specs or [MOVED_SPEC] + [VMEM_SPEC] * (len(args) - 1)) + [ANY_SPEC] * len(after),
            out_specs=(VMEM_SPEC,) * 2,
            scratch_shapes=[pltpu.VMEM(scratch, f32)],
            compiler_params=pltpu.CompilerParams(vmem_limit_bytes=32 * 1024 * 1024),
            name=name,
        )(*args, *after)

    def swap(value, axis):
        return lax.all_to_all(value, axis, split_axis=0, concat_axis=0, tiled=True)

    force = pl.BlockSpec((rows, 128), lambda i: (1, 0))
    lanes = 6 * wide * share
    ids = jnp.stack([lax.axis_index("gx"), lax.axis_index("gy")]).astype(jnp.int32)
    value, token = run("depth", depth_kernel, (n_gx, tall, lanes), (pltpu.with_memory_space_constraint(grid_data, pltpu.HBM), tables["ahead"]), (rows, 128),
                [force, VMEM_SPEC], n_gx=n_gx, tall=tall, wide=wide)
    after = fill(0, token)
    value = swap(value, "gx").reshape(G, lanes)
    value, token = run("first", first_kernel, (n_gy, 6 * views, wide, 128), (value, tables["first"]), (rows, 128),
                after=after, n_gy=n_gy, share=share, wide=wide)
    after = fill(1, token)
    value = swap(value.reshape(n_gy, 6 * views * wide, 128), "gy").reshape(n_gy, 6 * views, wide, 128)
    args = (ids, value, tables["second"], tables["across"], tables["deep"], tables["down"])
    value, token = run("second", second_kernel, (n_gy, 6 * views, wide, 128), args, (8, 128),
                [SMEM_SPEC, MOVED_SPEC] + [VMEM_SPEC] * 4, after, n_gy=n_gy, views=views, wide=wide)
    after = fill(2, token)
    value = swap(value.reshape(n_gy, 6 * views * wide, 128), "gy").reshape(n_gy, 6 * views, wide, 128)
    value, token = run("first_back", first_back_kernel, (G, lanes), (value, tables["first_back"]), (rows, 128),
                after=after, n_gy=n_gy, share=share, wide=wide)
    after = fill(3, token)
    value = swap(value.reshape(n_gx, tall, lanes), "gx")
    value, _ = run("depth_back", depth_back_kernel, (rows, 128), (value, tables["back"]), (rows, 128),
               after=after, n_gx=n_gx, tall=tall, wide=wide)
    return value


def shards(positions, noise, route, node_perm, pair_first, pair_second, pair_count):
    n_gx = lax.axis_size("gx")
    n_gy = lax.axis_size("gy")
    both = ("gx", "gy")
    peers = n_gx * n_gy
    slots = node_perm.shape[2]
    depth = slots // peers // 128
    rows = positions.shape[1] // 128
    rp = slots // 128
    swap = partial(lax.all_to_all, axis_name=both, split_axis=0, concat_axis=0, tiled=True)

    bounds = jnp.arange(peers + 1, dtype=jnp.int32) * (slots // peers)
    starts = jnp.sum(route[None, :] < bounds[:, None], axis=1, dtype=jnp.int32)
    taken = swap(slots_call(starts, route.reshape(rows, 128), depth))
    places = positions.reshape(3, rows, 128)
    data = swap(pack_call(starts, places, depth))
    counts = jnp.sum(taken >= 0, axis=(1, 2), dtype=jnp.int32)
    own_order = lax.dynamic_index_in_dim(node_perm, lax.axis_index("gx"), 0, False)
    nodes, node_lists, row_lists = nodes_call(taken, own_order.reshape(peers, depth, 128), slots)
    own_pairs, far_pairs, totals = order_call(pair_first[0], pair_second[0], pair_count, slots // CELL)
    grid_data, cells = scatter_call(node_lists, counts, data, rp, after=(totals,))

    state = {"sums": None}

    def within(n, after):
        state["sums"], token = pair_call(own_pairs, totals, n, cells, state["sums"], after=after)
        return token

    def fill(n, token):
        if n < 3:
            if n == 1:
                ready, _ = lax.optimization_barrier((grid_data, token))
                state["beside"] = shifted(ready, "gx", -1)
            return (within(n, (token,)),)
        state["sums"], _, far = pair_call(
            far_pairs, totals, len(PARTS) + 2, cells, state["sums"], state["beside"], after=(token,)
        )
        state["far"] = shifted(far, "gx", 1)
        return (within(3, ()),)

    share = G // 2 // n_gx
    if share % 8 == 0 and share * (G // n_gy) % 128 == 0:
        wave_vel = waves(grid_data, n_gx, n_gy, fill)
    else:
        wave_vel = kspace_part(grid_data[3 * rp :], n_gx, n_gy).reshape(3 * rp, 128)
        for n in range(4):
            fill(n, wave_vel)
    back = swap(gather_call(row_lists, counts, nodes, state["sums"], wave_vel, state["far"]))
    moved, drift = finish_call(starts, back, places, noise.reshape(3, rows, 128))
    return (moved.reshape(positions.shape), drift.reshape(positions.shape))


def solution(mesh):
    in_specs = (
        P(None, ("gx", "gy")),
        P(None, ("gx", "gy")),
        P(("gx", "gy")),
        P(None, "gy", None),
        P(("gx", "gy"), None),
        P(("gx", "gy"), None),
        P(("gx", "gy")),
    )
    out_specs = (P(None, ("gx", "gy")), P(None, ("gx", "gy")))
    return jax.shard_map(shards, mesh=mesh, in_specs=in_specs, out_specs=out_specs, check_vma=False)
```
